32 devices in a mesh: shard: 16 (over z, y, x), rep: 2 (over core).
Axes of the slice: x: 2, y: 2, z: 4, core: 2. Of those that a mesh axis runs over, the one named last changes fastest.
Arguments:
- tokens: bfloat16 [65536, 768], P(('shard', 'rep')), may hold values from -6 to 6
- grad_out: bfloat16 [65536, 768], P(('shard', 'rep')), may hold values from -6 to 6
- first_gain: bfloat16 [768], P('shard'), may hold values from 0.5 to 1.5
- first_shift: bfloat16 [768], P('shard'), may hold values from -3 to 3
- query_proj: bfloat16 [768, 768], P('shard'), may hold values from -0.21875 to 0.21875
- query_bias: bfloat16 [768], P('shard'), may hold values from -3 to 3
- key_proj: bfloat16 [768, 768], P('shard'), may hold values from -0.21875 to 0.21875
- value_proj: bfloat16 [768, 768], P('shard'), may hold values from -0.21875 to 0.21875
- value_bias: bfloat16 [768], P('shard'), may hold values from -3 to 3
- output_proj: bfloat16 [768, 768], P('shard'), may hold values from -0.875 to 0.875
- output_bias: bfloat16 [768], P('shard'), may hold values from -3 to 3
- second_gain: bfloat16 [768], P('shard'), may hold values from 0.5 to 1.5
- second_shift: bfloat16 [768], P('shard'), may hold values from -3 to 3
- hidden_proj: bfloat16 [768, 3072], P('shard'), may hold values from -0.21875 to 0.21875
- hidden_bias: bfloat16 [3072], P('shard'), may hold values from -3 to 3
- final_proj: bfloat16 [3072, 768], P('shard'), may hold values from -0.109375 to 0.109375
- final_bias: bfloat16 [768], P('shard'), may hold values from -3 to 3
- threshold: float32 [12], replicated, may hold values from 0.5 to 3
Outputs:
- layer_output: bfloat16 [65536, 768], P(('shard', 'rep'))
- grad_tokens: bfloat16 [65536, 768], P(('shard', 'rep'))
- grad_first_gain: float32 [768], P('shard')
- grad_first_shift: float32 [768], P('shard')
- grad_query_proj: float32 [768, 768], P('shard')
- grad_query_bias: float32 [768], P('shard')
- grad_key_proj: float32 [768, 768], P('shard')
- grad_value_proj: float32 [768, 768], P('shard')
- grad_value_bias: float32 [768], P('shard')
- grad_output_proj: float32 [768, 768], P('shard')
- grad_output_bias: float32 [768], P('shard')
- grad_second_gain: float32 [768], P('shard')
- grad_second_shift: float32 [768], P('shard')
- grad_hidden_proj: float32 [768, 3072], P('shard')
- grad_hidden_bias: float32 [3072], P('shard')
- grad_final_proj: float32 [3072, 768], P('shard')
- grad_final_bias: float32 [768], P('shard')
- head_max: float32 [12], replicated
- clip_factor: float32 [12], replicated
- clipped_query: float32 [768, 768], P('shard')
- clipped_query_bias: float32 [768], P('shard')
- clipped_key: float32 [768, 768], P('shard')
The draws below stay inside these ranges and needn't reach their ends.
All inputs are finite; a program needn't handle non-finite values.
Results may differ from the reference program's by a relative error of at most 0.019.
Values may be sent and summed in bfloat16 or wider, within the bound.
A program may use at most 256 MiB of HBM per device.

```python
import math
import jax
import jax.numpy as jnp
from jax import lax

D = 768
HEADS = 12
HEAD_DIM = 64
FF = 3072
FRAMES = 16
TOKENS = 65536


def block_levels(own_key, shape, shards, least, largest):
    def one(position, shards_of):
        heights = jax.random.uniform(jax.random.fold_in(jax.random.fold_in(own_key, 6), position), (shards_of,), jnp.float32, least / len(shards), largest / len(shards))
        return jnp.repeat(jnp.exp(heights), shape[position] // shards_of).reshape((-1,) + (1,) * (len(shape) - position - 1))

    factor_of = one(*shards[0])
    for cut in shards[1:]:
        factor_of = factor_of * one(*cut)
    return factor_of


def normal_values(own_key, dims, deviation, reach, pieces=(), dtype=jnp.bfloat16):
    loudness = block_levels(own_key, dims, pieces, -0.22, 0.18) if pieces else 1.0
    drawn = jax.random.normal(own_key, dims, jnp.float32) * deviation * loudness
    return jnp.minimum(jnp.maximum(drawn, -reach), reach).astype(dtype)


def setup_inputs(seed: int = 0) -> dict:
    splits = jax.random.split(jax.random.key(seed), 19)
    return {
        "tokens": normal_values(splits[0], (TOKENS, D), 1.0, 6.0, ((0, 32),)),
        "grad_out": normal_values(splits[1], (TOKENS, D), 1.0, 6.0, ((0, 32),)),
        "first_gain": jnp.clip(1.0 + 0.1 * jax.random.normal(splits[2], (D,), jnp.float32), 0.5, 1.5).astype(jnp.bfloat16),
        "first_shift": normal_values(splits[3], (D,), 0.5, 3.0, ((0, 16),)),
        "query_proj": normal_values(splits[4], (D, D), D ** -0.5, 0.21875, ((0, 16),)),
        "query_bias": normal_values(splits[5], (D,), 0.5, 3.0, ((0, 16),)),
        "key_proj": normal_values(splits[6], (D, D), D ** -0.5, 0.21875, ((0, 16),)),
        "value_proj": normal_values(splits[7], (D, D), D ** -0.5, 0.21875, ((0, 16),)),
        "value_bias": normal_values(splits[8], (D,), 0.5, 3.0, ((0, 16),)),
        "output_proj": normal_values(splits[9], (D, D), (D // FRAMES) ** -0.5, 0.875, ((0, 16),)),
        "output_bias": normal_values(splits[10], (D,), 0.5, 3.0, ((0, 16),)),
        "second_gain": jnp.clip(1.0 + 0.1 * jax.random.normal(splits[11], (D,), jnp.float32), 0.5, 1.5).astype(jnp.bfloat16),
        "second_shift": normal_values(splits[12], (D,), 0.5, 3.0, ((0, 16),)),
        "hidden_proj": normal_values(splits[13], (D, FF), D ** -0.5, 0.21875, ((0, 16),)),
        "hidden_bias": normal_values(splits[14], (FF,), 0.5, 3.0, ((0, 16),)),
        "final_proj": normal_values(splits[15], (FF, D), FF ** -0.5, 0.109375, ((0, 16),)),
        "final_bias": normal_values(splits[16], (D,), 0.5, 3.0, ((0, 16),)),
        "threshold": jnp.clip(jnp.exp(jax.random.uniform(splits[17], (HEADS,), jnp.float32, math.log(0.5), math.log(3.0))), 0.5, 3.0),
    }


@jax.custom_vjp
def low(v):
    return lax.optimization_barrier(v.astype(jnp.bfloat16)).astype(jnp.float32)

@jax.custom_vjp
def low_back(v):
    return v

def low_keep(v):
    return (low(v), None)

def low_pass(kept, grad):
    return (grad,)

def back_keep(v):
    return (v, None)

def back_low(kept, grad):
    return (low(grad),)
low.defvjp(low_keep, low_pass)
low_back.defvjp(back_keep, back_low)
EPSILON = 1e-06
HIGH = lax.Precision.HIGHEST

def layer_norm(values, gain, shift):
    centred = values - lax.optimization_barrier(jnp.mean(values, axis=-1, keepdims=True))
    scaled = centred * lax.rsqrt(lax.optimization_barrier(jnp.mean(centred * centred, axis=-1, keepdims=True)) + EPSILON)
    return scaled * gain + shift

def matmul(left, right):
    return jnp.dot(left, right, precision=HIGH)

def forward(params, block):
    first_gain, first_shift, query_proj, query_bias, key_proj, value_proj, value_bias, output_proj, output_bias, second_gain, second_shift, hidden_proj, hidden_bias, final_proj, final_bias = params
    rows = block.shape[0]
    places = rows // FRAMES
    scale = 1.0 / math.sqrt(HEAD_DIM)
    inputs_one = low(layer_norm(block, first_gain, first_shift))
    queries = low(low_back(matmul(inputs_one, query_proj) + query_bias))
    keys = low(low_back(matmul(inputs_one, key_proj)))
    values = low(low_back(matmul(inputs_one, value_proj) + value_bias))
    queries = queries.reshape(places, FRAMES, HEADS, HEAD_DIM)
    keys = keys.reshape(places, FRAMES, HEADS, HEAD_DIM)
    values = values.reshape(places, FRAMES, HEADS, HEAD_DIM)
    scores = low_back(jnp.einsum('pfhd,pghd->phfg', queries, keys, precision=HIGH) * scale)
    top_logit = lax.optimization_barrier(jnp.max(scores, axis=(0, 2, 3)))
    probs = low(jax.nn.softmax(scores, axis=-1))
    mixed = jnp.einsum('phfg,pghd->pfhd', probs, values, precision=HIGH).reshape(rows, D)
    mixed = low(low_back(mixed))
    attended = low_back(matmul(mixed, output_proj) + output_bias)
    middle = block + attended
    inputs_two = low(layer_norm(middle, second_gain, second_shift))
    hidden_pre = low_back(matmul(inputs_two, hidden_proj) + hidden_bias)
    activated = low(jax.nn.gelu(hidden_pre))
    result = middle + (matmul(activated, final_proj) + final_bias)
    return (result, top_logit)

def add_pair(left, right):
    return left + right

def reference(tokens, grad_out, first_gain, first_shift, query_proj, query_bias, key_proj, value_proj, value_bias, output_proj, output_bias, second_gain, second_shift, hidden_proj, hidden_bias, final_proj, final_bias, threshold):
    params = tuple((item.astype(jnp.float32) for item in (first_gain, first_shift, query_proj, query_bias, key_proj, value_proj, value_bias, output_proj, output_bias, second_gain, second_shift, hidden_proj, hidden_bias, final_proj, final_bias)))
    block_rows = math.gcd(TOKENS, 4096)
    count = TOKENS // block_rows
    inputs = tokens.astype(jnp.float32).reshape(count, block_rows, D)
    cotangents = grad_out.astype(jnp.float32).reshape(count, block_rows, D)
    totals = jax.tree.map(jnp.zeros_like, params)
    lowest = jnp.full((HEADS,), -1e+30, jnp.float32)

    def step(carry, pair):
        sums, highest = carry
        block, cotangent = pair
        result, backward, top_logit = jax.vjp(forward, params, block, has_aux=True)
        param_grads, input_grad = backward(cotangent)
        sums = jax.tree.map(add_pair, sums, param_grads)
        return ((sums, jnp.maximum(highest, top_logit)), (result.astype(jnp.bfloat16), input_grad.astype(jnp.bfloat16)))
    (sums, highest), (results, input_grads) = lax.scan(step, (totals, lowest), (inputs, cotangents))
    layer_output = results.reshape(TOKENS, D)
    grad_tokens = input_grads.reshape(TOKENS, D)
    factor = jnp.minimum(1.0, threshold / highest)
    column_scale = jnp.repeat(jnp.sqrt(factor), HEAD_DIM)
    clipped_query = params[2] * column_scale[None, :]
    clipped_query_bias = params[3] * column_scale
    clipped_key = params[4] * column_scale[None, :]
    return (layer_output, grad_tokens, sums[0], sums[1], sums[2], sums[3], sums[4], sums[5], sums[6], sums[7], sums[8], sums[9], sums[10], sums[11], sums[12], sums[13], sums[14], highest, factor, clipped_query, clipped_query_bias, clipped_key)
```

```python
import math

import jax
import jax.numpy as jnp
from jax import lax
from jax.experimental import pallas as pl
from jax.experimental.pallas import tpu as pltpu
from jax.sharding import PartitionSpec as P

FRAMES = 16
EPSILON = 1e-06
BF = jnp.bfloat16
F32 = jnp.float32
ROWS = 512
BLOCK = 128
PAIR = 128


def nn(left, right):
    return lax.dot_general(left, right, (((1,), (0,)), ((), ())), preferred_element_type=F32)


def nt(left, right):
    return lax.dot_general(left, right, (((1,), (1,)), ((), ())), preferred_element_type=F32)


def tn(left, right):
    return lax.dot_general(left, right, (((0,), (0,)), ((), ())), preferred_element_type=F32)


def normalise(values):
    centred = values - jnp.mean(values, axis=-1, keepdims=True)
    inverse = lax.rsqrt(jnp.mean(centred * centred, axis=-1, keepdims=True) + EPSILON)
    return centred * inverse, inverse


def norm_back(grad, unit, inverse, gain):
    scaled = grad * gain
    return inverse * (
        scaled
        - jnp.mean(scaled, axis=-1, keepdims=True)
        - unit * jnp.mean(scaled * unit, axis=-1, keepdims=True)
    )


def column_sum(values):
    return jnp.sum(values, axis=0, keepdims=True)


def place_masks():
    lane = lax.broadcasted_iota(jnp.int32, (FRAMES, 2 * BLOCK), 1)
    return [(lane % BLOCK) // FRAMES == p for p in range(BLOCK // FRAMES)]


def halves(width):
    lane = lax.broadcasted_iota(jnp.int32, (1, PAIR), 1)
    first = (lane < width).astype(F32)
    return first.astype(BF), (1.0 - first).astype(BF)


def compress(wide, masks):
    total = wide[:FRAMES]
    for p in range(1, len(masks)):
        total = jnp.where(masks[p], wide[p * FRAMES : (p + 1) * FRAMES], total)
    return total


def expand(packed, masks):
    zero = jnp.zeros_like(packed)
    return jnp.concatenate([jnp.where(m, packed, zero).astype(BF) for m in masks], axis=0)


def split(two, first, second):
    return jnp.concatenate([two * first, two * second], axis=0)


def stack(wide):
    return jnp.concatenate([wide[:, :BLOCK], wide[:, BLOCK:]], axis=0)


def attend_kernel(
    width, tok_ref, wq_ref, wk_ref, wv_ref, wo_ref, vec_ref,
    q_ref, k_ref, v_ref, p_ref, mix_ref, mid_ref, top_ref,
):
    scale = 1.0 / math.sqrt(width)
    gain, shift = vec_ref[0:1], vec_ref[1:2]
    tok = tok_ref[...].astype(F32)
    unit, _ = normalise(tok)
    one = (unit * gain + shift).astype(BF)
    q_ref[...] = (nn(one, wq_ref[...]) + vec_ref[2:3]).astype(BF)
    k_ref[...] = nn(one, wk_ref[...]).astype(BF)
    v_ref[...] = (nn(one, wv_ref[...]) + vec_ref[3:4]).astype(BF)
    masks = place_masks()
    first, second = halves(width)
    pairs = tok_ref.shape[1] // PAIR

    @pl.when(pl.program_id(0) == 0)
    def _():
        top_ref[...] = jnp.full(top_ref.shape, -3e38, F32)

    def body(i, carry):
        rows = pl.ds(pl.multiple_of(i * BLOCK, BLOCK), BLOCK)
        for h in range(pairs):
            cols = slice(h * PAIR, (h + 1) * PAIR)
            two_q, two_k, two_v = q_ref[rows, cols], k_ref[rows, cols], v_ref[rows, cols]
            scores = compress(nt(two_k, split(two_q, first, second)), masks) * scale
            top_ref[h] = jnp.maximum(top_ref[h], scores)
            expo = jnp.exp(scores - jnp.max(scores, axis=0, keepdims=True))
            probs = expo / jnp.sum(expo, axis=0, keepdims=True)
            p_ref[i, h] = probs
            mixed = tn(stack(expand(probs, masks)), split(two_v, first, second))
            mix_ref[rows, cols] = mixed.astype(BF)
        return carry

    lax.fori_loop(0, tok_ref.shape[0] // BLOCK, body, 0)
    mid_ref[...] = tok + (nn(mix_ref[...], wo_ref[...]) + vec_ref[4:5])


def mlp_kernel(
    chunk, mid_ref, dy_ref, w1_ref, w2_ref, vec_ref, hb_ref,
    out_ref, mg_ref, w1g_ref, w2g_ref, vg_ref, hbg_ref,
    acc1, acc2, res_ref, two_ref,
):
    step, last = pl.program_id(0), pl.num_programs(0) - 1
    gain, shift = vec_ref[5:6], vec_ref[6:7]
    mid = mid_ref[...]
    unit, inverse = normalise(mid)
    inp = (unit * gain + shift).astype(BF)
    dy = dy_ref[...]
    hidden = w1_ref.shape[1]

    @pl.when(step == 0)
    def _():
        acc1[...] = jnp.zeros_like(acc1)
        acc2[...] = jnp.zeros_like(acc2)
        vg_ref[...] = jnp.zeros_like(vg_ref)
        hbg_ref[...] = jnp.zeros_like(hbg_ref)

    res_ref[...] = mid + vec_ref[7:8]
    two_ref[...] = jnp.zeros_like(two_ref)
    root = math.sqrt(2.0 / math.pi)

    def body(j, carry):
        cols = pl.ds(pl.multiple_of(j * chunk, chunk), chunk)
        z = nn(inp, w1_ref[:, cols]) + hb_ref[:, cols]
        act_grad = nt(dy, w2_ref[cols, :])
        square = z * z
        bend = jnp.tanh(root * z * (1.0 + 0.044715 * square))
        half = 0.5 * (1.0 + bend)
        act = (z * half).astype(BF)
        slope = half + 0.5 * z * (1.0 - bend * bend) * (root * (1.0 + 0.134145 * square))
        grad = (act_grad * slope).astype(BF)
        res_ref[...] += nn(act, w2_ref[cols, :])
        two_ref[...] += nt(grad, w1_ref[:, cols])
        acc2[cols, :] += tn(act, dy)
        acc1[:, cols] += tn(inp, grad)
        hbg_ref[:, cols] += column_sum(grad.astype(F32))
        return carry

    lax.fori_loop(0, hidden // chunk, body, 0)
    out_ref[...] = res_ref[...].astype(BF)
    two = two_ref[...]
    up = dy.astype(F32)
    mg_ref[...] = up + norm_back(two, unit, inverse, gain)
    vg_ref[0:1] += column_sum(two * unit)
    vg_ref[1:2] += column_sum(two)
    vg_ref[2:3] += column_sum(up)

    @pl.when(step == last)
    def _():
        w1g_ref[...] = acc1[...].astype(BF)
        w2g_ref[...] = acc2[...].astype(BF)


def back_kernel(
    width, tok_ref, mg_ref, q_ref, k_ref, v_ref, p_ref, mix_ref,
    wq_ref, wk_ref, wv_ref, wo_ref, vec_ref,
    gt_ref, wqg_ref, wkg_ref, wvg_ref, wog_ref, vg_ref,
    accq, acck, accv, acco, mgl_ref, dq_ref, dk_ref, dv_ref,
):
    step, last = pl.program_id(0), pl.num_programs(0) - 1
    scale = 1.0 / math.sqrt(width)
    gain, shift = vec_ref[0:1], vec_ref[1:2]
    accs = (accq, acck, accv, acco)

    @pl.when(step == 0)
    def _():
        for acc in accs:
            acc[...] = jnp.zeros_like(acc)
        vg_ref[...] = jnp.zeros_like(vg_ref)

    branch = mg_ref[...].astype(BF)
    mgl_ref[...] = nt(branch, wo_ref[...]).astype(BF)
    acco[...] += tn(mix_ref[...], branch)
    vg_ref[4:5] += column_sum(branch.astype(F32))
    masks = place_masks()
    first, second = halves(width)
    pairs = tok_ref.shape[1] // PAIR

    def body(i, carry):
        rows = pl.ds(pl.multiple_of(i * BLOCK, BLOCK), BLOCK)
        for h in range(pairs):
            cols = slice(h * PAIR, (h + 1) * PAIR)
            two_q, two_k, two_v = q_ref[rows, cols], k_ref[rows, cols], v_ref[rows, cols]
            mixed = split(mgl_ref[rows, cols], first, second)
            probs = p_ref[i, h]
            slope = compress(nt(two_v, mixed), masks)
            score = probs * (slope - jnp.sum(slope * probs, axis=0, keepdims=True))
            wide = expand(score, masks)
            dv_ref[rows, cols] = nn(expand(probs, masks), mixed).astype(BF)
            dk_ref[rows, cols] = (nn(wide, split(two_q, first, second)) * scale).astype(BF)
            dq_ref[rows, cols] = (tn(stack(wide), split(two_k, first, second)) * scale).astype(BF)
        return carry

    lax.fori_loop(0, tok_ref.shape[0] // BLOCK, body, 0)
    unit, inverse = normalise(tok_ref[...].astype(F32))
    one = (unit * gain + shift).astype(BF)
    dq, dk, dv = dq_ref[...], dk_ref[...], dv_ref[...]
    vg_ref[2:3] += column_sum(dq.astype(F32))
    vg_ref[3:4] += column_sum(dv.astype(F32))
    accq[...] += tn(one, dq)
    acck[...] += tn(one, dk)
    accv[...] += tn(one, dv)
    grad = nt(dq, wq_ref[...]) + nt(dk, wk_ref[...]) + nt(dv, wv_ref[...])
    vg_ref[0:1] += column_sum(grad * unit)
    vg_ref[1:2] += column_sum(grad)
    gt_ref[...] = (mg_ref[...] + norm_back(grad, unit, inverse, gain)).astype(BF)

    @pl.when(step == last)
    def _():
        for out, acc in zip((wqg_ref, wkg_ref, wvg_ref, wog_ref), accs):
            out[...] = acc[...].astype(BF)


def whole(shape):
    return pl.BlockSpec(shape, lambda i: (0,) * len(shape), pipeline_mode=pl.Buffered(1))


def tiles(height, width):
    return pl.BlockSpec((height, width), lambda i: (i, 0))


def shaped(shape, dtype):
    return jax.ShapeDtypeStruct(shape, dtype)


VMEM_LIMIT = 60 * 1024 * 1024


def params():
    return pltpu.CompilerParams(
        dimension_semantics=("arbitrary",), vmem_limit_bytes=VMEM_LIMIT
    )


def attend(tokens, wq, wk, wv, wo, vec, heads):
    rows, d = tokens.shape
    t = min(ROWS, rows)
    pairs = d // PAIR
    blocks = rows // BLOCK
    big = tiles(t, d)
    w = whole((d, d))
    return pl.pallas_call(
        lambda *refs: attend_kernel(d // heads, *refs),
        grid=(rows // t,),
        in_specs=[big, w, w, w, w, whole(vec.shape)],
        out_specs=[
            big, big, big,
            pl.BlockSpec((t // BLOCK, pairs, FRAMES, 2 * BLOCK), lambda i: (i, 0, 0, 0)),
            big, big,
            whole((pairs, FRAMES, 2 * BLOCK)),
        ],
        out_shape=[shaped((rows, d), BF)] * 3
        + [shaped((blocks, pairs, FRAMES, 2 * BLOCK), F32), shaped((rows, d), BF), shaped((rows, d), F32)]
        + [shaped((pairs, FRAMES, 2 * BLOCK), F32)],
        compiler_params=params(),
        cost_estimate=pl.CostEstimate(flops=10 * rows * d * d, bytes_accessed=24 * rows * d, transcendentals=0),
        name="attend",
    )(tokens, wq, wk, wv, wo, vec)


def mlp(middle, dy, w1, w2, vec, hb):
    rows, d = middle.shape
    hidden = w1.shape[1]
    t = min(ROWS, rows)
    big = tiles(t, d)
    return pl.pallas_call(
        lambda *refs: mlp_kernel(768, *refs),
        grid=(rows // t,),
        in_specs=[big, big, whole(w1.shape), whole(w2.shape), whole(vec.shape), whole(hb.shape)],
        out_specs=[big, big, whole(w1.shape), whole(w2.shape), whole((8, d)), whole((1, hidden))],
        out_shape=[
            shaped((rows, d), BF), shaped((rows, d), F32), shaped(w1.shape, BF), shaped(w2.shape, BF),
            shaped((8, d), F32), shaped((1, hidden), F32),
        ],
        scratch_shapes=[
            pltpu.VMEM(w1.shape, F32), pltpu.VMEM(w2.shape, F32), pltpu.VMEM((t, d), F32), pltpu.VMEM((t, d), F32),
        ],
        compiler_params=params(),
        cost_estimate=pl.CostEstimate(flops=12 * rows * d * hidden, bytes_accessed=14 * rows * d, transcendentals=0),
        name="mlp",
    )(middle, dy, w1, w2, vec, hb)


def back(tokens, mg, q, k, v, p, mixed, wq, wk, wv, wo, vec, heads):
    rows, d = tokens.shape
    t = min(ROWS, rows)
    pairs = d // PAIR
    big = tiles(t, d)
    w = whole((d, d))
    return pl.pallas_call(
        lambda *refs: back_kernel(d // heads, *refs),
        grid=(rows // t,),
        in_specs=[
            big, big, big, big, big,
            pl.BlockSpec((t // BLOCK, pairs, FRAMES, 2 * BLOCK), lambda i: (i, 0, 0, 0)),
            big, w, w, w, w, whole(vec.shape),
        ],
        out_specs=[big, w, w, w, w, whole((8, d))],
        out_shape=[shaped((rows, d), BF)] + [shaped((d, d), BF)] * 4 + [shaped((8, d), F32)],
        scratch_shapes=[pltpu.VMEM((d, d), F32)] * 4 + [pltpu.VMEM((t, d), BF)] * 4,
        compiler_params=params(),
        cost_estimate=pl.CostEstimate(flops=20 * rows * d * d, bytes_accessed=24 * rows * d, transcendentals=0),
        name="back",
    )(tokens, mg, q, k, v, p, mixed, wq, wk, wv, wo, vec)


def on_device(
    tokens, grad_out, first_gain, first_shift, query_proj, query_bias, key_proj, value_proj, value_bias,
    output_proj, output_bias, second_gain, second_shift, hidden_proj, hidden_bias, final_proj, final_bias, threshold,
):
    def gather(x):
        return lax.all_gather(x, "shard", axis=0, tiled=True)

    heads = threshold.shape[0]
    wq, wk, wv, wo = (gather(x) for x in (query_proj, key_proj, value_proj, output_proj))
    small = (first_gain, first_shift, query_bias, value_bias, output_bias, second_gain, second_shift, final_bias)
    vec = jnp.stack([gather(x) for x in small]).astype(F32)
    hb = gather(hidden_bias).astype(F32)[None]
    w1, w2 = gather(hidden_proj), gather(final_proj)
    q, k, v, p, mixed, middle, top = attend(tokens, wq, wk, wv, wo, vec, heads)
    head_dim = tokens.shape[1] // heads
    local = jnp.max(top.reshape(top.shape[0], FRAMES, 2, BLOCK), axis=(1, 3)).reshape(heads)
    global_max = lax.pmax(local, ("shard", "rep"))
    layer_output, mg, w1g, w2g, vg2, hbg = mlp(middle, grad_out, w1, w2, vec, hb)
    grad_tokens, wqg, wkg, wvg, wog, vg1 = back(tokens, mg, q, k, v, p, mixed, wq, wk, wv, wo, vec, heads)

    def scatter(x):
        y = lax.psum_scatter(x.astype(BF), "shard", scatter_dimension=0, tiled=True)
        return lax.psum(y, "rep").astype(F32)

    factor = jnp.minimum(1.0, threshold / global_max)
    column_scale = jnp.repeat(jnp.sqrt(factor), head_dim)
    shard_rows = query_bias.shape[0]
    bias_scale = lax.dynamic_slice_in_dim(column_scale, lax.axis_index("shard") * shard_rows, shard_rows)
    return (
        layer_output, grad_tokens, scatter(vg1[0]), scatter(vg1[1]), scatter(wqg), scatter(vg1[2]), scatter(wkg),
        scatter(wvg), scatter(vg1[3]), scatter(wog), scatter(vg1[4]), scatter(vg2[0]), scatter(vg2[1]), scatter(w1g),
        scatter(hbg[0]), scatter(w2g), scatter(vg2[2]), global_max, factor,
        query_proj.astype(F32) * column_scale[None, :], query_bias.astype(F32) * bias_scale,
        key_proj.astype(F32) * column_scale[None, :],
    )


def solution(mesh):
    in_specs = (
        P(("shard", "rep"), None),
        P(("shard", "rep"), None),
        P("shard"),
        P("shard"),
        P("shard", None),
        P("shard"),
        P("shard", None),
        P("shard", None),
        P("shard"),
        P("shard", None),
        P("shard"),
        P("shard"),
        P("shard"),
        P("shard", None),
        P("shard"),
        P("shard", None),
        P("shard"),
        P(),
    )
    out_specs = (
        P(("shard", "rep"), None),
        P(("shard", "rep"), None),
        P("shard"),
        P("shard"),
        P("shard", None),
        P("shard"),
        P("shard", None),
        P("shard", None),
        P("shard"),
        P("shard", None),
        P("shard"),
        P("shard"),
        P("shard"),
        P("shard", None),
        P("shard"),
        P("shard", None),
        P("shard"),
        P(),
        P(),
        P("shard", None),
        P("shard"),
        P("shard", None),
    )
    return jax.shard_map(
        on_device, mesh=mesh, in_specs=in_specs, out_specs=out_specs, check_vma=False
    )
```

```python
import functools
import math

import jax
import jax.numpy as jnp
from jax import lax
from jax.experimental import pallas as pl
from jax.experimental.pallas import tpu as pltpu
from jax.sharding import PartitionSpec as P

FRAMES = 16
EPSILON = 1e-06
BF = jnp.bfloat16
F32 = jnp.float32
ROWS = 512
BLOCK = 128
PAIR = 128


def nn(left, right):
    return lax.dot_general(left, right, (((1,), (0,)), ((), ())), preferred_element_type=F32)


def nt(left, right):
    return lax.dot_general(left, right, (((1,), (1,)), ((), ())), preferred_element_type=F32)


def tn(left, right):
    return lax.dot_general(left, right, (((0,), (0,)), ((), ())), preferred_element_type=F32)


def normalise(values):
    centred = values - jnp.mean(values, axis=-1, keepdims=True)
    inverse = lax.rsqrt(jnp.mean(centred * centred, axis=-1, keepdims=True) + EPSILON)
    return centred * inverse, inverse


def norm_back(grad, unit, inverse, gain):
    scaled = grad * gain
    return inverse * (
        scaled
        - jnp.mean(scaled, axis=-1, keepdims=True)
        - unit * jnp.mean(scaled * unit, axis=-1, keepdims=True)
    )


def column_sum(values):
    return jnp.sum(values, axis=0, keepdims=True)


def place_masks():
    lane = lax.broadcasted_iota(jnp.int32, (FRAMES, 2 * BLOCK), 1)
    return [(lane % BLOCK) // FRAMES == p for p in range(BLOCK // FRAMES)]


def halves(width):
    lane = lax.broadcasted_iota(jnp.int32, (1, PAIR), 1)
    first = (lane < width).astype(F32)
    return first.astype(BF), (1.0 - first).astype(BF)


def compress(wide, masks):
    total = wide[:FRAMES]
    for p in range(1, len(masks)):
        total = jnp.where(masks[p], wide[p * FRAMES : (p + 1) * FRAMES], total)
    return total


def expand(packed, masks):
    zero = jnp.zeros_like(packed)
    return jnp.concatenate([jnp.where(m, packed, zero).astype(BF) for m in masks], axis=0)


def split(two, first, second):
    return jnp.concatenate([two * first, two * second], axis=0)


def stack(wide):
    return jnp.concatenate([wide[:, :BLOCK], wide[:, BLOCK:]], axis=0)


def square(ref):
    value = ref[...]
    return value.reshape(-1, value.shape[-1])


def attend_kernel(
    width, tok_ref, w_refs, vec_ref,
    q_ref, k_ref, v_ref, p_ref, mix_ref, mid_ref, top_ref,
):
    scale = 1.0 / math.sqrt(width)
    wq, wk, wv, wo = (square(w) for w in w_refs)
    gain, shift = vec_ref[0:1], vec_ref[1:2]
    tok = tok_ref[...].astype(F32)
    unit, _ = normalise(tok)
    one = (unit * gain + shift).astype(BF)
    q_ref[...] = (nn(one, wq) + vec_ref[2:3]).astype(BF)
    k_ref[...] = nn(one, wk).astype(BF)
    v_ref[...] = (nn(one, wv) + vec_ref[3:4]).astype(BF)
    masks = place_masks()
    first, second = halves(width)
    pairs = tok_ref.shape[1] // PAIR

    @pl.when(pl.program_id(0) == 0)
    def _():
        top_ref[...] = jnp.full(top_ref.shape, -3e38, F32)

    def body(i, carry):
        rows = pl.ds(pl.multiple_of(i * BLOCK, BLOCK), BLOCK)
        for h in range(pairs):
            cols = slice(h * PAIR, (h + 1) * PAIR)
            two_q, two_k, two_v = q_ref[rows, cols], k_ref[rows, cols], v_ref[rows, cols]
            scores = compress(nt(two_k, split(two_q, first, second)), masks) * scale
            top_ref[h] = jnp.maximum(top_ref[h], scores)
            expo = jnp.exp(scores - jnp.max(scores, axis=0, keepdims=True))
            probs = expo / jnp.sum(expo, axis=0, keepdims=True)
            p_ref[i, h] = probs
            mixed = tn(stack(expand(probs, masks)), split(two_v, first, second))
            mix_ref[rows, cols] = mixed.astype(BF)
        return carry

    lax.fori_loop(0, tok_ref.shape[0] // BLOCK, body, 0)
    mid_ref[...] = tok + (nn(mix_ref[...], wo) + vec_ref[4:5])


def mlp_kernel(
    chunk, mid_ref, dy_ref, w1_ref, w2_ref, vec_ref, hb_ref,
    out_ref, mg_ref, w1g_ref, w2g_ref, vg_ref, hbg_ref,
    acc1, acc2, res_ref, two_ref,
):
    step, last = pl.program_id(0), pl.num_programs(0) - 1
    gain, shift = vec_ref[5:6], vec_ref[6:7]
    mid = mid_ref[...]
    unit, inverse = normalise(mid)
    inp = (unit * gain + shift).astype(BF)
    dy = dy_ref[...]
    hidden = w1_ref.shape[1]

    @pl.when(step == 0)
    def _():
        acc1[...] = jnp.zeros_like(acc1)
        acc2[...] = jnp.zeros_like(acc2)
        vg_ref[...] = jnp.zeros_like(vg_ref)
        hbg_ref[...] = jnp.zeros_like(hbg_ref)

    res_ref[...] = mid + vec_ref[7:8]
    two_ref[...] = jnp.zeros_like(two_ref)
    root = math.sqrt(2.0 / math.pi)

    def body(j, carry):
        cols = pl.ds(pl.multiple_of(j * chunk, chunk), chunk)
        z = nn(inp, w1_ref[:, cols]) + hb_ref[:, cols]
        act_grad = nt(dy, w2_ref[cols, :])
        square = z * z
        bend = jnp.tanh(root * z * (1.0 + 0.044715 * square))
        half = 0.5 * (1.0 + bend)
        act = (z * half).astype(BF)
        slope = half + 0.5 * z * (1.0 - bend * bend) * (root * (1.0 + 0.134145 * square))
        grad = (act_grad * slope).astype(BF)
        res_ref[...] += nn(act, w2_ref[cols, :])
        two_ref[...] += nt(grad, w1_ref[:, cols])
        acc2[cols, :] += tn(act, dy)
        acc1[:, cols] += tn(inp, grad)
        hbg_ref[:, cols] += column_sum(grad.astype(F32))
        return carry

    lax.fori_loop(0, hidden // chunk, body, 0)
    out_ref[...] = res_ref[...].astype(BF)
    two = two_ref[...]
    up = dy.astype(F32)
    mg_ref[...] = up + norm_back(two, unit, inverse, gain)
    vg_ref[0:1] += column_sum(two * unit)
    vg_ref[1:2] += column_sum(two)
    vg_ref[2:3] += column_sum(up)

    @pl.when(step == last)
    def _():
        w1g_ref[...] = acc1[...].astype(BF)
        w2g_ref[...] = acc2[...].astype(BF)


def back_kernel(
    width, tok_ref, mg_ref, q_ref, k_ref, v_ref, p_ref, mix_ref,
    w_refs, vec_ref,
    gt_ref, wg_refs, vg_ref,
    accq, acck, accv, acco, mgl_ref, dq_ref, dk_ref, dv_ref,
):
    step, last = pl.program_id(0), pl.num_programs(0) - 1
    scale = 1.0 / math.sqrt(width)
    gain, shift = vec_ref[0:1], vec_ref[1:2]
    accs = (accq, acck, accv, acco)
    wq, wk, wv, wo = (square(w) for w in w_refs)

    @pl.when(step == 0)
    def _():
        for acc in accs:
            acc[...] = jnp.zeros_like(acc)
        vg_ref[...] = jnp.zeros_like(vg_ref)

    branch = mg_ref[...].astype(BF)
    mgl_ref[...] = nt(branch, wo).astype(BF)
    acco[...] += tn(mix_ref[...], branch)
    vg_ref[4:5] += column_sum(branch.astype(F32))
    masks = place_masks()
    first, second = halves(width)
    pairs = tok_ref.shape[1] // PAIR

    def body(i, carry):
        rows = pl.ds(pl.multiple_of(i * BLOCK, BLOCK), BLOCK)
        for h in range(pairs):
            cols = slice(h * PAIR, (h + 1) * PAIR)
            two_q, two_k, two_v = q_ref[rows, cols], k_ref[rows, cols], v_ref[rows, cols]
            mixed = split(mgl_ref[rows, cols], first, second)
            probs = p_ref[i, h]
            slope = compress(nt(two_v, mixed), masks)
            score = probs * (slope - jnp.sum(slope * probs, axis=0, keepdims=True))
            wide = expand(score, masks)
            dv_ref[rows, cols] = nn(expand(probs, masks), mixed).astype(BF)
            dk_ref[rows, cols] = (nn(wide, split(two_q, first, second)) * scale).astype(BF)
            dq_ref[rows, cols] = (tn(stack(wide), split(two_k, first, second)) * scale).astype(BF)
        return carry

    lax.fori_loop(0, tok_ref.shape[0] // BLOCK, body, 0)
    unit, inverse = normalise(tok_ref[...].astype(F32))
    one = (unit * gain + shift).astype(BF)
    dq, dk, dv = dq_ref[...], dk_ref[...], dv_ref[...]
    vg_ref[2:3] += column_sum(dq.astype(F32))
    vg_ref[3:4] += column_sum(dv.astype(F32))
    accq[...] += tn(one, dq)
    acck[...] += tn(one, dk)
    accv[...] += tn(one, dv)
    grad = nt(dq, wq) + nt(dk, wk) + nt(dv, wv)
    vg_ref[0:1] += column_sum(grad * unit)
    vg_ref[1:2] += column_sum(grad)
    gt_ref[...] = (mg_ref[...] + norm_back(grad, unit, inverse, gain)).astype(BF)

    @pl.when(step == last)
    def _():
        for i, acc in enumerate(accs):
            value = acc[...].astype(BF)
            if len(wg_refs) == 1:
                rows = wg_refs[0].shape[1] // 4
                wg_refs[0][:, i * rows : (i + 1) * rows, :] = value.reshape(-1, rows, value.shape[1])
            else:
                wg_refs[i][...] = value


def whole(shape):
    return pl.BlockSpec(shape, lambda i: (0,) * len(shape), pipeline_mode=pl.Buffered(1))


def tiles(height, width):
    return pl.BlockSpec((height, width), lambda i: (i, 0))


def shaped(shape, dtype):
    return jax.ShapeDtypeStruct(shape, dtype)


VMEM_LIMIT = 60 * 1024 * 1024


def params():
    return pltpu.CompilerParams(
        dimension_semantics=("arbitrary",), vmem_limit_bytes=VMEM_LIMIT
    )


def weight_specs(weights):
    if len(weights) == 1:
        shards, rows, d = weights[0].shape
        return [
            pl.BlockSpec((shards, rows // 4, d), lambda i, j=j: (0, j, 0), pipeline_mode=pl.Buffered(1))
            for j in range(4)
        ]
    return [whole(w.shape) for w in weights]


def four(weights):
    return tuple(weights) * (4 // len(weights))


def attend(tokens, weights, vec, heads):
    rows, d = tokens.shape
    t = min(ROWS, rows)
    pairs = d // PAIR
    blocks = rows // BLOCK
    big = tiles(t, d)
    return pl.pallas_call(
        lambda tok, wq, wk, wv, wo, *refs: attend_kernel(d // heads, tok, (wq, wk, wv, wo), *refs),
        grid=(rows // t,),
        in_specs=[big] + weight_specs(weights) + [whole(vec.shape)],
        out_specs=[
            big, big, big,
            pl.BlockSpec((t // BLOCK, pairs, FRAMES, 2 * BLOCK), lambda i: (i, 0, 0, 0)),
            big, big,
            whole((pairs, FRAMES, 2 * BLOCK)),
        ],
        out_shape=[shaped((rows, d), BF)] * 3
        + [shaped((blocks, pairs, FRAMES, 2 * BLOCK), F32), shaped((rows, d), BF), shaped((rows, d), F32)]
        + [shaped((pairs, FRAMES, 2 * BLOCK), F32)],
        compiler_params=params(),
        cost_estimate=pl.CostEstimate(flops=10 * rows * d * d, bytes_accessed=24 * rows * d, transcendentals=0),
        name="attend",
    )(tokens, *four(weights), vec)


def mlp(middle, dy, w1, w2, vec, hb):
    rows, d = middle.shape
    hidden = w1.shape[1]
    t = min(ROWS, rows)
    big = tiles(t, d)
    return pl.pallas_call(
        lambda *refs: mlp_kernel(768, *refs),
        grid=(rows // t,),
        in_specs=[big, big, whole(w1.shape), whole(w2.shape), whole(vec.shape), whole(hb.shape)],
        out_specs=[big, big, whole(w1.shape), whole(w2.shape), whole((8, d)), whole((1, hidden))],
        out_shape=[
            shaped((rows, d), BF), shaped((rows, d), F32), shaped(w1.shape, BF), shaped(w2.shape, BF),
            shaped((8, d), F32), shaped((1, hidden), F32),
        ],
        scratch_shapes=[
            pltpu.VMEM(w1.shape, F32), pltpu.VMEM(w2.shape, F32), pltpu.VMEM((t, d), F32), pltpu.VMEM((t, d), F32),
        ],
        compiler_params=params(),
        cost_estimate=pl.CostEstimate(flops=12 * rows * d * hidden, bytes_accessed=14 * rows * d, transcendentals=0),
        name="mlp",
    )(middle, dy, w1, w2, vec, hb)


def back(tokens, mg, q, k, v, p, mixed, weights, vec, heads):
    rows, d = tokens.shape
    t = min(ROWS, rows)
    pairs = d // PAIR
    big = tiles(t, d)
    count = len(weights)

    def kernel(*refs):
        ins, w_refs, vec_ref, gt_ref = refs[:7], refs[7:11], refs[11], refs[12]
        wg_refs, rest = refs[13 : 13 + count], refs[13 + count :]
        back_kernel(d // heads, *ins, w_refs, vec_ref, gt_ref, wg_refs, *rest)

    out = pl.pallas_call(
        kernel,
        grid=(rows // t,),
        in_specs=[
            big, big, big, big, big,
            pl.BlockSpec((t // BLOCK, pairs, FRAMES, 2 * BLOCK), lambda i: (i, 0, 0, 0)),
            big,
        ] + weight_specs(weights) + [whole(vec.shape)],
        out_specs=[big] + [whole(w.shape) for w in weights] + [whole((8, d))],
        out_shape=[shaped((rows, d), BF)] + [shaped(w.shape, BF) for w in weights] + [shaped((8, d), F32)],
        scratch_shapes=[pltpu.VMEM((d, d), F32)] * 4 + [pltpu.VMEM((t, d), BF)] * 4,
        compiler_params=params(),
        cost_estimate=pl.CostEstimate(flops=20 * rows * d * d, bytes_accessed=24 * rows * d, transcendentals=0),
        name="back",
    )(tokens, mg, q, k, v, p, mixed, *four(weights), vec)
    return out[0], out[1 : 1 + count], out[1 + count]


MESH = pl.DeviceIdType.MESH


class Place:
    def __init__(self, shards):
        self.shards = shards
        self.depth = shards // 4
        self.me = lax.axis_index("shard")
        self.core = lax.axis_index("rep")
        self.zed = self.me // 4
        x, y = self.me % 2, (self.me // 2) % 2
        self.near_step, self.far_step = 1 + self.core, 2 - self.core
        self.near = x + self.core * (y - x)
        self.far = y + self.core * (x - y)
        self.sibling = (self.me, 1 - self.core)
        self.near_peer = (self.block(self.zed, 1 - self.near, self.far), self.core)
        self.far_peer = (self.block(self.zed, self.near, 1 - self.far), self.core)
        self.columns = [lax.rem(self.zed + k, self.depth) for k in range(self.depth)]
        self.column_peers = [(self.block(z, self.near, self.far), self.core) for z in self.columns]

    def block(self, zed, near, far):
        return zed * 4 + near * self.near_step + far * self.far_step

    def greet(self):
        barrier = pltpu.get_barrier_semaphore()
        peers = [self.sibling, self.near_peer, self.far_peer] + self.column_peers[1:]
        for peer in peers:
            pl.semaphore_signal(barrier, inc=1, device_id=peer, device_id_type=MESH)
        pl.semaphore_wait(barrier, len(peers))


def half_of(ref, core):
    width = ref.shape[-1] // 2
    return pl.ds(pl.multiple_of(core * width, width), width)


class Gather:
    def __init__(self, place, full, send, recv, other):
        self.place, self.full, self.send, self.recv, self.other = place, full, send, recv, other
        self.cols = half_of(full, place.core)
        self.count = 0
        self.sent = []

    def push(self, block, peer, recv):
        view = self.full.at[block, :, self.cols]
        copy = pltpu.make_async_remote_copy(
            src_ref=view, dst_ref=view, send_sem=self.send.at[self.count], recv_sem=recv.at[block],
            device_id=peer, device_id_type=MESH,
        )
        copy.start()
        self.count += 1
        self.sent.append(copy)

    def arrived(self, block, recv, cols):
        view = self.full.at[block, :, cols]
        pltpu.make_async_remote_copy(
            src_ref=view, dst_ref=view, send_sem=self.send.at[0], recv_sem=recv.at[block],
            device_id=self.place.sibling, device_id_type=MESH,
        ).wait_recv()

    def own(self):
        p = self.place
        for peer in p.column_peers[1:]:
            self.push(p.me, peer, self.recv)
        self.push(p.me, p.near_peer, self.recv)
        self.push(p.me, p.far_peer, self.recv)

    def column(self):
        p = self.place
        for z in p.columns[1:]:
            block = p.block(z, p.near, p.far)
            self.arrived(block, self.recv, self.cols)
            self.push(block, p.near_peer, self.recv)
            self.push(block, p.far_peer, self.recv)
            self.push(block, p.sibling, self.other)

    def plane(self):
        p = self.place
        for z in p.columns:
            block = p.block(z, 1 - p.near, p.far)
            self.arrived(block, self.recv, self.cols)
            self.push(block, p.far_peer, self.recv)
            self.push(block, p.sibling, self.other)

    def rest(self):
        p = self.place
        for z in p.columns:
            for near in (p.near, 1 - p.near):
                block = p.block(z, near, 1 - p.far)
                self.arrived(block, self.recv, self.cols)
                self.push(block, p.sibling, self.other)

    def finish(self):
        p = self.place
        cols = half_of(self.full, 1 - p.core)
        for k in range(1, p.shards):
            self.arrived(lax.rem(p.me + k, p.shards), self.other, cols)
        for copy in self.sent:
            copy.wait_send()

    def sends(shards):
        return 3 * (shards // 4) + (shards // 4 - 1) + shards // 4 + shards - 1


def gather_kernel(shards, wq, wk, wv, wo, w1, w2, small, attn_out, w1_out, w2_out, small_out, local, send, recv, other):
    p = Place(shards)
    rows = wq.shape[0]
    copies = [
        pltpu.make_async_copy(w, attn_out.at[p.me, pl.ds(i * rows, rows), :], local.at[i])
        for i, w in enumerate((wq, wk, wv, wo))
    ] + [
        pltpu.make_async_copy(w, out.at[p.me], local.at[4 + i])
        for i, (w, out) in enumerate(((w1, w1_out), (w2, w2_out), (small, small_out)))
    ]
    for copy in copies:
        copy.start()
    p.greet()
    for copy in copies:
        copy.wait()
    s, a, b, c = (
        Gather(p, full, send.at[i], recv.at[i], other.at[i])
        for i, full in enumerate((small_out, attn_out, w1_out, w2_out))
    )
    s.own(), a.own(), b.own(), s.column(), a.column(), c.own()
    s.plane(), a.plane(), b.column(), s.rest(), b.plane(), c.column(), c.plane()
    a.rest(), b.rest(), c.rest()
    for g in (s, a, b, c):
        g.finish()


def gather_all(shards, wq, wk, wv, wo, w1, w2, small):
    rows, d = wq.shape
    sends = Gather.sends(shards)
    anywhere = pl.BlockSpec(memory_space=pl.ANY)
    return pl.pallas_call(
        lambda *refs: gather_kernel(shards, *refs),
        in_specs=[pl.BlockSpec(memory_space=pltpu.VMEM)] * 7,
        out_specs=[anywhere] * 4,
        out_shape=[
            shaped((shards, 4 * rows, d), BF), shaped((shards,) + w1.shape, BF), shaped((shards,) + w2.shape, BF),
            shaped((shards,) + small.shape, F32),
        ],
        scratch_shapes=[
            pltpu.SemaphoreType.DMA((7,)), pltpu.SemaphoreType.DMA((4, sends)),
            pltpu.SemaphoreType.DMA((4, shards)), pltpu.SemaphoreType.DMA((4, shards)),
        ],
        compiler_params=pltpu.CompilerParams(collective_id=0, has_side_effects=True),
        name="gather",
    )(wq, wk, wv, wo, w1, w2, small)


class Scatter:
    def kinds(shards, rows, cols, dtype):
        depth, half = shards // 4, cols // 2
        many = lambda *lead: pltpu.VMEM(lead + (rows, half), dtype)
        return [
            many(shards), many(shards), many(depth, 2), many(depth, 2), many(depth), many(depth),
            many(depth - 1), many(depth - 1), pltpu.VMEM((rows, half), F32), pltpu.VMEM((rows, half), F32),
            pltpu.SemaphoreType.DMA((depth,)), pltpu.SemaphoreType.DMA((4 * depth,)), pltpu.SemaphoreType.DMA((4 * depth,)),
        ]

    def __init__(self, place, full, out, scratch):
        self.p, self.full, self.out = place, full, out
        (self.mine, self.got_one, self.send_two, self.got_two, self.send_three, self.got_three,
         self.send_four, self.got_four, self.total, self.joined, self.local, self.send, self.recv) = scratch
        self.sent = []

    def copy(self, src, dst, slot, peer):
        return pltpu.make_async_remote_copy(
            src_ref=src, dst_ref=dst, send_sem=self.send.at[slot], recv_sem=self.recv.at[slot],
            device_id=peer, device_id_type=MESH,
        )

    def push(self, src, dst, slot, peer):
        copy = self.copy(src, dst, slot, peer)
        copy.start()
        self.sent.append(copy)

    def order(self):
        return self.p.columns[1:] + self.p.columns[:1]

    def first(self):
        p = self.p
        for z in self.order():
            rows = pl.ds(4 * z, 4)
            self.push(self.full.at[rows, :, half_of(self.full, 1 - p.core)], self.got_one.at[rows], z, p.sibling)
        for z in self.order():
            self.load(z).start()

    def load(self, z):
        rows = pl.ds(4 * z, 4)
        return pltpu.make_async_copy(
            self.full.at[rows, :, half_of(self.full, self.p.core)], self.mine.at[rows], self.local.at[z]
        )

    def pair(self, block):
        return self.mine[block].astype(F32) + self.got_one[block].astype(F32)

    def second(self):
        p, d = self.p, self.p.depth
        for z in self.order():
            rows = pl.ds(4 * z, 4)
            self.load(z).wait()
            self.copy(self.got_one.at[rows], self.got_one.at[rows], z, p.sibling).wait_recv()
            for near in range(2):
                block = p.block(z, near, 1 - p.far)
                self.send_two[z, near] = self.pair(block).astype(self.mine.dtype)
            self.push(self.send_two.at[z], self.got_two.at[z], d + z, p.far_peer)

    def third(self):
        p, d = self.p, self.p.depth
        for z in self.order():
            self.copy(self.send_two.at[z], self.got_two.at[z], d + z, p.far_peer).wait_recv()
            block = p.block(z, 1 - p.near, p.far)
            value = self.pair(block) + self.got_two[z, 1 - p.near].astype(F32)
            self.send_three[z] = value.astype(self.mine.dtype)
            self.push(self.send_three.at[z], self.got_three.at[z], 2 * d + z, p.near_peer)

    def triple(self, z):
        p, d = self.p, self.p.depth
        self.copy(self.send_three.at[z], self.got_three.at[z], 2 * d + z, p.near_peer).wait_recv()
        block = p.block(z, p.near, p.far)
        return self.pair(block) + self.got_two[z, p.near].astype(F32) + self.got_three[z].astype(F32)

    def fourth(self):
        p, d = self.p, self.p.depth
        for k in range(1, d):
            self.send_four[k - 1] = self.triple(p.columns[k]).astype(self.mine.dtype)
            self.push(self.send_four.at[k - 1], self.got_four.at[k - 1], 3 * d + k - 1, p.column_peers[k])

    def fifth(self):
        p, d = self.p, self.p.depth
        value = self.triple(p.zed)
        for k in range(1, d):
            self.copy(self.send_four.at[k - 1], self.got_four.at[k - 1], 3 * d + k - 1, p.column_peers[k]).wait_recv()
            value = value + self.got_four[k - 1].astype(F32)
        self.total[...] = value
        self.push(self.total, self.joined, 4 * d - 1, p.sibling)
        self.out[:, half_of(self.out, p.core)] = value

    def finish(self):
        p, d = self.p, self.p.depth
        self.copy(self.total, self.joined, 4 * d - 1, p.sibling).wait_recv()
        self.out[:, half_of(self.out, 1 - p.core)] = self.joined[...]
        for copy in self.sent:
            copy.wait_send()


class Largest:
    def __init__(self, place, own, out, got, kept, send, recv):
        self.p, self.own, self.out, self.got, self.kept, self.send, self.recv = place, own, out, got, kept, send, recv
        self.sent = []
        d = place.depth
        self.stages = [
            [(place.sibling, 0)], [(place.far_peer, 1)], [(place.near_peer, 2)],
            [(place.column_peers[k], 2 + k) for k in range(1, d)],
        ]

    def push(self, stage):
        if stage == 0:
            self.kept[0] = self.own[...]
        for peer, slot in self.stages[stage]:
            copy = pltpu.make_async_remote_copy(
                src_ref=self.kept.at[stage], dst_ref=self.got.at[slot], send_sem=self.send.at[slot],
                recv_sem=self.recv.at[slot], device_id=peer, device_id_type=MESH,
            )
            copy.start()
            self.sent.append((copy, stage))

    def take(self, stage):
        value = self.kept[stage]
        for (copy, s), (_, slot) in zip([c for c in self.sent if c[1] == stage], self.stages[stage]):
            copy.wait_recv()
            value = jnp.maximum(value, self.got[slot])
        if stage == 3:
            self.out[...] = value
            for copy, _ in self.sent:
                copy.wait_send()
        else:
            self.kept[stage + 1] = value


def scatter_kernel(shards, *refs):
    (attn, w1, w2, small, top, attn_out, w1_out, w2_out, small_out, top_out), scratch = refs[:10], refs[10:]
    p = Place(shards)
    count = len(scratch) // 4
    s, a, b, c = (
        Scatter(p, full, out, scratch[13 * i : 13 * i + 13])
        for i, (full, out) in enumerate(((small, small_out), (attn, attn_out), (w1, w1_out), (w2, w2_out)))
    )
    t = Largest(p, top, top_out, *scratch[52:])
    p.greet()
    t.push(0)
    for g in (s, c, b, a):
        g.first()
    s.second(), t.take(0), t.push(1), c.second(), s.third(), b.second(), c.third(), a.second(), b.third()
    t.take(1), t.push(2), s.fourth(), c.fourth(), a.third(), b.fourth(), a.fourth()
    t.take(2), t.push(3), s.fifth(), c.fifth(), b.fifth(), a.fifth(), t.take(3)
    for g in (s, c, b, a):
        g.finish()


def scatter_all(shards, attn, w1, w2, small, top):
    depth = shards // 4
    arrays = ((small, F32), (attn, BF), (w1, BF), (w2, BF))
    scratch = sum((Scatter.kinds(shards, x.shape[1], x.shape[2], dtype) for x, dtype in arrays), [])
    scratch += [
        pltpu.VMEM((depth + 2, 8, 128), F32), pltpu.VMEM((4, 8, 128), F32),
        pltpu.SemaphoreType.DMA((depth + 2,)), pltpu.SemaphoreType.DMA((depth + 2,)),
    ]
    anywhere, inside = pl.BlockSpec(memory_space=pl.ANY), pl.BlockSpec(memory_space=pltpu.VMEM)
    return pl.pallas_call(
        lambda *refs: scatter_kernel(shards, *refs),
        in_specs=[anywhere] * 4 + [inside],
        out_specs=[inside] * 5,
        out_shape=[shaped(x.shape[1:], F32) for x in (attn, w1, w2, small)] + [shaped((8, 128), F32)],
        scratch_shapes=scratch,
        compiler_params=pltpu.CompilerParams(collective_id=1, has_side_effects=True, vmem_limit_bytes=VMEM_LIMIT),
        name="scatter",
    )(attn, w1, w2, small, top)


def on_device(shards, reps, *args):
    (
        tokens, grad_out, first_gain, first_shift, query_proj, query_bias, key_proj, value_proj, value_bias,
        output_proj, output_bias, second_gain, second_shift, hidden_proj, hidden_bias, final_proj, final_bias, threshold,
    ) = args
    heads = threshold.shape[0]
    d = tokens.shape[1]
    hidden = hidden_proj.shape[1]
    head_dim = d // heads
    small = (first_gain, first_shift, query_bias, value_bias, output_bias, second_gain, second_shift, final_bias)
    rows, more = small[0].shape[0], hidden_bias.shape[0] // 8
    own = reps == 2 and shards % 4 == 0 and shards > 4 and rows % 16 == 0 and rows <= 128 and more <= 128

    def gather(x):
        return lax.all_gather(x, "shard", axis=0, tiled=True)

    def scatter(x):
        y = lax.psum_scatter(x.astype(BF), "shard", scatter_dimension=0, tiled=True)
        return lax.psum(y, "rep").astype(F32)

    if own:
        tile = jnp.concatenate(
            [
                jnp.pad(jnp.stack(small).astype(F32), ((0, 0), (0, 128 - rows))),
                jnp.pad(hidden_bias.astype(F32).reshape(8, more), ((0, 0), (0, 128 - more))),
            ],
            axis=1,
        )
        attn, w1, w2, tile = gather_all(
            shards, query_proj, key_proj, value_proj, output_proj, hidden_proj, final_proj, tile
        )
        weights = (attn,)
        w1, w2 = w1.reshape(d, hidden), w2.reshape(hidden, d)
        vec = jnp.moveaxis(tile[:, :, :rows], 0, 1).reshape(8, d)
        hb = tile[:, :, 128 : 128 + more].reshape(1, hidden)
    else:
        weights = tuple(gather(x) for x in (query_proj, key_proj, value_proj, output_proj))
        w1, w2 = gather(hidden_proj), gather(final_proj)
        vec = jnp.stack([gather(x) for x in small]).astype(F32)
        hb = gather(hidden_bias).astype(F32)[None]
    q, k, v, p, mixed, middle, top = attend(tokens, weights, vec, heads)
    local = jnp.max(top.reshape(top.shape[0], FRAMES, 2, BLOCK), axis=(1, 3)).reshape(heads)
    layer_output, mg, w1g, w2g, vg2, hbg = mlp(middle, grad_out, w1, w2, vec, hb)
    grad_tokens, wg, vg1 = back(tokens, mg, q, k, v, p, mixed, weights, vec, heads)
    vg = jnp.concatenate([vg1[:5], vg2[:3]])
    if own:
        tile = jnp.concatenate(
            [
                jnp.pad(jnp.moveaxis(vg.reshape(8, shards, rows), 1, 0), ((0, 0), (0, 0), (0, 128 - rows))),
                jnp.pad(hbg.reshape(shards, 8, more), ((0, 0), (0, 0), (0, 128 - more))),
            ],
            axis=2,
        )
        attn, w1g, w2g, tile, top = scatter_all(
            shards, wg[0], w1g.reshape(shards, -1, hidden), w2g.reshape(shards, -1, d), tile,
            jnp.broadcast_to(jnp.pad(local, (0, 128 - heads))[None], (8, 128)),
        )
        wg = tuple(attn[i * rows : (i + 1) * rows] for i in range(4))
        vg = tuple(tile[i, :rows] for i in range(8))
        hbg = tile[:, 128 : 128 + more].reshape(-1)
        global_max = top[0, :heads]
    else:
        global_max = lax.pmax(local, ("shard", "rep"))
        wg = tuple(scatter(x) for x in wg)
        w1g, w2g = scatter(w1g), scatter(w2g)
        vg = tuple(scatter(vg[i]) for i in range(8))
        hbg = scatter(hbg[0])
    factor = jnp.minimum(1.0, threshold / global_max)
    column_scale = jnp.repeat(jnp.sqrt(factor), head_dim)
    bias_scale = lax.dynamic_slice_in_dim(column_scale, lax.axis_index("shard") * rows, rows)
    return (
        layer_output, grad_tokens, vg[0], vg[1], wg[0], vg[2], wg[1], wg[2], vg[3], wg[3], vg[4], vg[5], vg[6],
        w1g, hbg, w2g, vg[7], global_max, factor,
        query_proj.astype(F32) * column_scale[None, :], query_bias.astype(F32) * bias_scale,
        key_proj.astype(F32) * column_scale[None, :],
    )


def solution(mesh):
    in_specs = (
        P(("shard", "rep"), None),
        P(("shard", "rep"), None),
        P("shard"),
        P("shard"),
        P("shard", None),
        P("shard"),
        P("shard", None),
        P("shard", None),
        P("shard"),
        P("shard", None),
        P("shard"),
        P("shard"),
        P("shard"),
        P("shard", None),
        P("shard"),
        P("shard", None),
        P("shard"),
        P(),
    )
    out_specs = (
        P(("shard", "rep"), None),
        P(("shard", "rep"), None),
        P("shard"),
        P("shard"),
        P("shard", None),
        P("shard"),
        P("shard", None),
        P("shard", None),
        P("shard"),
        P("shard", None),
        P("shard"),
        P("shard"),
        P("shard"),
        P("shard", None),
        P("shard"),
        P("shard", None),
        P("shard"),
        P(),
        P(),
        P("shard", None),
        P("shard"),
        P("shard", None),
    )
    shards, reps = mesh.shape["shard"], mesh.shape["rep"]
    return jax.shard_map(
        functools.partial(on_device, shards, reps), mesh=mesh, in_specs=in_specs, out_specs=out_specs, check_vma=False
    )
```

```python
import functools
import math

import jax
import jax.numpy as jnp
from jax import lax
from jax.experimental import pallas as pl
from jax.experimental.pallas import tpu as pltpu
from jax.sharding import PartitionSpec as P

FRAMES = 16
EPSILON = 1e-06
BF = jnp.bfloat16
F32 = jnp.float32
ROWS = 512
BLOCK = 128
PAIR = 128


def nn(left, right):
    return lax.dot_general(left, right, (((1,), (0,)), ((), ())), preferred_element_type=F32)


def nt(left, right):
    return lax.dot_general(left, right, (((1,), (1,)), ((), ())), preferred_element_type=F32)


def tn(left, right):
    return lax.dot_general(left, right, (((0,), (0,)), ((), ())), preferred_element_type=F32)


def normalise(values):
    centred = values - jnp.mean(values, axis=-1, keepdims=True)
    inverse = lax.rsqrt(jnp.mean(centred * centred, axis=-1, keepdims=True) + EPSILON)
    return centred * inverse, inverse


def norm_back(grad, unit, inverse, gain):
    scaled = grad * gain
    return inverse * (
        scaled
        - jnp.mean(scaled, axis=-1, keepdims=True)
        - unit * jnp.mean(scaled * unit, axis=-1, keepdims=True)
    )


def column_sum(values):
    return jnp.sum(values, axis=0, keepdims=True)


def place_masks():
    lane = lax.broadcasted_iota(jnp.int32, (FRAMES, 2 * BLOCK), 1)
    return [(lane % BLOCK) // FRAMES == p for p in range(BLOCK // FRAMES)]


def halves(width):
    lane = lax.broadcasted_iota(jnp.int32, (1, PAIR), 1)
    first = (lane < width).astype(F32)
    return first.astype(BF), (1.0 - first).astype(BF)


def compress(wide, masks):
    total = wide[:FRAMES]
    for p in range(1, len(masks)):
        total = jnp.where(masks[p], wide[p * FRAMES : (p + 1) * FRAMES], total)
    return total


def expand(packed, masks):
    zero = jnp.zeros_like(packed)
    return jnp.concatenate([jnp.where(m, packed, zero).astype(BF) for m in masks], axis=0)


def split(two, first, second):
    return jnp.concatenate([two * first, two * second], axis=0)


def stack(wide):
    return jnp.concatenate([wide[:, :BLOCK], wide[:, BLOCK:]], axis=0)


def square(ref):
    value = ref[...]
    return value.reshape(-1, value.shape[-1])


def attend_kernel(
    width, tok_ref, w_refs, vec_ref,
    q_ref, k_ref, v_ref, p_ref, mix_ref, mid_ref, top_ref, tick=lambda point: None,
):
    scale = 1.0 / math.sqrt(width)
    wq, wk, wv, wo = (square(w) for w in w_refs)
    gain, shift = vec_ref[0:1], vec_ref[1:2]
    tok = tok_ref[...].astype(F32)
    unit, _ = normalise(tok)
    one = (unit * gain + shift).astype(BF)
    q_ref[...] = (nn(one, wq) + vec_ref[2:3]).astype(BF)
    k_ref[...] = nn(one, wk).astype(BF)
    v_ref[...] = (nn(one, wv) + vec_ref[3:4]).astype(BF)
    tick(1)
    masks = place_masks()
    first, second = halves(width)
    pairs = tok_ref.shape[1] // PAIR

    @pl.when(pl.program_id(0) == 0)
    def _():
        top_ref[...] = jnp.full(top_ref.shape, -3e38, F32)

    def body(i, carry):
        rows = pl.ds(pl.multiple_of(i * BLOCK, BLOCK), BLOCK)
        for h in range(pairs):
            cols = slice(h * PAIR, (h + 1) * PAIR)
            two_q, two_k, two_v = q_ref[rows, cols], k_ref[rows, cols], v_ref[rows, cols]
            scores = compress(nt(two_k, split(two_q, first, second)), masks) * scale
            top_ref[h] = jnp.maximum(top_ref[h], scores)
            expo = jnp.exp(scores - jnp.max(scores, axis=0, keepdims=True))
            probs = expo / jnp.sum(expo, axis=0, keepdims=True)
            p_ref[i, h] = probs
            mixed = tn(stack(expand(probs, masks)), split(two_v, first, second))
            mix_ref[rows, cols] = mixed.astype(BF)
        return carry

    lax.fori_loop(0, tok_ref.shape[0] // BLOCK, body, 0)
    tick(2)
    mid_ref[...] = tok_ref[...].astype(F32) + (nn(mix_ref[...], wo) + vec_ref[4:5])
    tick(3)


def mlp_kernel(
    chunk, mid_ref, dy_ref, w1_ref, w2_ref, vec_ref, hb_ref,
    out_ref, mg_ref, w1g_ref, w2g_ref, vg_ref, hbg_ref,
    acc1, acc2, res_ref, two_ref,
):
    step, last = pl.program_id(0), pl.num_programs(0) - 1
    gain, shift = vec_ref[5:6], vec_ref[6:7]
    mid = mid_ref[...]
    unit, inverse = normalise(mid)
    inp = (unit * gain + shift).astype(BF)
    dy = dy_ref[...]
    hidden = w1_ref.shape[1]

    @pl.when(step == 0)
    def _():
        acc1[...] = jnp.zeros_like(acc1)
        acc2[...] = jnp.zeros_like(acc2)
        vg_ref[...] = jnp.zeros_like(vg_ref)
        hbg_ref[...] = jnp.zeros_like(hbg_ref)

    res_ref[...] = mid + vec_ref[7:8]
    two_ref[...] = jnp.zeros_like(two_ref)
    root = math.sqrt(2.0 / math.pi)

    def body(j, carry):
        cols = pl.ds(pl.multiple_of(j * chunk, chunk), chunk)
        z = nn(inp, w1_ref[:, cols]) + hb_ref[:, cols]
        act_grad = nt(dy, w2_ref[cols, :])
        square = z * z
        bend = jnp.tanh(root * z * (1.0 + 0.044715 * square))
        half = 0.5 * (1.0 + bend)
        act = (z * half).astype(BF)
        slope = half + 0.5 * z * (1.0 - bend * bend) * (root * (1.0 + 0.134145 * square))
        grad = (act_grad * slope).astype(BF)
        res_ref[...] += nn(act, w2_ref[cols, :])
        two_ref[...] += nt(grad, w1_ref[:, cols])
        acc2[cols, :] += tn(act, dy)
        acc1[:, cols] += tn(inp, grad)
        hbg_ref[:, cols] += column_sum(grad.astype(F32))
        return carry

    lax.fori_loop(0, hidden // chunk, body, 0)
    out_ref[...] = res_ref[...].astype(BF)
    two = two_ref[...]
    up = dy.astype(F32)
    mg_ref[...] = up + norm_back(two, unit, inverse, gain)
    vg_ref[0:1] += column_sum(two * unit)
    vg_ref[1:2] += column_sum(two)
    vg_ref[2:3] += column_sum(up)

    @pl.when(step == last)
    def _():
        w1g_ref[...] = acc1[...].astype(BF)
        w2g_ref[...] = acc2[...].astype(BF)


def back_kernel(
    width, tok_ref, mg_ref, q_ref, k_ref, v_ref, p_ref, mix_ref,
    w_refs, vec_ref,
    gt_ref, wg_refs, vg_ref,
    accq, acck, accv, acco, mgl_ref, dq_ref, dk_ref, dv_ref, tick=lambda point: None,
):
    step, last = pl.program_id(0), pl.num_programs(0) - 1
    scale = 1.0 / math.sqrt(width)
    gain, shift = vec_ref[0:1], vec_ref[1:2]
    accs = (accq, acck, accv, acco)
    wq, wk, wv, wo = (square(w) for w in w_refs)

    @pl.when(step == 0)
    def _():
        for acc in accs:
            acc[...] = jnp.zeros_like(acc)
        vg_ref[...] = jnp.zeros_like(vg_ref)

    tick(0)
    branch = mg_ref[...].astype(BF)
    mgl_ref[...] = nt(branch, wo).astype(BF)
    acco[...] += tn(mix_ref[...], branch)
    vg_ref[4:5] += column_sum(branch.astype(F32))
    tick(1)
    masks = place_masks()
    first, second = halves(width)
    pairs = tok_ref.shape[1] // PAIR

    def body(i, carry):
        rows = pl.ds(pl.multiple_of(i * BLOCK, BLOCK), BLOCK)
        for h in range(pairs):
            cols = slice(h * PAIR, (h + 1) * PAIR)
            two_q, two_k, two_v = q_ref[rows, cols], k_ref[rows, cols], v_ref[rows, cols]
            mixed = split(mgl_ref[rows, cols], first, second)
            probs = p_ref[i, h]
            slope = compress(nt(two_v, mixed), masks)
            score = probs * (slope - jnp.sum(slope * probs, axis=0, keepdims=True))
            wide = expand(score, masks)
            dv_ref[rows, cols] = nn(expand(probs, masks), mixed).astype(BF)
            dk_ref[rows, cols] = (nn(wide, split(two_q, first, second)) * scale).astype(BF)
            dq_ref[rows, cols] = (tn(stack(wide), split(two_k, first, second)) * scale).astype(BF)
        return carry

    lax.fori_loop(0, tok_ref.shape[0] // BLOCK, body, 0)
    tick(2)
    unit, inverse = normalise(tok_ref[...].astype(F32))
    one = (unit * gain + shift).astype(BF)
    dq, dk, dv = dq_ref[...], dk_ref[...], dv_ref[...]
    vg_ref[2:3] += column_sum(dq.astype(F32))
    vg_ref[3:4] += column_sum(dv.astype(F32))
    accq[...] += tn(one, dq)
    acck[...] += tn(one, dk)
    accv[...] += tn(one, dv)
    tick(3)
    grad = nt(dq, wq) + nt(dk, wk) + nt(dv, wv)
    vg_ref[0:1] += column_sum(grad * unit)
    vg_ref[1:2] += column_sum(grad)
    gt_ref[...] = (mg_ref[...] + norm_back(grad, unit, inverse, gain)).astype(BF)
    tick(4)

    @pl.when(step == last)
    def _():
        for i, acc in enumerate(accs):
            value = acc[...].astype(BF)
            if len(wg_refs) == 1:
                rows = wg_refs[0].shape[1] // 4
                wg_refs[0][:, i * rows : (i + 1) * rows, :] = value.reshape(-1, rows, value.shape[1])
            else:
                wg_refs[i][...] = value


def whole(shape):
    return pl.BlockSpec(shape, lambda i: (0,) * len(shape), pipeline_mode=pl.Buffered(1))


def tiles(height, width):
    return pl.BlockSpec((height, width), lambda i: (i, 0))


def shaped(shape, dtype):
    return jax.ShapeDtypeStruct(shape, dtype)


VMEM_LIMIT = 60 * 1024 * 1024


def params():
    return pltpu.CompilerParams(
        dimension_semantics=("arbitrary",), vmem_limit_bytes=VMEM_LIMIT
    )


def weight_specs(weights):
    if len(weights) == 1:
        shards, rows, d = weights[0].shape
        return [
            pl.BlockSpec((shards, rows // 4, d), lambda i, j=j: (0, j, 0), pipeline_mode=pl.Buffered(1))
            for j in range(4)
        ]
    return [whole(w.shape) for w in weights]


def four(weights):
    return tuple(weights) * (4 // len(weights))


def attend(tokens, weights, vec, heads):
    rows, d = tokens.shape
    t = min(ROWS, rows)
    pairs = d // PAIR
    blocks = rows // BLOCK
    big = tiles(t, d)
    return pl.pallas_call(
        lambda tok, wq, wk, wv, wo, *refs: attend_kernel(d // heads, tok, (wq, wk, wv, wo), *refs),
        grid=(rows // t,),
        in_specs=[big] + weight_specs(weights) + [whole(vec.shape)],
        out_specs=[
            big, big, big,
            pl.BlockSpec((t // BLOCK, pairs, FRAMES, 2 * BLOCK), lambda i: (i, 0, 0, 0)),
            big, big,
            whole((pairs, FRAMES, 2 * BLOCK)),
        ],
        out_shape=[shaped((rows, d), BF)] * 3
        + [shaped((blocks, pairs, FRAMES, 2 * BLOCK), F32), shaped((rows, d), BF), shaped((rows, d), F32)]
        + [shaped((pairs, FRAMES, 2 * BLOCK), F32)],
        compiler_params=params(),
        cost_estimate=pl.CostEstimate(flops=10 * rows * d * d, bytes_accessed=24 * rows * d, transcendentals=0),
        name="attend",
    )(tokens, *four(weights), vec)


def mlp(middle, dy, w1, w2, vec, hb):
    rows, d = middle.shape
    hidden = w1.shape[1]
    t = min(ROWS, rows)
    big = tiles(t, d)
    return pl.pallas_call(
        lambda *refs: mlp_kernel(768, *refs),
        grid=(rows // t,),
        in_specs=[big, big, whole(w1.shape), whole(w2.shape), whole(vec.shape), whole(hb.shape)],
        out_specs=[big, big, whole(w1.shape), whole(w2.shape), whole((8, d)), whole((1, hidden))],
        out_shape=[
            shaped((rows, d), BF), shaped((rows, d), F32), shaped(w1.shape, BF), shaped(w2.shape, BF),
            shaped((8, d), F32), shaped((1, hidden), F32),
        ],
        scratch_shapes=[
            pltpu.VMEM(w1.shape, F32), pltpu.VMEM(w2.shape, F32), pltpu.VMEM((t, d), F32), pltpu.VMEM((t, d), F32),
        ],
        compiler_params=params(),
        cost_estimate=pl.CostEstimate(flops=12 * rows * d * hidden, bytes_accessed=14 * rows * d, transcendentals=0),
        name="mlp",
    )(middle, dy, w1, w2, vec, hb)


def back(tokens, mg, q, k, v, p, mixed, weights, vec, heads):
    rows, d = tokens.shape
    t = min(ROWS, rows)
    pairs = d // PAIR
    big = tiles(t, d)
    count = len(weights)

    def kernel(*refs):
        ins, w_refs, vec_ref, gt_ref = refs[:7], refs[7:11], refs[11], refs[12]
        wg_refs, rest = refs[13 : 13 + count], refs[13 + count :]
        back_kernel(d // heads, *ins, w_refs, vec_ref, gt_ref, wg_refs, *rest)

    out = pl.pallas_call(
        kernel,
        grid=(rows // t,),
        in_specs=[
            big, big, big, big, big,
            pl.BlockSpec((t // BLOCK, pairs, FRAMES, 2 * BLOCK), lambda i: (i, 0, 0, 0)),
            big,
        ] + weight_specs(weights) + [whole(vec.shape)],
        out_specs=[big] + [whole(w.shape) for w in weights] + [whole((8, d))],
        out_shape=[shaped((rows, d), BF)] + [shaped(w.shape, BF) for w in weights] + [shaped((8, d), F32)],
        scratch_shapes=[pltpu.VMEM((d, d), F32)] * 4 + [pltpu.VMEM((t, d), BF)] * 4,
        compiler_params=params(),
        cost_estimate=pl.CostEstimate(flops=20 * rows * d * d, bytes_accessed=24 * rows * d, transcendentals=0),
        name="back",
    )(tokens, mg, q, k, v, p, mixed, *four(weights), vec)
    return out[0], out[1 : 1 + count], out[1 + count]


MESH = pl.DeviceIdType.MESH


class Place:
    def __init__(self, shards):
        self.shards = shards
        self.depth = shards // 4
        self.me = lax.axis_index("shard")
        self.core = lax.axis_index("rep")
        self.zed = self.me // 4
        x, y = self.me % 2, (self.me // 2) % 2
        self.near_step, self.far_step = 1 + self.core, 2 - self.core
        self.near = x + self.core * (y - x)
        self.far = y + self.core * (x - y)
        self.sibling = (self.me, 1 - self.core)
        self.near_peer = (self.block(self.zed, 1 - self.near, self.far), self.core)
        self.far_peer = (self.block(self.zed, self.near, 1 - self.far), self.core)
        self.columns = [lax.rem(self.zed + k, self.depth) for k in range(self.depth)]
        self.column_peers = [(self.block(z, self.near, self.far), self.core) for z in self.columns]

    def block(self, zed, near, far):
        return zed * 4 + near * self.near_step + far * self.far_step

    def greet(self):
        barrier = pltpu.get_barrier_semaphore()
        peers = [self.sibling, self.near_peer, self.far_peer] + self.column_peers[1:]
        for peer in peers:
            pl.semaphore_signal(barrier, inc=1, device_id=peer, device_id_type=MESH)
        pl.semaphore_wait(barrier, len(peers))


def half_of(ref, core):
    width = ref.shape[-1] // 2
    return pl.ds(pl.multiple_of(core * width, width), width)


class Gather:
    def __init__(self, place, full, send, recv, other):
        self.p, self.full, self.send, self.recv, self.other = place, full, send, recv, other
        self.cols = half_of(full, place.core)
        self.count = 0

    def copy(self, block, slot, peer, recv, cols):
        view = self.full.at[block, :, cols]
        return pltpu.make_async_remote_copy(
            src_ref=view, dst_ref=view, send_sem=self.send.at[slot], recv_sem=recv.at[block],
            device_id=peer, device_id_type=MESH,
        )

    def push(self, block, *peers):
        for peer in peers:
            recv = self.other if peer is self.p.sibling else self.recv
            self.copy(block, self.count, peer, recv, self.cols).start()
            self.count += 1

    def arrived(self, block, recv, cols):
        self.copy(block, 0, self.p.sibling, recv, cols).wait_recv()

    def own(self):
        p = self.p
        self.push(p.me, *p.column_peers[1:], p.near_peer, p.far_peer)

    def column(self, k):
        p = self.p
        block = p.block(p.columns[k + 1], p.near, p.far)
        self.arrived(block, self.recv, self.cols)
        self.push(block, p.near_peer, p.far_peer, p.sibling)

    def plane(self, k):
        p = self.p
        block = p.block(p.columns[k], 1 - p.near, p.far)
        self.arrived(block, self.recv, self.cols)
        self.push(block, p.far_peer, p.sibling)

    def rest(self, k):
        p = self.p
        for near in (p.near, 1 - p.near):
            block = p.block(p.columns[k], near, 1 - p.far)
            self.arrived(block, self.recv, self.cols)
            self.push(block, p.sibling)

    def joined(self):
        p = self.p
        cols = half_of(self.full, 1 - p.core)
        for k in range(1, p.shards):
            self.arrived(lax.rem(p.me + k, p.shards), self.other, cols)

    def drained(self):
        p = self.p
        for slot in range(self.count):
            self.copy(p.me, slot, p.sibling, self.other, self.cols).wait_send()

    def sends(shards):
        return 3 * (shards // 4) + (shards // 4 - 1) + shards // 4 + shards - 1


def ticker(plan, step):
    def tick(point):
        for (when, where), events in plan.items():
            if where == point:
                @pl.when(step == when)
                def _():
                    for event in events:
                        event()

    return tick


class Scatter:
    def kinds(shards, rows, cols, dtype):
        depth, half = shards // 4, cols // 2
        many = lambda *lead: pltpu.VMEM(lead + (rows, half), dtype)
        return [
            many(shards), many(shards), many(depth, 2), many(depth, 2), many(depth), many(depth),
            many(depth - 1), many(depth - 1), pltpu.VMEM((rows, half), F32), pltpu.VMEM((rows, half), F32),
            pltpu.SemaphoreType.DMA((depth,)), pltpu.SemaphoreType.DMA((4 * depth,)), pltpu.SemaphoreType.DMA((4 * depth,)),
        ]

    def __init__(self, place, full, out, scratch):
        self.p, self.full, self.out = place, full, out
        (self.mine, self.got_one, self.send_two, self.got_two, self.send_three, self.got_three,
         self.send_four, self.got_four, self.total, self.joined, self.local, self.send, self.recv) = scratch

    def copy(self, src, dst, slot, peer):
        return pltpu.make_async_remote_copy(
            src_ref=src, dst_ref=dst, send_sem=self.send.at[slot], recv_sem=self.recv.at[slot],
            device_id=peer, device_id_type=MESH,
        )

    def push(self, src, dst, slot, peer):
        self.copy(src, dst, slot, peer).start()

    def order(self):
        return self.p.columns[1:] + self.p.columns[:1]

    def first(self):
        p = self.p
        for z in self.order():
            rows = pl.ds(4 * z, 4)
            self.push(self.full.at[rows, :, half_of(self.full, 1 - p.core)], self.got_one.at[rows], z, p.sibling)
        for z in self.order():
            self.load(z).start()

    def load(self, z):
        rows = pl.ds(4 * z, 4)
        return pltpu.make_async_copy(
            self.full.at[rows, :, half_of(self.full, self.p.core)], self.mine.at[rows], self.local.at[z]
        )

    def pair(self, block):
        return self.mine[block].astype(F32) + self.got_one[block].astype(F32)

    def second(self, *turns):
        p, d = self.p, self.p.depth
        for i in turns or range(d):
            z = self.order()[i]
            rows = pl.ds(4 * z, 4)
            self.load(z).wait()
            self.copy(self.got_one.at[rows], self.got_one.at[rows], z, p.sibling).wait_recv()
            for near in range(2):
                block = p.block(z, near, 1 - p.far)
                self.send_two[z, near] = self.pair(block).astype(self.mine.dtype)
            self.push(self.send_two.at[z], self.got_two.at[z], d + z, p.far_peer)

    def third(self, *turns):
        p, d = self.p, self.p.depth
        for i in turns or range(d):
            z = self.order()[i]
            self.copy(self.send_two.at[z], self.got_two.at[z], d + z, p.far_peer).wait_recv()
            block = p.block(z, 1 - p.near, p.far)
            value = self.pair(block) + self.got_two[z, 1 - p.near].astype(F32)
            self.send_three[z] = value.astype(self.mine.dtype)
            self.push(self.send_three.at[z], self.got_three.at[z], 2 * d + z, p.near_peer)

    def triple(self, z):
        p, d = self.p, self.p.depth
        self.copy(self.send_three.at[z], self.got_three.at[z], 2 * d + z, p.near_peer).wait_recv()
        block = p.block(z, p.near, p.far)
        return self.pair(block) + self.got_two[z, p.near].astype(F32) + self.got_three[z].astype(F32)

    def fourth(self, *turns):
        p, d = self.p, self.p.depth
        for i in turns or range(d - 1):
            self.send_four[i] = self.triple(p.columns[i + 1]).astype(self.mine.dtype)
            self.push(self.send_four.at[i], self.got_four.at[i], 3 * d + i, p.column_peers[i + 1])

    def fifth(self):
        p, d = self.p, self.p.depth
        value = self.triple(p.zed)
        for i in range(d - 1):
            self.copy(self.send_four.at[i], self.got_four.at[i], 3 * d + i, p.column_peers[i + 1]).wait_recv()
            value = value + self.got_four[i].astype(F32)
        self.total[...] = value
        self.push(self.total, self.joined, 4 * d - 1, p.sibling)
        self.out[:, half_of(self.out, p.core)] = value

    def finish(self):
        p, d = self.p, self.p.depth
        self.copy(self.total, self.joined, 4 * d - 1, p.sibling).wait_recv()
        self.out[:, half_of(self.out, 1 - p.core)] = self.joined[...]
        for z in range(d):
            rows = self.got_one.at[pl.ds(4 * z, 4)]
            self.copy(rows, rows, z, p.sibling).wait_send()
            self.copy(self.send_two.at[z], self.got_two.at[z], d + z, p.far_peer).wait_send()
            self.copy(self.send_three.at[z], self.got_three.at[z], 2 * d + z, p.near_peer).wait_send()
            if z < d - 1:
                self.copy(self.send_four.at[z], self.got_four.at[z], 3 * d + z, p.sibling).wait_send()
        self.copy(self.total, self.joined, 4 * d - 1, p.sibling).wait_send()


class Largest:
    def __init__(self, place, own, out, got, kept, send, recv):
        self.p, self.own, self.out, self.got, self.kept, self.send, self.recv = place, own, out, got, kept, send, recv
        self.sent = []
        d = place.depth
        self.stages = [
            [(place.sibling, 0)], [(place.far_peer, 1)], [(place.near_peer, 2)],
            [(place.column_peers[k], 2 + k) for k in range(1, d)],
        ]

    def push(self, stage):
        if stage == 0:
            self.kept[0] = self.own[...]
        for peer, slot in self.stages[stage]:
            copy = pltpu.make_async_remote_copy(
                src_ref=self.kept.at[stage], dst_ref=self.got.at[slot], send_sem=self.send.at[slot],
                recv_sem=self.recv.at[slot], device_id=peer, device_id_type=MESH,
            )
            copy.start()
            self.sent.append((copy, stage))

    def take(self, stage):
        value = self.kept[stage]
        for (copy, s), (_, slot) in zip([c for c in self.sent if c[1] == stage], self.stages[stage]):
            copy.wait_recv()
            value = jnp.maximum(value, self.got[slot])
        if stage == 3:
            self.out[...] = value
            for copy, _ in self.sent:
                copy.wait_send()
        else:
            self.kept[stage + 1] = value


def scatter_kernel(shards, *refs):
    (attn, small, top, attn_out, small_out, top_out), scratch = refs[:6], refs[6:]
    p = Place(shards)
    s = Scatter(p, small, small_out, scratch[:13])
    a = Scatter(p, attn, attn_out, scratch[13:26])
    t = Largest(p, top, top_out, *scratch[26:])
    p.greet()
    t.push(0), s.first(), a.first()
    s.second(), t.take(0), t.push(1), a.second(), s.third(), t.take(1), t.push(2), a.third()
    s.fourth(), t.take(2), t.push(3), a.fourth(), s.fifth(), t.take(3), a.fifth()
    s.finish(), a.finish()


def scatter_last(shards, attn, small, top):
    depth = shards // 4
    scratch = Scatter.kinds(shards, small.shape[1], small.shape[2], F32)
    scratch += Scatter.kinds(shards, attn.shape[1], attn.shape[2], BF)
    scratch += [
        pltpu.VMEM((depth + 2, 8, 128), F32), pltpu.VMEM((4, 8, 128), F32),
        pltpu.SemaphoreType.DMA((depth + 2,)), pltpu.SemaphoreType.DMA((depth + 2,)),
    ]
    anywhere, inside = pl.BlockSpec(memory_space=pl.ANY), pl.BlockSpec(memory_space=pltpu.VMEM)
    return pl.pallas_call(
        lambda *refs: scatter_kernel(shards, *refs),
        in_specs=[anywhere] * 2 + [inside],
        out_specs=[inside] * 3,
        out_shape=[shaped(x.shape[1:], F32) for x in (attn, small)] + [shaped((8, 128), F32)],
        scratch_shapes=scratch,
        compiler_params=pltpu.CompilerParams(collective_id=2, has_side_effects=True, vmem_limit_bytes=VMEM_LIMIT),
        name="scatter",
    )(attn, small, top)


def enter_kernel(shards, width, steps, *refs):
    tok_ref, wq, wk, wv, wo, w1, w2, small = refs[:8]
    attn_out, w1_out, w2_out, small_out, vec_out = refs[8:13]
    results = refs[13:20]
    attn, tiles_in, local, send, recv, other = refs[20:]
    step = pl.program_id(0)
    p = Place(shards)
    rows = wq.shape[0]
    s, a, b, c = (
        Gather(p, full, send.at[i], recv.at[i], other.at[i])
        for i, full in enumerate((tiles_in, attn, w1_out, w2_out))
    )
    depth = p.depth

    def start():
        attn[p.me] = jnp.concatenate([w[...] for w in (wq, wk, wv, wo)], axis=0)
        tiles_in[p.me] = small[...]
        copies = [pltpu.make_async_copy(w, out.at[p.me], local.at[i]) for i, (w, out) in enumerate(((w1, w1_out), (w2, w2_out)))]
        for copy in copies:
            copy.start()
        p.greet()
        s.own(), a.own()
        for copy in copies:
            copy.wait()
        b.own()
        for g in (s, a):
            for k in range(depth - 1):
                g.column(k)
        c.own()
        for g in (s, a):
            for k in range(depth):
                g.plane(k)
        for k in range(depth):
            s.rest(k)
        for k in range(depth):
            a.rest(k)
            if k < depth - 1:
                b.column(k)
        s.joined(), a.joined()
        keep().start()
        vec = jnp.zeros(vec_out.shape, F32)
        blank = jnp.zeros((8, vec.shape[1] - 128), F32)
        for i in range(shards):
            piece = jnp.concatenate([tiles_in[i, :, :128], blank], axis=1)
            vec = vec + (pltpu.roll(piece, i * rows, 1) if i else piece)
        vec_out[...] = vec
        small_out[...] = tiles_in[...]

    def keep():
        return pltpu.make_async_copy(attn, attn_out, local.at[2])

    def end():
        b.joined(), c.joined()
        for g in (s, a, b, c):
            g.drained()
        keep().wait()

    pl.when(step == 0)(start)
    queue = (
        [[(c.column, k), (b.plane, k)] for k in range(depth - 1)] + [[(b.plane, depth - 1)]]
        + [[(b.rest, k), (c.plane, k)] for k in range(depth)] + [[(c.rest, k)] for k in range(depth)]
    )
    points = [(when, where) for when in range(steps) for where in (1, 2, 3)]
    plan = {}
    for i, events in enumerate(queue):
        point = points[min(i, len(points) - 1)]
        plan.setdefault(point, []).extend(functools.partial(event, k) for event, k in events)
    plan.setdefault(points[-1], []).append(end)
    view = [attn.at[:, i * rows : (i + 1) * rows, :] for i in range(4)]
    attend_kernel(width, tok_ref, view, vec_out, *results, tick=ticker(plan, step))


def enter(shards, tokens, wq, wk, wv, wo, w1, w2, small, heads):
    rows, d = tokens.shape
    t = min(ROWS, rows)
    pairs = d // PAIR
    blocks = rows // BLOCK
    big = tiles(t, d)
    sends = Gather.sends(shards)
    anywhere = pl.BlockSpec(memory_space=pl.ANY)
    packed = (shards, 4 * wq.shape[0], d)
    full_small = (shards,) + small.shape
    return pl.pallas_call(
        lambda *refs: enter_kernel(shards, d // heads, rows // t, *refs),
        grid=(rows // t,),
        in_specs=[big] + [whole(w.shape) for w in (wq, wk, wv, wo, w1, w2, small)],
        out_specs=[
            anywhere, anywhere, anywhere, whole(full_small), whole((8, d)), big, big, big,
            pl.BlockSpec((t // BLOCK, pairs, FRAMES, 2 * BLOCK), lambda i: (i, 0, 0, 0)),
            big, big,
            whole((pairs, FRAMES, 2 * BLOCK)),
        ],
        out_shape=[
            shaped(packed, BF), shaped((shards,) + w1.shape, BF), shaped((shards,) + w2.shape, BF),
            shaped(full_small, F32), shaped((8, d), F32),
        ]
        + [shaped((rows, d), BF)] * 3
        + [shaped((blocks, pairs, FRAMES, 2 * BLOCK), F32), shaped((rows, d), BF), shaped((rows, d), F32)]
        + [shaped((pairs, FRAMES, 2 * BLOCK), F32)],
        scratch_shapes=[
            pltpu.VMEM(packed, BF), pltpu.VMEM(full_small, F32), pltpu.SemaphoreType.DMA((3,)), pltpu.SemaphoreType.DMA((4, sends)),
            pltpu.SemaphoreType.DMA((4, shards)), pltpu.SemaphoreType.DMA((4, shards)),
        ],
        compiler_params=pltpu.CompilerParams(
            dimension_semantics=("arbitrary",), collective_id=0, has_side_effects=True, vmem_limit_bytes=VMEM_LIMIT
        ),
        name="enter",
    )(tokens, wq, wk, wv, wo, w1, w2, small)


BACK_ROWS = 256


def leave_kernel(shards, width, steps, *refs):
    ins, w_refs, vec_ref, w1g, w2g = refs[:7], refs[7:11], refs[11], refs[12], refs[13]
    gt_ref, wg_ref, vg_ref, w1_out, w2_out = refs[14:19]
    scratch, own = refs[19:27], refs[27:]
    step = pl.program_id(0)
    p = Place(shards)
    b = Scatter(p, w1g, w1_out, own[:13])
    c = Scatter(p, w2g, w2_out, own[13:26])
    depth = p.depth
    many = lambda event, *turns: functools.partial(event, *turns)
    events = [(0, p.greet), (0, c.first), (0, b.first)]
    for i in range(depth):
        events += [(1 + i, many(c.second, i)), (5 + i, many(b.second, i)), (9 + i, many(c.third, i)), (16 + i, many(b.third, i))]
    for i in range(depth - 1):
        events += [(17 + i, many(c.fourth, i)), (24 + i, many(b.fourth, i))]
    events += [(23, c.fifth)]
    points = [(when, where) for when in range(steps) for where in range(4)]
    plan = {}
    for at, event in events:
        plan.setdefault(points[at * len(points) // 32], []).append(event)
    plan[(steps - 1, 4)] = [c.finish, b.fifth, b.finish]
    back_kernel(width, *ins, w_refs, vec_ref, gt_ref, (wg_ref,), vg_ref, *scratch, tick=ticker(plan, step))


def leave(shards, tokens, mg, q, k, v, p, mixed, attn, vec, w1g, w2g, heads):
    rows, d = tokens.shape
    t = min(BACK_ROWS, rows)
    pairs = d // PAIR
    big = tiles(t, d)
    anywhere = pl.BlockSpec(memory_space=pl.ANY)
    return pl.pallas_call(
        lambda *refs: leave_kernel(shards, d // heads, rows // t, *refs),
        grid=(rows // t,),
        in_specs=[
            big, big, big, big, big,
            pl.BlockSpec((t // BLOCK, pairs, FRAMES, 2 * BLOCK), lambda i: (i, 0, 0, 0)),
            big,
        ] + weight_specs((attn,)) + [whole(vec.shape), anywhere, anywhere],
        out_specs=[big, whole(attn.shape), whole((8, d)), whole(w1g.shape[1:]), whole(w2g.shape[1:])],
        out_shape=[
            shaped((rows, d), BF), shaped(attn.shape, BF), shaped((8, d), F32),
            shaped(w1g.shape[1:], F32), shaped(w2g.shape[1:], F32),
        ],
        scratch_shapes=[pltpu.VMEM((d, d), F32)] * 4 + [pltpu.VMEM((t, d), BF)] * 4
        + Scatter.kinds(shards, w1g.shape[1], w1g.shape[2], BF) + Scatter.kinds(shards, w2g.shape[1], w2g.shape[2], BF),
        compiler_params=pltpu.CompilerParams(
            dimension_semantics=("arbitrary",), collective_id=1, has_side_effects=True, vmem_limit_bytes=VMEM_LIMIT
        ),
        name="leave",
    )(tokens, mg, q, k, v, p, mixed, *four((attn,)), vec, w1g, w2g)


def on_device(shards, reps, *args):
    (
        tokens, grad_out, first_gain, first_shift, query_proj, query_bias, key_proj, value_proj, value_bias,
        output_proj, output_bias, second_gain, second_shift, hidden_proj, hidden_bias, final_proj, final_bias, threshold,
    ) = args
    heads = threshold.shape[0]
    d = tokens.shape[1]
    hidden = hidden_proj.shape[1]
    head_dim = d // heads
    small = (first_gain, first_shift, query_bias, value_bias, output_bias, second_gain, second_shift, final_bias)
    rows, more = small[0].shape[0], hidden_bias.shape[0] // 8
    own = reps == 2 and shards % 4 == 0 and shards > 4 and rows % 16 == 0 and rows <= 128 and more <= 128

    def gather(x):
        return lax.all_gather(x, "shard", axis=0, tiled=True)

    def scatter(x):
        y = lax.psum_scatter(x.astype(BF), "shard", scatter_dimension=0, tiled=True)
        return lax.psum(y, "rep").astype(F32)

    if own:
        tile = jnp.concatenate(
            [
                jnp.pad(jnp.stack(small).astype(F32), ((0, 0), (0, 128 - rows))),
                jnp.pad(hidden_bias.astype(F32).reshape(8, more), ((0, 0), (0, 128 - more))),
            ],
            axis=1,
        )
        attn, w1, w2, tile, vec, q, k, v, p, mixed, middle, top = enter(
            shards, tokens, query_proj, key_proj, value_proj, output_proj, hidden_proj, final_proj, tile, heads
        )
        w1, w2 = w1.reshape(d, hidden), w2.reshape(hidden, d)
        hb = tile[:, :, 128 : 128 + more].reshape(1, hidden)
    else:
        weights = tuple(gather(x) for x in (query_proj, key_proj, value_proj, output_proj))
        w1, w2 = gather(hidden_proj), gather(final_proj)
        vec = jnp.stack([gather(x) for x in small]).astype(F32)
        hb = gather(hidden_bias).astype(F32)[None]
        q, k, v, p, mixed, middle, top = attend(tokens, weights, vec, heads)
    local = jnp.max(top.reshape(top.shape[0], FRAMES, 2, BLOCK), axis=(1, 3)).reshape(heads)
    layer_output, mg, w1g, w2g, vg2, hbg = mlp(middle, grad_out, w1, w2, vec, hb)
    if own:
        grad_tokens, wg, vg1, w1g, w2g = leave(
            shards, tokens, mg, q, k, v, p, mixed, attn, vec,
            w1g.reshape(shards, -1, hidden), w2g.reshape(shards, -1, d), heads,
        )
    else:
        grad_tokens, wg, vg1 = back(tokens, mg, q, k, v, p, mixed, weights, vec, heads)
    vg = jnp.concatenate([vg1[:5], vg2[:3]])
    if own:
        tile = jnp.concatenate(
            [
                jnp.pad(jnp.moveaxis(vg.reshape(8, shards, rows), 1, 0), ((0, 0), (0, 0), (0, 128 - rows))),
                jnp.pad(hbg.reshape(shards, 8, more), ((0, 0), (0, 0), (0, 128 - more))),
            ],
            axis=2,
        )
        attn, tile, top = scatter_last(
            shards, wg, tile, jnp.broadcast_to(jnp.pad(local, (0, 128 - heads))[None], (8, 128))
        )
        wg = tuple(attn[i * rows : (i + 1) * rows] for i in range(4))
        vg = tuple(tile[i, :rows] for i in range(8))
        hbg = tile[:, 128 : 128 + more].reshape(-1)
        global_max = top[0, :heads]
    else:
        global_max = lax.pmax(local, ("shard", "rep"))
        wg = tuple(scatter(x) for x in wg)
        w1g, w2g = scatter(w1g), scatter(w2g)
        vg = tuple(scatter(vg[i]) for i in range(8))
        hbg = scatter(hbg[0])
    factor = jnp.minimum(1.0, threshold / global_max)
    column_scale = jnp.repeat(jnp.sqrt(factor), head_dim)
    bias_scale = lax.dynamic_slice_in_dim(column_scale, lax.axis_index("shard") * rows, rows)
    return (
        layer_output, grad_tokens, vg[0], vg[1], wg[0], vg[2], wg[1], wg[2], vg[3], wg[3], vg[4], vg[5], vg[6],
        w1g, hbg, w2g, vg[7], global_max, factor,
        query_proj.astype(F32) * column_scale[None, :], query_bias.astype(F32) * bias_scale,
        key_proj.astype(F32) * column_scale[None, :],
    )


def solution(mesh):
    in_specs = (
        P(("shard", "rep"), None),
        P(("shard", "rep"), None),
        P("shard"),
        P("shard"),
        P("shard", None),
        P("shard"),
        P("shard", None),
        P("shard", None),
        P("shard"),
        P("shard", None),
        P("shard"),
        P("shard"),
        P("shard"),
        P("shard", None),
        P("shard"),
        P("shard", None),
        P("shard"),
        P(),
    )
    out_specs = (
        P(("shard", "rep"), None),
        P(("shard", "rep"), None),
        P("shard"),
        P("shard"),
        P("shard", None),
        P("shard"),
        P("shard", None),
        P("shard", None),
        P("shard"),
        P("shard", None),
        P("shard"),
        P("shard"),
        P("shard"),
        P("shard", None),
        P("shard"),
        P("shard", None),
        P("shard"),
        P(),
        P(),
        P("shard", None),
        P("shard"),
        P("shard", None),
    )
    shards, reps = mesh.shape["shard"], mesh.shape["rep"]
    return jax.shard_map(
        functools.partial(on_device, shards, reps), mesh=mesh, in_specs=in_specs, out_specs=out_specs, check_vma=False
    )
```

```python
import functools
import math

import jax
import jax.numpy as jnp
from jax import lax
from jax.experimental import pallas as pl
from jax.experimental.pallas import tpu as pltpu
from jax.sharding import PartitionSpec as P

FRAMES = 16
EPSILON = 1e-06
BF = jnp.bfloat16
F32 = jnp.float32
ROWS = 512
BLOCK = 128
PAIR = 128


def nn(left, right):
    return lax.dot_general(left, right, (((1,), (0,)), ((), ())), preferred_element_type=F32)


def nt(left, right):
    return lax.dot_general(left, right, (((1,), (1,)), ((), ())), preferred_element_type=F32)


def tn(left, right):
    return lax.dot_general(left, right, (((0,), (0,)), ((), ())), preferred_element_type=F32)


def normalise(values):
    centred = values - jnp.mean(values, axis=-1, keepdims=True)
    inverse = lax.rsqrt(jnp.mean(centred * centred, axis=-1, keepdims=True) + EPSILON)
    return centred * inverse, inverse


def norm_back(grad, unit, inverse, gain):
    scaled = grad * gain
    return inverse * (
        scaled
        - jnp.mean(scaled, axis=-1, keepdims=True)
        - unit * jnp.mean(scaled * unit, axis=-1, keepdims=True)
    )


def column_sum(values):
    return jnp.sum(values, axis=0, keepdims=True)


def place_masks():
    lane = lax.broadcasted_iota(jnp.int32, (FRAMES, 2 * BLOCK), 1)
    return [(lane % BLOCK) // FRAMES == p for p in range(BLOCK // FRAMES)]


def halves(width):
    lane = lax.broadcasted_iota(jnp.int32, (1, PAIR), 1)
    first = (lane < width).astype(F32)
    return first.astype(BF), (1.0 - first).astype(BF)


def compress(wide, masks):
    total = wide[:FRAMES]
    for p in range(1, len(masks)):
        total = jnp.where(masks[p], wide[p * FRAMES : (p + 1) * FRAMES], total)
    return total


def expand(packed, masks):
    zero = jnp.zeros_like(packed)
    return jnp.concatenate([jnp.where(m, packed, zero).astype(BF) for m in masks], axis=0)


def split(two, first, second):
    return jnp.concatenate([two * first, two * second], axis=0)


def stack(wide):
    return jnp.concatenate([wide[:, :BLOCK], wide[:, BLOCK:]], axis=0)


def square(ref):
    value = ref[...]
    return value.reshape(-1, value.shape[-1])


def attend_kernel(
    width, tok_ref, w_refs, vec_ref,
    q_ref, k_ref, v_ref, p_ref, mix_ref, mid_ref, top_ref, one_ref=None, tick=lambda point: None,
):
    scale = 1.0 / math.sqrt(width)
    wq, wk, wv = (square(w) for w in w_refs[:3])
    gain, shift = vec_ref[0:1], vec_ref[1:2]
    tok = tok_ref[...].astype(F32)
    unit, _ = normalise(tok)
    one = (unit * gain + shift).astype(BF)
    if one_ref is not None:
        one_ref[...] = one
    q_ref[...] = (nn(one, wq) + vec_ref[2:3]).astype(BF)
    k_ref[...] = nn(one, wk).astype(BF)
    v_ref[...] = (nn(one, wv) + vec_ref[3:4]).astype(BF)
    tick(1)
    masks = place_masks()
    first, second = halves(width)
    pairs = tok_ref.shape[1] // PAIR

    @pl.when(pl.program_id(0) == 0)
    def _():
        top_ref[...] = jnp.full(top_ref.shape, -3e38, F32)

    def body(i, carry):
        rows = pl.ds(pl.multiple_of(i * BLOCK, BLOCK), BLOCK)
        for h in range(pairs):
            cols = slice(h * PAIR, (h + 1) * PAIR)
            two_q, two_k, two_v = q_ref[rows, cols], k_ref[rows, cols], v_ref[rows, cols]
            scores = compress(nt(two_k, split(two_q, first, second)), masks) * scale
            top_ref[h] = jnp.maximum(top_ref[h], scores)
            expo = jnp.exp(scores - jnp.max(scores, axis=0, keepdims=True))
            probs = expo / jnp.sum(expo, axis=0, keepdims=True)
            p_ref[i, h] = probs
            mixed = tn(stack(expand(probs, masks)), split(two_v, first, second))
            mix_ref[rows, cols] = mixed.astype(BF)
        return carry

    lax.fori_loop(0, tok_ref.shape[0] // BLOCK, body, 0)
    tick(2)
    mid_ref[...] = tok_ref[...].astype(F32) + (nn(mix_ref[...], square(w_refs[3])) + vec_ref[4:5])
    tick(3)


def mlp_kernel(
    chunk, mid_ref, dy_ref, w1_ref, w2_ref, vec_ref, hb_ref,
    out_ref, mg_ref, w1g_ref, w2g_ref, vg_ref, hbg_ref,
    acc1, acc2, res_ref, two_ref,
):
    step, last = pl.program_id(0), pl.num_programs(0) - 1
    gain, shift = vec_ref[5:6], vec_ref[6:7]
    mid = mid_ref[...]
    unit, inverse = normalise(mid)
    inp = (unit * gain + shift).astype(BF)
    dy = dy_ref[...]
    hidden = w1_ref.shape[1]

    @pl.when(step == 0)
    def _():
        acc1[...] = jnp.zeros_like(acc1)
        acc2[...] = jnp.zeros_like(acc2)
        vg_ref[...] = jnp.zeros_like(vg_ref)
        hbg_ref[...] = jnp.zeros_like(hbg_ref)

    res_ref[...] = mid + vec_ref[7:8]
    two_ref[...] = jnp.zeros_like(two_ref)
    root = math.sqrt(2.0 / math.pi)

    def body(j, carry):
        cols = pl.ds(pl.multiple_of(j * chunk, chunk), chunk)
        z = nn(inp, w1_ref[:, cols]) + hb_ref[:, cols]
        act_grad = nt(dy, w2_ref[cols, :])
        square = z * z
        bend = jnp.tanh(root * z * (1.0 + 0.044715 * square))
        half = 0.5 * (1.0 + bend)
        act = (z * half).astype(BF)
        slope = half + 0.5 * z * (1.0 - bend * bend) * (root * (1.0 + 0.134145 * square))
        grad = (act_grad * slope).astype(BF)
        res_ref[...] += nn(act, w2_ref[cols, :])
        two_ref[...] += nt(grad, w1_ref[:, cols])
        acc2[cols, :] += tn(act, dy)
        acc1[:, cols] += tn(inp, grad)
        hbg_ref[:, cols] += column_sum(grad.astype(F32))
        return carry

    lax.fori_loop(0, hidden // chunk, body, 0)
    out_ref[...] = res_ref[...].astype(BF)
    two = two_ref[...]
    up = dy.astype(F32)
    mg_ref[...] = up + norm_back(two, unit, inverse, gain)
    vg_ref[0:1] += column_sum(two * unit)
    vg_ref[1:2] += column_sum(two)
    vg_ref[2:3] += column_sum(up)

    @pl.when(step == last)
    def _():
        w1g_ref[...] = acc1[...].astype(BF)
        w2g_ref[...] = acc2[...].astype(BF)


def attention_back(width, mgl_ref, q_ref, k_ref, v_ref, p_ref, dq_ref, dk_ref, dv_ref):
    scale = 1.0 / math.sqrt(width)
    masks = place_masks()
    first, second = halves(width)
    pairs = q_ref.shape[1] // PAIR

    def body(i, carry):
        rows = pl.ds(pl.multiple_of(i * BLOCK, BLOCK), BLOCK)
        for h in range(pairs):
            cols = slice(h * PAIR, (h + 1) * PAIR)
            two_q, two_k, two_v = q_ref[rows, cols], k_ref[rows, cols], v_ref[rows, cols]
            mixed = split(mgl_ref[rows, cols], first, second)
            probs = p_ref[i, h]
            slope = compress(nt(two_v, mixed), masks)
            score = probs * (slope - jnp.sum(slope * probs, axis=0, keepdims=True))
            wide = expand(score, masks)
            dv_ref[rows, cols] = nn(expand(probs, masks), mixed).astype(BF)
            dk_ref[rows, cols] = (nn(wide, split(two_q, first, second)) * scale).astype(BF)
            dq_ref[rows, cols] = (tn(stack(wide), split(two_k, first, second)) * scale).astype(BF)
        return carry

    lax.fori_loop(0, q_ref.shape[0] // BLOCK, body, 0)


def back_kernel(
    width, tok_ref, mg_ref, q_ref, k_ref, v_ref, p_ref, mix_ref,
    w_refs, vec_ref,
    gt_ref, wg_refs, vg_ref,
    accq, acck, accv, acco, mgl_ref, dq_ref, dk_ref, dv_ref,
):
    step, last = pl.program_id(0), pl.num_programs(0) - 1
    gain, shift = vec_ref[0:1], vec_ref[1:2]
    accs = (accq, acck, accv, acco)
    wq, wk, wv, wo = (square(w) for w in w_refs)

    @pl.when(step == 0)
    def _():
        for acc in accs:
            acc[...] = jnp.zeros_like(acc)
        vg_ref[...] = jnp.zeros_like(vg_ref)

    branch = mg_ref[...].astype(BF)
    mgl_ref[...] = nt(branch, wo).astype(BF)
    acco[...] += tn(mix_ref[...], branch)
    vg_ref[4:5] += column_sum(branch.astype(F32))
    attention_back(width, mgl_ref, q_ref, k_ref, v_ref, p_ref, dq_ref, dk_ref, dv_ref)
    unit, inverse = normalise(tok_ref[...].astype(F32))
    one = (unit * gain + shift).astype(BF)
    dq, dk, dv = dq_ref[...], dk_ref[...], dv_ref[...]
    vg_ref[2:3] += column_sum(dq.astype(F32))
    vg_ref[3:4] += column_sum(dv.astype(F32))
    accq[...] += tn(one, dq)
    acck[...] += tn(one, dk)
    accv[...] += tn(one, dv)
    grad = nt(dq, wq) + nt(dk, wk) + nt(dv, wv)
    vg_ref[0:1] += column_sum(grad * unit)
    vg_ref[1:2] += column_sum(grad)
    gt_ref[...] = (mg_ref[...] + norm_back(grad, unit, inverse, gain)).astype(BF)

    @pl.when(step == last)
    def _():
        for i, acc in enumerate(accs):
            value = acc[...].astype(BF)
            if len(wg_refs) == 1:
                rows = wg_refs[0].shape[1] // 4
                wg_refs[0][:, i * rows : (i + 1) * rows, :] = value.reshape(-1, rows, value.shape[1])
            else:
                wg_refs[i][...] = value


def whole(shape):
    return pl.BlockSpec(shape, lambda i: (0,) * len(shape), pipeline_mode=pl.Buffered(1))


def tiles(height, width):
    return pl.BlockSpec((height, width), lambda i: (i, 0))


def shaped(shape, dtype):
    return jax.ShapeDtypeStruct(shape, dtype)


VMEM_LIMIT = 60 * 1024 * 1024


def params():
    return pltpu.CompilerParams(
        dimension_semantics=("arbitrary",), vmem_limit_bytes=VMEM_LIMIT
    )


def weight_specs(weights):
    if len(weights) == 1:
        shards, rows, d = weights[0].shape
        return [
            pl.BlockSpec((shards, rows // 4, d), lambda i, j=j: (0, j, 0), pipeline_mode=pl.Buffered(1))
            for j in range(4)
        ]
    return [whole(w.shape) for w in weights]


def four(weights):
    return tuple(weights) * (4 // len(weights))


def attend(tokens, weights, vec, heads):
    rows, d = tokens.shape
    t = min(ROWS, rows)
    pairs = d // PAIR
    blocks = rows // BLOCK
    big = tiles(t, d)
    return pl.pallas_call(
        lambda tok, wq, wk, wv, wo, *refs: attend_kernel(d // heads, tok, (wq, wk, wv, wo), *refs),
        grid=(rows // t,),
        in_specs=[big] + weight_specs(weights) + [whole(vec.shape)],
        out_specs=[
            big, big, big,
            pl.BlockSpec((t // BLOCK, pairs, FRAMES, 2 * BLOCK), lambda i: (i, 0, 0, 0)),
            big, big,
            whole((pairs, FRAMES, 2 * BLOCK)),
        ],
        out_shape=[shaped((rows, d), BF)] * 3
        + [shaped((blocks, pairs, FRAMES, 2 * BLOCK), F32), shaped((rows, d), BF), shaped((rows, d), F32)]
        + [shaped((pairs, FRAMES, 2 * BLOCK), F32)],
        compiler_params=params(),
        cost_estimate=pl.CostEstimate(flops=10 * rows * d * d, bytes_accessed=24 * rows * d, transcendentals=0),
        name="attend",
    )(tokens, *four(weights), vec)


def mlp(middle, dy, w1, w2, vec, hb):
    rows, d = middle.shape
    hidden = w1.shape[1]
    t = min(ROWS, rows)
    big = tiles(t, d)
    return pl.pallas_call(
        lambda *refs: mlp_kernel(768, *refs),
        grid=(rows // t,),
        in_specs=[big, big, whole(w1.shape), whole(w2.shape), whole(vec.shape), whole(hb.shape)],
        out_specs=[big, big, whole(w1.shape), whole(w2.shape), whole((8, d)), whole((1, hidden))],
        out_shape=[
            shaped((rows, d), BF), shaped((rows, d), F32), shaped(w1.shape, BF), shaped(w2.shape, BF),
            shaped((8, d), F32), shaped((1, hidden), F32),
        ],
        scratch_shapes=[
            pltpu.VMEM(w1.shape, F32), pltpu.VMEM(w2.shape, F32), pltpu.VMEM((t, d), F32), pltpu.VMEM((t, d), F32),
        ],
        compiler_params=params(),
        cost_estimate=pl.CostEstimate(flops=12 * rows * d * hidden, bytes_accessed=14 * rows * d, transcendentals=0),
        name="mlp",
    )(middle, dy, w1, w2, vec, hb)


def back(tokens, mg, q, k, v, p, mixed, weights, vec, heads):
    rows, d = tokens.shape
    t = min(ROWS, rows)
    pairs = d // PAIR
    big = tiles(t, d)
    count = len(weights)

    def kernel(*refs):
        ins, w_refs, vec_ref, gt_ref = refs[:7], refs[7:11], refs[11], refs[12]
        wg_refs, rest = refs[13 : 13 + count], refs[13 + count :]
        back_kernel(d // heads, *ins, w_refs, vec_ref, gt_ref, wg_refs, *rest)

    out = pl.pallas_call(
        kernel,
        grid=(rows // t,),
        in_specs=[
            big, big, big, big, big,
            pl.BlockSpec((t // BLOCK, pairs, FRAMES, 2 * BLOCK), lambda i: (i, 0, 0, 0)),
            big,
        ] + weight_specs(weights) + [whole(vec.shape)],
        out_specs=[big] + [whole(w.shape) for w in weights] + [whole((8, d))],
        out_shape=[shaped((rows, d), BF)] + [shaped(w.shape, BF) for w in weights] + [shaped((8, d), F32)],
        scratch_shapes=[pltpu.VMEM((d, d), F32)] * 4 + [pltpu.VMEM((t, d), BF)] * 4,
        compiler_params=params(),
        cost_estimate=pl.CostEstimate(flops=20 * rows * d * d, bytes_accessed=24 * rows * d, transcendentals=0),
        name="back",
    )(tokens, mg, q, k, v, p, mixed, *four(weights), vec)
    return out[0], out[1 : 1 + count], out[1 + count]


MESH = pl.DeviceIdType.MESH


class Place:
    def __init__(self, shards):
        self.shards = shards
        self.depth = shards // 4
        self.me = lax.axis_index("shard")
        self.core = lax.axis_index("rep")
        self.zed = self.me // 4
        x, y = self.me % 2, (self.me // 2) % 2
        self.near_step, self.far_step = 1 + self.core, 2 - self.core
        self.near = x + self.core * (y - x)
        self.far = y + self.core * (x - y)
        self.sibling = (self.me, 1 - self.core)
        self.near_peer = (self.block(self.zed, 1 - self.near, self.far), self.core)
        self.far_peer = (self.block(self.zed, self.near, 1 - self.far), self.core)
        self.columns = [lax.rem(self.zed + k, self.depth) for k in range(self.depth)]
        self.column_peers = [(self.block(z, self.near, self.far), self.core) for z in self.columns]

    def block(self, zed, near, far):
        return zed * 4 + near * self.near_step + far * self.far_step

    def greet(self):
        barrier = pltpu.get_barrier_semaphore()
        peers = [self.sibling, self.near_peer, self.far_peer] + self.column_peers[1:]
        for peer in peers:
            pl.semaphore_signal(barrier, inc=1, device_id=peer, device_id_type=MESH)
        pl.semaphore_wait(barrier, len(peers))


def half_of(ref, core):
    width = ref.shape[-1] // 2
    return pl.ds(pl.multiple_of(core * width, width), width)


class Gather:
    def kinds(depth, count):
        return [pltpu.SemaphoreType.DMA((count, depth + 6)), pltpu.SemaphoreType.DMA((count, depth + 6))]

    def __init__(self, place, full, sems, at, first=0, width=None):
        self.p, self.full = place, full
        self.send, self.recv = (sem.at[at] for sem in sems)
        half = (width or full.shape[-1]) // 2
        self.cols = pl.ds(pl.multiple_of(first + place.core * half, half), half)
        self.here = place.near * place.near_step + place.far * place.far_step
        self.there = (1 - place.near) * place.near_step + place.far * place.far_step
        self.beyond = [near * place.near_step + (1 - place.far) * place.far_step for near in (place.near, 1 - place.near)]

    def copy(self, slot):
        p, d = self.p, self.p.depth
        if slot < d - 1:
            view, peer = self.full.at[p.zed, self.here, :, self.cols], p.column_peers[slot + 1]
        elif slot < d + 1:
            view, peer = self.full.at[:, self.here, :, self.cols], (p.near_peer, p.far_peer)[slot - d + 1]
        elif slot == d + 1:
            view, peer = self.full.at[:, self.there, :, self.cols], p.far_peer
        else:
            at = (self.here, self.there, *self.beyond)[slot - d - 2]
            view, peer = self.full.at[:, at, :, self.cols], p.sibling
        return pltpu.make_async_remote_copy(
            src_ref=view, dst_ref=view, send_sem=self.send.at[slot], recv_sem=self.recv.at[slot],
            device_id=peer, device_id_type=MESH,
        )

    def own(self):
        for slot in range(self.p.depth - 1):
            self.copy(slot).start()

    def column(self):
        d = self.p.depth
        for slot in range(d - 1):
            self.copy(slot).wait_recv()
        for slot in (d - 1, d, d + 2):
            self.copy(slot).start()

    def plane(self):
        d = self.p.depth
        self.copy(d - 1).wait_recv()
        self.copy(d + 1).start()
        self.copy(d + 3).start()

    def rest(self):
        d = self.p.depth
        for slot in (d, d + 1):
            self.copy(slot).wait_recv()
            self.copy(slot + 4).start()

    def joined(self):
        for slot in range(self.p.depth + 2, self.p.depth + 6):
            self.copy(slot).wait_recv()

    def drained(self):
        for slot in range(self.p.depth + 6):
            self.copy(slot).wait_send()


def ticker(plan, step):
    def tick(point):
        for (when, where), events in plan.items():
            if where == point:
                @pl.when(step == when)
                def _():
                    for event in events:
                        event()

    return tick


class Largest:
    def __init__(self, place, own, out, got, kept, send, recv):
        self.p, self.own, self.out, self.got, self.kept, self.send, self.recv = place, own, out, got, kept, send, recv
        d = place.depth
        self.stages = [
            [(place.sibling, 0)], [(place.far_peer, 1)], [(place.near_peer, 2)],
            [(place.column_peers[k], 2 + k) for k in range(1, d)],
        ]

    def copies(self, stage):
        return [
            pltpu.make_async_remote_copy(
                src_ref=self.kept.at[stage], dst_ref=self.got.at[slot], send_sem=self.send.at[slot],
                recv_sem=self.recv.at[slot], device_id=peer, device_id_type=MESH,
            )
            for peer, slot in self.stages[stage]
        ]

    def push(self, stage):
        if stage == 0:
            self.kept[0] = self.own[...]
        for copy in self.copies(stage):
            copy.start()

    def take(self, stage):
        value = self.kept[stage]
        for copy, (_, slot) in zip(self.copies(stage), self.stages[stage]):
            copy.wait_recv()
            value = jnp.maximum(value, self.got[slot])
        if stage == 3:
            self.out[...] = value
            for done in range(4):
                for copy in self.copies(done):
                    copy.wait_send()
        else:
            self.kept[stage + 1] = value


class BlockSum:
    def kinds(full, dtype, sets=1):
        depth, _, rows, cols = full
        one = (rows, cols // 2)
        many = lambda *lead: pltpu.VMEM((sets,) + lead + one, dtype)
        return [
            many(depth, 4), many(2, depth), many(2, depth), many(depth), many(depth), many(depth - 1), many(depth - 1),
            pltpu.VMEM((sets,) + one, F32), pltpu.VMEM((sets,) + one, F32),
            pltpu.SemaphoreType.DMA((sets, 4 + depth)), pltpu.SemaphoreType.DMA((sets, 4 + depth)),
        ]

    def __init__(self, place, full, scratch, at=0):
        self.p, self.full = place, full
        (self.got_one, self.send_two, self.got_two, self.send_three, self.got_three, self.send_four, self.got_four,
         self.total, self.joined, self.send, self.recv) = (ref.at[at] for ref in scratch)
        self.dtype = scratch[0].dtype
        self.cols, self.others = half_of(full, place.core), half_of(full, 1 - place.core)

    def copy(self, slot):
        p = self.p
        if slot < 4:
            src, dst, peer = (
                (self.full.at[:, :, :, self.others], self.got_one, p.sibling),
                (self.send_two.at[0], self.got_two.at[0], p.far_peer),
                (self.send_two.at[1], self.got_two.at[1], p.far_peer),
                (self.send_three, self.got_three, p.near_peer),
            )[slot]
        elif slot < 3 + p.depth:
            src, dst, peer = self.send_four.at[slot - 4], self.got_four.at[slot - 4], p.column_peers[slot - 3]
        else:
            src, dst, peer = self.total, self.joined, p.sibling
        return pltpu.make_async_remote_copy(
            src_ref=src, dst_ref=dst, send_sem=self.send.at[slot], recv_sem=self.recv.at[slot],
            device_id=peer, device_id_type=MESH,
        )

    def pair(self, near, far):
        at = near * self.p.near_step + far * self.p.far_step
        return self.full[:, at, :, self.cols].astype(F32) + self.got_one[:, at].astype(F32)

    def first(self):
        self.copy(0).start()

    def second(self):
        p = self.p
        self.copy(0).wait_recv()
        for slot, near in ((1, 1 - p.near), (0, p.near)):
            at = near * p.near_step + (1 - p.far) * p.far_step
            self.send_two[slot] = self.full[:, at, :, self.cols] + self.got_one[:, at]
            self.copy(1 + slot).start()

    def third(self):
        p = self.p
        self.copy(2).wait_recv()
        self.send_three[...] = (self.pair(1 - p.near, p.far) + self.got_two[1].astype(F32)).astype(self.dtype)
        self.copy(3).start()

    def fourth(self):
        p = self.p
        self.copy(1).wait_recv()
        self.copy(3).wait_recv()
        self.copy(0).wait_send()
        at = p.near * p.near_step + p.far * p.far_step

        def value(z):
            return (
                self.full[z, at, :, self.cols].astype(F32) + self.got_one[z, at].astype(F32)
                + self.got_two[0, z].astype(F32) + self.got_three[z].astype(F32)
            )

        for i in range(p.depth - 1):
            self.send_four[i] = value(p.columns[i + 1]).astype(self.dtype)
            self.copy(4 + i).start()
        self.total[...] = value(p.zed)

    def fifth(self):
        p = self.p
        value = self.total[...]
        for i in range(p.depth - 1):
            self.copy(4 + i).wait_recv()
            value = value + self.got_four[i].astype(F32)
        self.total[...] = value
        self.copy(3 + p.depth).start()

    def finish(self, write):
        self.copy(3 + self.p.depth).wait_recv()
        write(self.p.core, self.total[...])
        write(1 - self.p.core, self.joined[...])
        for slot in range(1, 4 + self.p.depth):
            self.copy(slot).wait_send()


def writer(ref, rows, first, width):
    def write(core, value):
        ref[rows, pl.ds(pl.multiple_of(first + core * width, width), width)] = value

    return write


def middle_kernel(shards, tall, *refs):
    mid_hbm, dy_ref, own_ref, b0_hbm, w2_ref, vec_ref, hb_ref = refs[:7]
    out_hbm, mg_hbm, bl_hbm, w2g_ref, w1g_ref, vg_ref, hbg_ref = refs[7:14]
    inp_ref, act_ref, grad_ref, res_ref, two_ref, stage, w1_ref, fullb, local = refs[14:23]
    sems, sums = refs[23:25], refs[25:]
    j, p = pl.program_id(0), Place(shards)
    depth = p.depth
    chunk = w2_ref.shape[1] * 4
    rows_all = dy_ref.shape[0]
    turns = rows_all // tall
    gain, shift = vec_ref[5:6], vec_ref[6:7]
    root = math.sqrt(2.0 / math.pi)
    weights = [
        Gather(p, w1_ref, sems, k - 1, k * chunk, chunk) for k in range(1, depth)
    ]
    def blocks(k):
        return BlockSum(p, fullb.at[lax.rem(k, 2)], sums, k)

    def rows_of(t):
        return pl.ds(pl.multiple_of(t * tall, tall), tall)

    def fetch(t):
        return pltpu.make_async_copy(mid_hbm.at[rows_of(t)], res_ref.at[rows_of(t)], local.at[t])

    def again(t):
        return pltpu.make_async_copy(mid_hbm.at[rows_of(t)], stage.at[t % 2], local.at[t])

    def results(t):
        return (
            pltpu.make_async_copy(act_ref.at[rows_of(t)], out_hbm.at[rows_of(t)], local.at[turns + t]),
            pltpu.make_async_copy(two_ref.at[rows_of(t)], mg_hbm.at[rows_of(t)], local.at[2 * turns + t]),
        )

    def first_chunk():
        return pltpu.make_async_copy(b0_hbm, w1_ref.at[:, :, :, pl.ds(0, chunk)], local.at[3 * turns])

    @pl.when(j == 0)
    def _():
        first_chunk().start()
        for t in range(turns):
            fetch(t).start()
        w1_ref[p.zed, lax.rem(p.me, 4), :, pl.ds(chunk, (depth - 1) * chunk)] = own_ref[:, pl.ds(chunk, (depth - 1) * chunk)]
        p.greet()
        for w in weights:
            w.own()
        for t in range(turns):
            fetch(t).wait()
        first_chunk().wait()

        def body(t, carry):
            rows = rows_of(t)
            unit, _ = normalise(res_ref[rows, :])
            inp_ref[rows, :] = (unit * gain + shift).astype(BF)
            two_ref[rows, :] = jnp.zeros((tall, two_ref.shape[1]), F32)
            return carry

        lax.fori_loop(0, turns, body, 0)

    cols = pl.ds(pl.multiple_of(j * chunk, chunk), chunk)

    def chunk_rows(t, carry):
        rows = rows_of(t)
        w1 = w1_ref[:, :, :, cols].reshape(-1, chunk)
        w2 = w2_ref[...].reshape(chunk, -1)
        z = nn(inp_ref[rows, :], w1) + hb_ref[...]
        act_grad = nt(dy_ref[rows, :], w2)
        square = z * z
        bend = jnp.tanh(root * z * (1.0 + 0.044715 * square))
        half = 0.5 * (1.0 + bend)
        act = (z * half).astype(BF)
        slope = half + 0.5 * z * (1.0 - bend * bend) * (root * (1.0 + 0.134145 * square))
        grad = (act_grad * slope).astype(BF)
        act_ref[rows, :] = act
        grad_ref[rows, :] = grad
        res_ref[rows, :] += nn(act, w2)
        two_ref[rows, :] += nt(grad, w1)
        hbg_ref[...] += column_sum(grad.astype(F32))

        first, later = weights[0], weights[1:]

        @pl.when(j == 0)
        def _():
            @pl.when(t == 0)
            def _():
                first.column()

            @pl.when(t == 1)
            def _():
                first.plane()
                for w in later:
                    w.column()

            pl.when(t == 2)(first.rest)

            @pl.when(t == 3)
            def _():
                for w in later:
                    w.plane()

        @pl.when((j == 1) & (t == 0))
        def _():
            for w in later:
                w.rest()

        @pl.when(j > 0)
        def _():
            pl.when(t == 0)(blocks(j - 1).second)
            pl.when(t == 2)(blocks(j - 1).third)

            @pl.when(j > 1)
            def _():
                pl.when(t == 1)(blocks(j - 2).fifth)

        return carry

    hbg_ref[...] = jnp.zeros_like(hbg_ref)
    lax.fori_loop(0, turns, chunk_rows, 0)
    for k, w in enumerate(weights):
        pl.when(j == k)(w.joined)

    w2g_ref[...] = tn(act_ref[...], dy_ref[...]).astype(BF).reshape(w2g_ref.shape)
    fullb[lax.rem(j, 2)] = tn(inp_ref[...], grad_ref[...]).astype(BF).reshape(fullb.shape[1:])

    @pl.when(j < depth - 1)
    def _():
        blocks(j).first()

    @pl.when(j > 0)
    def _():
        blocks(j - 1).fourth()

    @pl.when(j == depth - 1)
    def _():
        last = pltpu.make_async_copy(fullb.at[(depth - 1) % 2], bl_hbm, local.at[3 * turns])
        last.start()
        again(0).start()
        vg_ref[...] = jnp.zeros_like(vg_ref)
        for t in range(turns):
            rows = rows_of(t)
            if t + 1 < turns:
                again(t + 1).start()
            again(t).wait()
            unit, inverse = normalise(stage[t % 2])
            two, up = two_ref[rows, :], dy_ref[rows, :].astype(F32)
            vg_ref[0:1] += column_sum(two * unit)
            vg_ref[1:2] += column_sum(two)
            vg_ref[2:3] += column_sum(up)
            act_ref[rows, :] = (res_ref[rows, :] + vec_ref[7:8]).astype(BF)
            two_ref[rows, :] = up + norm_back(two, unit, inverse, gain)
            for copy in results(t):
                copy.start()
        blocks(depth - 2).fifth()
        for t in range(turns):
            for copy in results(t):
                copy.wait()
        last.wait()
        for w in weights:
            w.drained()
        for k in range(depth - 1):
            blocks(k).finish(writer(w1g_ref, slice(None), k * chunk, chunk // 2))


def middle(shards, mid, dy, w1_own, b0, w2, vec, hb):
    rows, d = mid.shape
    depth = shards // 4
    hidden = w1_own.shape[1]
    chunk = hidden // depth
    tall = min(ROWS, rows)
    turns = rows // tall
    less = depth - 1
    anywhere = pl.BlockSpec(memory_space=pl.ANY)
    fullb = (depth, 4, w1_own.shape[0], chunk)
    w1g = (w1_own.shape[0], less * chunk)
    return pl.pallas_call(
        lambda *refs: middle_kernel(shards, tall, *refs),
        grid=(depth,),
        in_specs=[
            anywhere, whole(dy.shape), whole(w1_own.shape), anywhere,
            pl.BlockSpec((4,) + w2.shape[1:], lambda j: (j, 0, 0)), whole(vec.shape), pl.BlockSpec((1, chunk), lambda j: (0, j)),
        ],
        out_specs=[
            anywhere, anywhere, anywhere, pl.BlockSpec((4,) + w2.shape[1:], lambda j: (j, 0, 0)), whole(w1g), whole((8, d)),
            pl.BlockSpec((1, chunk), lambda j: (0, j)),
        ],
        out_shape=[
            shaped((rows, d), BF), shaped((rows, d), F32), shaped(fullb, BF), shaped(w2.shape, BF), shaped(w1g, F32),
            shaped((8, d), F32), shaped((1, hidden), F32),
        ],
        scratch_shapes=[
            pltpu.VMEM((rows, d), BF), pltpu.VMEM((rows, chunk), BF), pltpu.VMEM((rows, chunk), BF),
            pltpu.VMEM((rows, d), F32), pltpu.VMEM((rows, d), F32), pltpu.VMEM((2, tall, d), F32),
            pltpu.VMEM((depth, 4) + w1_own.shape, BF), pltpu.VMEM((2,) + fullb, BF),
            pltpu.SemaphoreType.DMA((3 * turns + 1,)),
        ] + Gather.kinds(depth, less) + BlockSum.kinds(fullb, BF, less),
        compiler_params=pltpu.CompilerParams(
            dimension_semantics=("arbitrary",), collective_id=3, has_side_effects=True, vmem_limit_bytes=VMEM_LIMIT
        ),
        name="middle",
    )(mid, dy, w1_own, b0, w2, vec, hb)


def enter_kernel(shards, width, steps, *refs):
    tok_ref, wq, wk, wv, wo, w1, w2, small = refs[:8]
    attn_out, w1_out, w2_out, small_out, vec_out = refs[8:13]
    results = refs[13:21]
    attn, tiles_in, local = refs[21:24]
    sems = refs[24:26]
    step = pl.program_id(0)
    p = Place(shards)
    depth = p.depth
    rows = wq.shape[0]
    s, b, c, *early = (
        Gather(p, full, sems, i)
        for i, full in enumerate(
            [tiles_in, w1_out, w2_out] + [attn.at[:, :, i * rows : (i + 1) * rows] for i in range(4)]
        )
    )
    early.insert(0, s)

    def start():
        mine = p.zed, lax.rem(p.me, 4)
        copies = [
            pltpu.make_async_copy(w, out.at[mine], local.at[i])
            for i, (w, out) in enumerate(((w1, w1_out), (w2, w2_out)))
        ]
        for copy in copies:
            copy.start()
        attn[mine] = jnp.concatenate([w[...] for w in (wq, wk, wv, wo)], axis=0)
        tiles_in[mine] = small[...]
        for copy in copies:
            copy.wait()
        p.greet()
        for g in early + [b, c]:
            g.own()
        for g in early:
            g.column()
        for g in early:
            g.plane()
        b.column()
        for g in early:
            g.rest()
        b.plane()
        for g in early[:-1]:
            g.joined()
        vec = jnp.zeros(vec_out.shape, F32)
        blank = jnp.zeros((8, vec.shape[1] - 128), F32)
        for i in range(shards):
            piece = jnp.concatenate([tiles_in[i // 4, i % 4, :, :128], blank], axis=1)
            vec = vec + (pltpu.roll(piece, i * rows, 1) if i else piece)
        vec_out[...] = vec
        small_out[...] = tiles_in[...]

    def keep():
        return pltpu.make_async_copy(attn, attn_out, local.at[2])

    def whole_attn():
        early[-1].joined()
        keep().start()

    def end():
        b.joined(), c.joined()
        for g in early + [b, c]:
            g.drained()
        keep().wait()

    pl.when(step == 0)(start)
    plan = {(0, 1): [whole_attn, c.column], (0, 2): [b.rest], (steps // 2 - 1, 3): [c.plane], (steps - 1, 2): [c.rest], (steps - 1, 3): [end]}
    view = [attn.at[:, :, i * rows : (i + 1) * rows, :] for i in range(4)]
    attend_kernel(width, tok_ref, view, vec_out, *results, tick=ticker(plan, step))


def enter(shards, tokens, wq, wk, wv, wo, w1, w2, small, heads):
    rows, d = tokens.shape
    t = min(ROWS, rows)
    pairs = d // PAIR
    blocks = rows // BLOCK
    big = tiles(t, d)
    depth = shards // 4
    lead = (depth, 4)
    anywhere = pl.BlockSpec(memory_space=pl.ANY)
    packed = lead + (4 * wq.shape[0], d)
    full_small = lead + small.shape
    chunk = w1.shape[1] // depth
    return pl.pallas_call(
        lambda *refs: enter_kernel(shards, d // heads, rows // t, *refs),
        grid=(rows // t,),
        in_specs=[big] + [whole(w.shape) for w in (wq, wk, wv, wo)] + [whole((w1.shape[0], chunk))] + [whole(w.shape) for w in (w2, small)],
        out_specs=[
            anywhere, anywhere, anywhere, whole(full_small), whole((8, d)), big, big, big,
            pl.BlockSpec((t // BLOCK, pairs, FRAMES, 2 * BLOCK), lambda i: (i, 0, 0, 0)),
            big, big,
            whole((pairs, FRAMES, 2 * BLOCK)), big,
        ],
        out_shape=[
            shaped(packed, BF), shaped(lead + (w1.shape[0], chunk), BF), shaped(lead + w2.shape, BF),
            shaped(full_small, F32), shaped((8, d), F32),
        ]
        + [shaped((rows, d), BF)] * 3
        + [shaped((blocks, pairs, FRAMES, 2 * BLOCK), F32), shaped((rows, d), BF), shaped((rows, d), F32)]
        + [shaped((pairs, FRAMES, 2 * BLOCK), F32), shaped((rows, d), BF)],
        scratch_shapes=[
            pltpu.VMEM(packed, BF), pltpu.VMEM(full_small, F32), pltpu.SemaphoreType.DMA((3,)),
        ] + Gather.kinds(depth, 7),
        compiler_params=pltpu.CompilerParams(
            dimension_semantics=("arbitrary",), collective_id=0, has_side_effects=True, vmem_limit_bytes=VMEM_LIMIT
        ),
        name="enter",
    )(tokens, wq, wk, wv, wo, w1, w2, small)


def leave_kernel(shards, width, steps, *refs):
    mg_ref, q_ref, k_ref, v_ref, p_ref, mix_ref, wo_ref, fullb, fullc = refs[:9]
    dq_ref, dk_ref, dv_ref, wog_ref, vg_ref, w1_out, w2_out = refs[9:16]
    acco, mgl_ref = refs[16:18]
    own = refs[18:]
    step, p = pl.program_id(0), Place(shards)
    rows = fullc.shape[2] // 2
    b = BlockSum(p, fullb, own[:11])
    c = BlockSum(p, fullc.at[:, :, :rows], own[11:22])
    e = BlockSum(p, fullc.at[:, :, rows:], own[22:33])

    def finish():
        wide = w2_out.shape[1] // 2
        c.finish(writer(w2_out, slice(0, rows), 0, wide))
        e.finish(writer(w2_out, slice(rows, None), 0, wide))
        b.finish(writer(w1_out, slice(None), 0, w1_out.shape[1] // 2))

    events = [
        (0, p.greet), (0, c.first), (0, e.first), (0, b.first), (1, c.second), (2, e.second), (3, b.second),
        (5, c.third), (6, e.third), (7, b.third), (8, c.fourth), (9, e.fourth), (9, b.fourth), (11, c.fifth),
        (11, e.fifth), (11, b.fifth),
    ]
    points = [(when, where) for when in range(steps) for where in range(3)]
    plan = {}
    for at, event in events:
        plan.setdefault(points[at * len(points) // 12], []).append(event)
    tick = ticker(plan, step)

    @pl.when(step == 0)
    def _():
        acco[...] = jnp.zeros_like(acco)
        vg_ref[...] = jnp.zeros_like(vg_ref)

    tick(0)
    branch = mg_ref[...].astype(BF)
    mgl_ref[...] = nt(branch, square(wo_ref)).astype(BF)
    acco[...] += tn(mix_ref[...], branch)
    vg_ref[4:5] += column_sum(branch.astype(F32))
    tick(1)
    attention_back(width, mgl_ref, q_ref, k_ref, v_ref, p_ref, dq_ref, dk_ref, dv_ref)
    vg_ref[2:3] += column_sum(dq_ref[...].astype(F32))
    vg_ref[3:4] += column_sum(dv_ref[...].astype(F32))
    tick(2)

    @pl.when(step == steps - 1)
    def _():
        wog_ref[...] = acco[...].astype(BF).reshape(wog_ref.shape)
        finish()


def leave(shards, mg, q, k, v, p, mixed, attn, fullb, fullc, heads):
    rows, d = mg.shape
    t = min(ROWS, rows)
    pairs = d // PAIR
    big = tiles(t, d)
    half = fullc.shape[:2] + (fullc.shape[2] // 2, fullc.shape[3])
    w1_out, w2_out = fullb.shape[2:], fullc.shape[2:]
    wog = (shards // 4, 4, attn.shape[1] // 4, d)
    return pl.pallas_call(
        lambda *refs: leave_kernel(shards, d // heads, rows // t, *refs),
        grid=(rows // t,),
        in_specs=[
            big, big, big, big,
            pl.BlockSpec((t // BLOCK, pairs, FRAMES, 2 * BLOCK), lambda i: (i, 0, 0, 0)),
            big, weight_specs((attn,))[3], whole(fullb.shape), whole(fullc.shape),
        ],
        out_specs=[big, big, big, whole(wog), whole((8, d)), whole(w1_out), whole(w2_out)],
        out_shape=[shaped((rows, d), BF)] * 3
        + [shaped(wog, BF), shaped((8, d), F32), shaped(w1_out, F32), shaped(w2_out, F32)],
        scratch_shapes=[pltpu.VMEM((d, d), F32), pltpu.VMEM((t, d), BF)]
        + BlockSum.kinds(fullb.shape, BF) + BlockSum.kinds(half, BF) + BlockSum.kinds(half, BF),
        compiler_params=pltpu.CompilerParams(
            dimension_semantics=("arbitrary",), collective_id=1, has_side_effects=True, vmem_limit_bytes=VMEM_LIMIT
        ),
        name="leave",
    )(mg, q, k, v, p, mixed, attn, fullb, fullc)


def last_kernel(shards, steps, *refs):
    tok_ref, mg_ref, dq_hbm, dk_hbm, dv_hbm, one_hbm, wq, wk, wv, vec_ref, wog_ref, vgin_ref, hbt_ref, top_ref = refs[:14]
    gt_ref, attn_out, small_out, top_out = refs[14:18]
    d_ref, one_ref, full, tile, vg, local = refs[18:24]
    jobs, little, most = refs[24:35], refs[35:46], refs[46:]
    step, p = pl.program_id(0), Place(shards)
    rows = wog_ref.shape[2]
    wide = attn_out.shape[1] // 2
    o = BlockSum(p, wog_ref, jobs, 3)
    s = BlockSum(p, tile, little)
    t = Largest(p, top_ref, top_out, *most)
    weight = lambda i: BlockSum(p, full.at[i], jobs, i)
    fetches = [
        pltpu.make_async_copy(src, dst, local.at[i])
        for i, (src, dst) in enumerate(
            ((dq_hbm, d_ref.at[0]), (dk_hbm, d_ref.at[1]), (dv_hbm, d_ref.at[2]), (one_hbm, one_ref))
        )
    ]

    @pl.when(step == 0)
    def _():
        for i in (3, 0, 1, 2):
            fetches[i].start()
        vg[...] = vgin_ref[...]
        p.greet()
        o.first(), t.push(0)
        fetches[3].wait()

    for i in range(3):
        pl.when(step == i)(fetches[i].wait)

    @pl.when(step < 3)
    def _():
        full[step] = tn(one_ref[...], d_ref[step]).astype(BF).reshape(full.shape[1:])
        weight(step).first()

    @pl.when(step >= 3)
    def _():
        tall = tok_ref.shape[0]
        at = pl.ds(pl.multiple_of((step - 3) * tall, tall), tall)
        unit, inverse = normalise(tok_ref[...].astype(F32))
        grad = nt(d_ref[0, at], square(wq)) + nt(d_ref[1, at], square(wk)) + nt(d_ref[2, at], square(wv))
        vg[0:1] += column_sum(grad * unit)
        vg[1:2] += column_sum(grad)
        gt_ref[...] = (mg_ref[...] + norm_back(grad, unit, inverse, vec_ref[0:1])).astype(BF)

    def end():
        d = vg.shape[1]
        value = vg[...]
        for i in range(shards):
            piece = pltpu.roll(value, d - i * rows, 1) if i else value
            tile[i // 4, i % 4, :, :128] = piece[:, :128]
        tile[:, :, :, 128:] = hbt_ref[...]
        s.first()
        weight(2).fourth()
        s.second()
        o.fifth(), weight(0).fifth()
        s.third()
        weight(1).fifth()
        s.fourth()
        weight(2).fifth()
        s.fifth()
        for i, job in ((3, o), (0, weight(0)), (1, weight(1)), (2, weight(2))):
            job.finish(writer(attn_out, slice(i * rows, (i + 1) * rows), 0, wide))
        s.finish(writer(small_out, slice(None), 0, small_out.shape[1] // 2))

    q, k, v = weight(0), weight(1), weight(2)
    events = [
        (0, o.second), (1, q.second), (1, lambda: t.take(0)), (1, lambda: t.push(1)), (2, k.second), (2, o.third),
        (3, v.second), (3, q.third), (3, lambda: t.take(1)), (3, lambda: t.push(2)), (4, o.fourth), (4, k.third),
        (4, lambda: t.take(2)), (4, lambda: t.push(3)), (5, v.third), (5, q.fourth), (6, k.fourth), (6, lambda: t.take(3)),
    ]
    plan = {}
    for at, event in events:
        plan.setdefault((min(at, steps - 1), 0), []).append(event)
    plan.setdefault((steps - 1, 0), []).append(end)
    ticker(plan, step)(0)


def last(shards, tokens, mg, dq, dk, dv, one, attn, vec, wog, vgin, hbt, top):
    rows, d = tokens.shape
    t = min(ROWS, rows)
    depth = shards // 4
    steps = 3 + rows // t
    later = pl.BlockSpec((t, d), lambda i: (jnp.maximum(i - 3, 0), 0))
    anywhere = pl.BlockSpec(memory_space=pl.ANY)
    small = (depth, 4, 8, 256)
    return pl.pallas_call(
        lambda *refs: last_kernel(shards, steps, *refs),
        grid=(steps,),
        in_specs=[later, later] + [anywhere] * 4 + weight_specs((attn,))[:3]
        + [whole(x.shape) for x in (vec, wog, vgin, hbt, top)],
        out_specs=[later, whole((4 * wog.shape[2], d)), whole((8, 256)), whole((8, 128))],
        out_shape=[
            shaped((rows, d), BF), shaped((4 * wog.shape[2], d), F32), shaped((8, 256), F32), shaped((8, 128), F32),
        ],
        scratch_shapes=[
            pltpu.VMEM((3, rows, d), BF), pltpu.VMEM((rows, d), BF), pltpu.VMEM((3,) + wog.shape, BF),
            pltpu.VMEM(small, F32), pltpu.VMEM((8, d), F32), pltpu.SemaphoreType.DMA((4,)),
        ] + BlockSum.kinds(wog.shape, BF, 4) + BlockSum.kinds(small, F32) + [
            pltpu.VMEM((depth + 2, 8, 128), F32), pltpu.VMEM((4, 8, 128), F32),
            pltpu.SemaphoreType.DMA((depth + 2,)), pltpu.SemaphoreType.DMA((depth + 2,)),
        ],
        compiler_params=pltpu.CompilerParams(
            dimension_semantics=("arbitrary",), collective_id=2, has_side_effects=True, vmem_limit_bytes=VMEM_LIMIT
        ),
        name="last",
    )(tokens, mg, dq, dk, dv, one, attn, attn, attn, vec, wog, vgin, hbt, top)


def on_device(shards, reps, *args):
    (
        tokens, grad_out, first_gain, first_shift, query_proj, query_bias, key_proj, value_proj, value_bias,
        output_proj, output_bias, second_gain, second_shift, hidden_proj, hidden_bias, final_proj, final_bias, threshold,
    ) = args
    heads = threshold.shape[0]
    d = tokens.shape[1]
    hidden = hidden_proj.shape[1]
    head_dim = d // heads
    small = (first_gain, first_shift, query_bias, value_bias, output_bias, second_gain, second_shift, final_bias)
    rows, more = small[0].shape[0], hidden_bias.shape[0] // 8
    whole_chunks = shards % 4 == 0 and hidden * 4 % (shards * 256) == 0 and hidden * 4 // shards == 4 * final_proj.shape[0]
    own = whole_chunks and reps == 2 and shards % 4 == 0 and shards > 4 and rows % 16 == 0 and rows <= 128 and more <= 128

    def gather(x):
        return lax.all_gather(x, "shard", axis=0, tiled=True)

    def scatter(x):
        y = lax.psum_scatter(x.astype(BF), "shard", scatter_dimension=0, tiled=True)
        return lax.psum(y, "rep").astype(F32)

    if own:
        tile = jnp.concatenate(
            [
                jnp.pad(jnp.stack(small).astype(F32), ((0, 0), (0, 128 - rows))),
                jnp.pad(hidden_bias.astype(F32).reshape(8, more), ((0, 0), (0, 128 - more))),
            ],
            axis=1,
        )
        attn, w1, w2, tile, vec, q, k, v, p, mixed, mid, top, one = enter(
            shards, tokens, query_proj, key_proj, value_proj, output_proj, hidden_proj, final_proj, tile, heads
        )
        tile = tile.reshape(shards, 8, -1)
        hb = tile[:, :, 128 : 128 + more].reshape(1, hidden)
        attn, w2 = attn.reshape(shards, -1, d), w2.reshape(shards, -1, d)
    else:
        weights = tuple(gather(x) for x in (query_proj, key_proj, value_proj, output_proj))
        w1, w2 = gather(hidden_proj), gather(final_proj)
        vec = jnp.stack([gather(x) for x in small]).astype(F32)
        hb = gather(hidden_bias).astype(F32)[None]
        q, k, v, p, mixed, mid, top = attend(tokens, weights, vec, heads)
    local = jnp.max(top.reshape(top.shape[0], FRAMES, 2, BLOCK), axis=(1, 3)).reshape(heads)
    if own:
        layer_output, mg, b3g, w2g, w1g, vg2, hbg = middle(shards, mid, grad_out, hidden_proj, w1, w2, vec, hb)
        dq, dk, dv, wog, vg1, w1l, w2g = leave(
            shards, mg, q, k, v, p, mixed, attn, b3g, w2g.reshape(shards // 4, 4, -1, d), heads
        )
        hbt = jnp.pad(hbg.reshape(shards // 4, 4, 8, more), ((0, 0), (0, 0), (0, 0), (0, 128 - more)))
        grad_tokens, attn, tile, top = last(
            shards, tokens, mg, dq, dk, dv, one, attn, vec, wog, jnp.concatenate([vg1[:5], vg2[:3]]), hbt,
            jnp.broadcast_to(jnp.pad(local, (0, 128 - heads))[None], (8, 128)),
        )
        w1g = jnp.concatenate([w1g, w1l], axis=1)
    else:
        layer_output, mg, w1g, w2g, vg2, hbg = mlp(mid, grad_out, w1, w2, vec, hb)
        grad_tokens, wg, vg1 = back(tokens, mg, q, k, v, p, mixed, weights, vec, heads)
    if own:
        wg = tuple(attn[i * rows : (i + 1) * rows] for i in range(4))
        vg = tuple(tile[i, :rows] for i in range(8))
        hbg = tile[:, 128 : 128 + more].reshape(-1)
        global_max = top[0, :heads]
    else:
        vg = jnp.concatenate([vg1[:5], vg2[:3]])
        global_max = lax.pmax(local, ("shard", "rep"))
        wg = tuple(scatter(x) for x in wg)
        w1g, w2g = scatter(w1g), scatter(w2g)
        vg = tuple(scatter(vg[i]) for i in range(8))
        hbg = scatter(hbg[0])
    factor = jnp.minimum(1.0, threshold / global_max)
    column_scale = jnp.repeat(jnp.sqrt(factor), head_dim)
    bias_scale = lax.dynamic_slice_in_dim(column_scale, lax.axis_index("shard") * rows, rows)
    return (
        layer_output, grad_tokens, vg[0], vg[1], wg[0], vg[2], wg[1], wg[2], vg[3], wg[3], vg[4], vg[5], vg[6],
        w1g, hbg, w2g, vg[7], global_max, factor,
        query_proj.astype(F32) * column_scale[None, :], query_bias.astype(F32) * bias_scale,
        key_proj.astype(F32) * column_scale[None, :],
    )


def solution(mesh):
    in_specs = (
        P(("shard", "rep"), None),
        P(("shard", "rep"), None),
        P("shard"),
        P("shard"),
        P("shard", None),
        P("shard"),
        P("shard", None),
        P("shard", None),
        P("shard"),
        P("shard", None),
        P("shard"),
        P("shard"),
        P("shard"),
        P("shard", None),
        P("shard"),
        P("shard", None),
        P("shard"),
        P(),
    )
    out_specs = (
        P(("shard", "rep"), None),
        P(("shard", "rep"), None),
        P("shard"),
        P("shard"),
        P("shard", None),
        P("shard"),
        P("shard", None),
        P("shard", None),
        P("shard"),
        P("shard", None),
        P("shard"),
        P("shard"),
        P("shard"),
        P("shard", None),
        P("shard"),
        P("shard", None),
        P("shard"),
        P(),
        P(),
        P("shard", None),
        P("shard"),
        P("shard", None),
    )
    shards, reps = mesh.shape["shard"], mesh.shape["rep"]
    return jax.shard_map(
        functools.partial(on_device, shards, reps), mesh=mesh, in_specs=in_specs, out_specs=out_specs, check_vma=False
    )
```

```python
import functools
import math

import jax
import jax.numpy as jnp
from jax import lax
from jax.experimental import pallas as pl
from jax.experimental.pallas import tpu as pltpu
from jax.sharding import PartitionSpec as P

FRAMES = 16
EPSILON = 1e-06
BF = jnp.bfloat16
F32 = jnp.float32
ROWS = 512
BLOCK = 128
PAIR = 128


def nn(left, right):
    return lax.dot_general(left, right, (((1,), (0,)), ((), ())), preferred_element_type=F32)


def nt(left, right):
    return lax.dot_general(left, right, (((1,), (1,)), ((), ())), preferred_element_type=F32)


def tn(left, right):
    return lax.dot_general(left, right, (((0,), (0,)), ((), ())), preferred_element_type=F32)


def normalise(values):
    centred = values - jnp.mean(values, axis=-1, keepdims=True)
    inverse = lax.rsqrt(jnp.mean(centred * centred, axis=-1, keepdims=True) + EPSILON)
    return centred * inverse, inverse


def norm_back(grad, unit, inverse, gain):
    scaled = grad * gain
    return inverse * (
        scaled
        - jnp.mean(scaled, axis=-1, keepdims=True)
        - unit * jnp.mean(scaled * unit, axis=-1, keepdims=True)
    )


def column_sum(values):
    return jnp.sum(values, axis=0, keepdims=True)


def place_masks():
    lane = lax.broadcasted_iota(jnp.int32, (FRAMES, 2 * BLOCK), 1)
    return [(lane % BLOCK) // FRAMES == p for p in range(BLOCK // FRAMES)]


def halves(width):
    lane = lax.broadcasted_iota(jnp.int32, (1, PAIR), 1)
    first = (lane < width).astype(F32)
    return first.astype(BF), (1.0 - first).astype(BF)


def compress(wide, masks):
    total = wide[:FRAMES]
    for p in range(1, len(masks)):
        total = jnp.where(masks[p], wide[p * FRAMES : (p + 1) * FRAMES], total)
    return total


def expand(packed, masks):
    zero = jnp.zeros_like(packed)
    return jnp.concatenate([jnp.where(m, packed, zero).astype(BF) for m in masks], axis=0)


def split(two, first, second):
    return jnp.concatenate([two * first, two * second], axis=0)


def stack(wide):
    return jnp.concatenate([wide[:, :BLOCK], wide[:, BLOCK:]], axis=0)


def square(ref):
    value = ref[...]
    return value.reshape(-1, value.shape[-1])


def attend_kernel(
    width, tok_ref, w_refs, vec_ref,
    q_ref, k_ref, v_ref, p_ref, mix_ref, mid_ref, top_ref, one_ref=None, tick=lambda point: None,
):
    scale = 1.0 / math.sqrt(width)
    wq, wk, wv = (square(w) for w in w_refs[:3])
    gain, shift = vec_ref[0:1], vec_ref[1:2]
    tok = tok_ref[...].astype(F32)
    unit, _ = normalise(tok)
    one = (unit * gain + shift).astype(BF)
    if one_ref is not None:
        one_ref[...] = one
    q_ref[...] = (nn(one, wq) + vec_ref[2:3]).astype(BF)
    k_ref[...] = nn(one, wk).astype(BF)
    v_ref[...] = (nn(one, wv) + vec_ref[3:4]).astype(BF)
    tick(1)
    masks = place_masks()
    first, second = halves(width)
    pairs = tok_ref.shape[1] // PAIR

    @pl.when(pl.program_id(0) == 0)
    def _():
        top_ref[...] = jnp.full(top_ref.shape, -3e38, F32)

    def body(i, carry):
        rows = pl.ds(pl.multiple_of(i * BLOCK, BLOCK), BLOCK)
        for h in range(pairs):
            cols = slice(h * PAIR, (h + 1) * PAIR)
            two_q, two_k, two_v = q_ref[rows, cols], k_ref[rows, cols], v_ref[rows, cols]
            scores = compress(nt(two_k, split(two_q, first, second)), masks) * scale
            top_ref[h] = jnp.maximum(top_ref[h], scores)
            expo = jnp.exp(scores - jnp.max(scores, axis=0, keepdims=True))
            probs = expo / jnp.sum(expo, axis=0, keepdims=True)
            p_ref[i, h] = probs
            mixed = tn(stack(expand(probs, masks)), split(two_v, first, second))
            mix_ref[rows, cols] = mixed.astype(BF)
        return carry

    lax.fori_loop(0, tok_ref.shape[0] // BLOCK, body, 0)
    tick(2)
    mid_ref[...] = tok_ref[...].astype(F32) + (nn(mix_ref[...], square(w_refs[3])) + vec_ref[4:5])
    tick(3)


def mlp_kernel(
    chunk, mid_ref, dy_ref, w1_ref, w2_ref, vec_ref, hb_ref,
    out_ref, mg_ref, w1g_ref, w2g_ref, vg_ref, hbg_ref,
    acc1, acc2, res_ref, two_ref,
):
    step, last = pl.program_id(0), pl.num_programs(0) - 1
    gain, shift = vec_ref[5:6], vec_ref[6:7]
    mid = mid_ref[...]
    unit, inverse = normalise(mid)
    inp = (unit * gain + shift).astype(BF)
    dy = dy_ref[...]
    hidden = w1_ref.shape[1]

    @pl.when(step == 0)
    def _():
        acc1[...] = jnp.zeros_like(acc1)
        acc2[...] = jnp.zeros_like(acc2)
        vg_ref[...] = jnp.zeros_like(vg_ref)
        hbg_ref[...] = jnp.zeros_like(hbg_ref)

    res_ref[...] = mid + vec_ref[7:8]
    two_ref[...] = jnp.zeros_like(two_ref)
    root = math.sqrt(2.0 / math.pi)

    def body(j, carry):
        cols = pl.ds(pl.multiple_of(j * chunk, chunk), chunk)
        z = nn(inp, w1_ref[:, cols]) + hb_ref[:, cols]
        act_grad = nt(dy, w2_ref[cols, :])
        square = z * z
        bend = jnp.tanh(root * z * (1.0 + 0.044715 * square))
        half = 0.5 * (1.0 + bend)
        act = (z * half).astype(BF)
        slope = half + 0.5 * z * (1.0 - bend * bend) * (root * (1.0 + 0.134145 * square))
        grad = (act_grad * slope).astype(BF)
        res_ref[...] += nn(act, w2_ref[cols, :])
        two_ref[...] += nt(grad, w1_ref[:, cols])
        acc2[cols, :] += tn(act, dy)
        acc1[:, cols] += tn(inp, grad)
        hbg_ref[:, cols] += column_sum(grad.astype(F32))
        return carry

    lax.fori_loop(0, hidden // chunk, body, 0)
    out_ref[...] = res_ref[...].astype(BF)
    two = two_ref[...]
    up = dy.astype(F32)
    mg_ref[...] = up + norm_back(two, unit, inverse, gain)
    vg_ref[0:1] += column_sum(two * unit)
    vg_ref[1:2] += column_sum(two)
    vg_ref[2:3] += column_sum(up)

    @pl.when(step == last)
    def _():
        w1g_ref[...] = acc1[...].astype(BF)
        w2g_ref[...] = acc2[...].astype(BF)


def attention_back(width, mgl_ref, q_ref, k_ref, v_ref, p_ref, dq_ref, dk_ref, dv_ref):
    scale = 1.0 / math.sqrt(width)
    masks = place_masks()
    first, second = halves(width)
    pairs = q_ref.shape[1] // PAIR

    def body(i, carry):
        rows = pl.ds(pl.multiple_of(i * BLOCK, BLOCK), BLOCK)
        for h in range(pairs):
            cols = slice(h * PAIR, (h + 1) * PAIR)
            two_q, two_k, two_v = q_ref[rows, cols], k_ref[rows, cols], v_ref[rows, cols]
            mixed = split(mgl_ref[rows, cols], first, second)
            probs = p_ref[i, h]
            slope = compress(nt(two_v, mixed), masks)
            score = probs * (slope - jnp.sum(slope * probs, axis=0, keepdims=True))
            wide = expand(score, masks)
            dv_ref[rows, cols] = nn(expand(probs, masks), mixed).astype(BF)
            dk_ref[rows, cols] = (nn(wide, split(two_q, first, second)) * scale).astype(BF)
            dq_ref[rows, cols] = (tn(stack(wide), split(two_k, first, second)) * scale).astype(BF)
        return carry

    lax.fori_loop(0, q_ref.shape[0] // BLOCK, body, 0)


def back_kernel(
    width, tok_ref, mg_ref, q_ref, k_ref, v_ref, p_ref, mix_ref,
    w_refs, vec_ref,
    gt_ref, wg_refs, vg_ref,
    accq, acck, accv, acco, mgl_ref, dq_ref, dk_ref, dv_ref,
):
    step, last = pl.program_id(0), pl.num_programs(0) - 1
    gain, shift = vec_ref[0:1], vec_ref[1:2]
    accs = (accq, acck, accv, acco)
    wq, wk, wv, wo = (square(w) for w in w_refs)

    @pl.when(step == 0)
    def _():
        for acc in accs:
            acc[...] = jnp.zeros_like(acc)
        vg_ref[...] = jnp.zeros_like(vg_ref)

    branch = mg_ref[...].astype(BF)
    mgl_ref[...] = nt(branch, wo).astype(BF)
    acco[...] += tn(mix_ref[...], branch)
    vg_ref[4:5] += column_sum(branch.astype(F32))
    attention_back(width, mgl_ref, q_ref, k_ref, v_ref, p_ref, dq_ref, dk_ref, dv_ref)
    unit, inverse = normalise(tok_ref[...].astype(F32))
    one = (unit * gain + shift).astype(BF)
    dq, dk, dv = dq_ref[...], dk_ref[...], dv_ref[...]
    vg_ref[2:3] += column_sum(dq.astype(F32))
    vg_ref[3:4] += column_sum(dv.astype(F32))
    accq[...] += tn(one, dq)
    acck[...] += tn(one, dk)
    accv[...] += tn(one, dv)
    grad = nt(dq, wq) + nt(dk, wk) + nt(dv, wv)
    vg_ref[0:1] += column_sum(grad * unit)
    vg_ref[1:2] += column_sum(grad)
    gt_ref[...] = (mg_ref[...] + norm_back(grad, unit, inverse, gain)).astype(BF)

    @pl.when(step == last)
    def _():
        for i, acc in enumerate(accs):
            value = acc[...].astype(BF)
            if len(wg_refs) == 1:
                rows = wg_refs[0].shape[1] // 4
                wg_refs[0][:, i * rows : (i + 1) * rows, :] = value.reshape(-1, rows, value.shape[1])
            else:
                wg_refs[i][...] = value


def whole(shape):
    return pl.BlockSpec(shape, lambda i: (0,) * len(shape), pipeline_mode=pl.Buffered(1))


def tiles(height, width):
    return pl.BlockSpec((height, width), lambda i: (i, 0))


def shaped(shape, dtype):
    return jax.ShapeDtypeStruct(shape, dtype)


VMEM_LIMIT = 60 * 1024 * 1024


def params():
    return pltpu.CompilerParams(
        dimension_semantics=("arbitrary",), vmem_limit_bytes=VMEM_LIMIT
    )


def weight_specs(weights):
    if len(weights) == 1:
        shards, rows, d = weights[0].shape
        return [
            pl.BlockSpec((shards, rows // 4, d), lambda i, j=j: (0, j, 0), pipeline_mode=pl.Buffered(1))
            for j in range(4)
        ]
    return [whole(w.shape) for w in weights]


def four(weights):
    return tuple(weights) * (4 // len(weights))


def attend(tokens, weights, vec, heads):
    rows, d = tokens.shape
    t = min(ROWS, rows)
    pairs = d // PAIR
    blocks = rows // BLOCK
    big = tiles(t, d)
    return pl.pallas_call(
        lambda tok, wq, wk, wv, wo, *refs: attend_kernel(d // heads, tok, (wq, wk, wv, wo), *refs),
        grid=(rows // t,),
        in_specs=[big] + weight_specs(weights) + [whole(vec.shape)],
        out_specs=[
            big, big, big,
            pl.BlockSpec((t // BLOCK, pairs, FRAMES, 2 * BLOCK), lambda i: (i, 0, 0, 0)),
            big, big,
            whole((pairs, FRAMES, 2 * BLOCK)),
        ],
        out_shape=[shaped((rows, d), BF)] * 3
        + [shaped((blocks, pairs, FRAMES, 2 * BLOCK), F32), shaped((rows, d), BF), shaped((rows, d), F32)]
        + [shaped((pairs, FRAMES, 2 * BLOCK), F32)],
        compiler_params=params(),
        cost_estimate=pl.CostEstimate(flops=10 * rows * d * d, bytes_accessed=24 * rows * d, transcendentals=0),
        name="attend",
    )(tokens, *four(weights), vec)


def mlp(middle, dy, w1, w2, vec, hb):
    rows, d = middle.shape
    hidden = w1.shape[1]
    t = min(ROWS, rows)
    big = tiles(t, d)
    return pl.pallas_call(
        lambda *refs: mlp_kernel(768, *refs),
        grid=(rows // t,),
        in_specs=[big, big, whole(w1.shape), whole(w2.shape), whole(vec.shape), whole(hb.shape)],
        out_specs=[big, big, whole(w1.shape), whole(w2.shape), whole((8, d)), whole((1, hidden))],
        out_shape=[
            shaped((rows, d), BF), shaped((rows, d), F32), shaped(w1.shape, BF), shaped(w2.shape, BF),
            shaped((8, d), F32), shaped((1, hidden), F32),
        ],
        scratch_shapes=[
            pltpu.VMEM(w1.shape, F32), pltpu.VMEM(w2.shape, F32), pltpu.VMEM((t, d), F32), pltpu.VMEM((t, d), F32),
        ],
        compiler_params=params(),
        cost_estimate=pl.CostEstimate(flops=12 * rows * d * hidden, bytes_accessed=14 * rows * d, transcendentals=0),
        name="mlp",
    )(middle, dy, w1, w2, vec, hb)


def back(tokens, mg, q, k, v, p, mixed, weights, vec, heads):
    rows, d = tokens.shape
    t = min(ROWS, rows)
    pairs = d // PAIR
    big = tiles(t, d)
    count = len(weights)

    def kernel(*refs):
        ins, w_refs, vec_ref, gt_ref = refs[:7], refs[7:11], refs[11], refs[12]
        wg_refs, rest = refs[13 : 13 + count], refs[13 + count :]
        back_kernel(d // heads, *ins, w_refs, vec_ref, gt_ref, wg_refs, *rest)

    out = pl.pallas_call(
        kernel,
        grid=(rows // t,),
        in_specs=[
            big, big, big, big, big,
            pl.BlockSpec((t // BLOCK, pairs, FRAMES, 2 * BLOCK), lambda i: (i, 0, 0, 0)),
            big,
        ] + weight_specs(weights) + [whole(vec.shape)],
        out_specs=[big] + [whole(w.shape) for w in weights] + [whole((8, d))],
        out_shape=[shaped((rows, d), BF)] + [shaped(w.shape, BF) for w in weights] + [shaped((8, d), F32)],
        scratch_shapes=[pltpu.VMEM((d, d), F32)] * 4 + [pltpu.VMEM((t, d), BF)] * 4,
        compiler_params=params(),
        cost_estimate=pl.CostEstimate(flops=20 * rows * d * d, bytes_accessed=24 * rows * d, transcendentals=0),
        name="back",
    )(tokens, mg, q, k, v, p, mixed, *four(weights), vec)
    return out[0], out[1 : 1 + count], out[1 + count]


MESH = pl.DeviceIdType.MESH


class Place:
    def __init__(self, shards):
        self.shards = shards
        self.depth = shards // 4
        self.me = lax.axis_index("shard")
        self.core = lax.axis_index("rep")
        self.zed = self.me // 4
        x, y = self.me % 2, (self.me // 2) % 2
        self.near_step, self.far_step = 1 + self.core, 2 - self.core
        self.near = x + self.core * (y - x)
        self.far = y + self.core * (x - y)
        self.sibling = (self.me, 1 - self.core)
        self.near_peer = (self.block(self.zed, 1 - self.near, self.far), self.core)
        self.far_peer = (self.block(self.zed, self.near, 1 - self.far), self.core)
        self.columns = [lax.rem(self.zed + k, self.depth) for k in range(self.depth)]
        self.column_peers = [(self.block(z, self.near, self.far), self.core) for z in self.columns]

    def block(self, zed, near, far):
        return zed * 4 + near * self.near_step + far * self.far_step

    def greet(self):
        barrier = pltpu.get_barrier_semaphore()
        peers = [self.sibling, self.near_peer, self.far_peer] + self.column_peers[1:]
        for peer in peers:
            pl.semaphore_signal(barrier, inc=1, device_id=peer, device_id_type=MESH)
        pl.semaphore_wait(barrier, len(peers))


def half_of(ref, core):
    width = ref.shape[-1] // 2
    return pl.ds(pl.multiple_of(core * width, width), width)


class Gather:
    def kinds(depth, count):
        return [pltpu.SemaphoreType.DMA((count, depth + 6)), pltpu.SemaphoreType.DMA((count, depth + 6))]

    def __init__(self, place, full, sems, at, first=0, width=None):
        self.p, self.full = place, full
        self.send, self.recv = (sem.at[at] for sem in sems)
        half = (width or full.shape[-1]) // 2
        self.cols = pl.ds(pl.multiple_of(first + place.core * half, half), half)
        self.here = place.near * place.near_step + place.far * place.far_step
        self.there = (1 - place.near) * place.near_step + place.far * place.far_step
        self.beyond = [near * place.near_step + (1 - place.far) * place.far_step for near in (place.near, 1 - place.near)]

    def copy(self, slot):
        p, d = self.p, self.p.depth
        if slot < d - 1:
            view, peer = self.full.at[p.zed, self.here, :, self.cols], p.column_peers[slot + 1]
        elif slot < d + 1:
            view, peer = self.full.at[:, self.here, :, self.cols], (p.near_peer, p.far_peer)[slot - d + 1]
        elif slot == d + 1:
            view, peer = self.full.at[:, self.there, :, self.cols], p.far_peer
        else:
            at = (self.here, self.there, *self.beyond)[slot - d - 2]
            view, peer = self.full.at[:, at, :, self.cols], p.sibling
        return pltpu.make_async_remote_copy(
            src_ref=view, dst_ref=view, send_sem=self.send.at[slot], recv_sem=self.recv.at[slot],
            device_id=peer, device_id_type=MESH,
        )

    def own(self):
        for slot in range(self.p.depth - 1):
            self.copy(slot).start()

    def column(self):
        d = self.p.depth
        for slot in range(d - 1):
            self.copy(slot).wait_recv()
        for slot in (d - 1, d, d + 2):
            self.copy(slot).start()

    def plane(self):
        d = self.p.depth
        self.copy(d - 1).wait_recv()
        self.copy(d + 1).start()
        self.copy(d + 3).start()

    def rest(self):
        d = self.p.depth
        for slot in (d, d + 1):
            self.copy(slot).wait_recv()
            self.copy(slot + 4).start()

    def joined(self):
        for slot in range(self.p.depth + 2, self.p.depth + 6):
            self.copy(slot).wait_recv()

    def drained(self):
        for slot in range(self.p.depth + 6):
            self.copy(slot).wait_send()


def ticker(plan, step):
    def tick(point):
        for (when, where), events in plan.items():
            if where == point:
                @pl.when(step == when)
                def _():
                    for event in events:
                        event()

    return tick


class Direct:
    def kinds(shards):
        return [
            pltpu.VMEM((shards, 8, 128), F32), pltpu.VMEM((2 * shards, 8, 128), F32),
            pltpu.SemaphoreType.DMA((2 * shards,)), pltpu.SemaphoreType.DMA((2 * shards,)),
        ]

    def __init__(self, place, scratch):
        self.tiles, self.got, self.send, self.recv = scratch
        self.count = 2 * place.shards
        self.at = 2 * place.me + place.core
        self.me = place.me

    def greet(self):
        barrier = pltpu.get_barrier_semaphore()
        for k in range(1, self.count):
            other = lax.rem(self.at + k, self.count)
            pl.semaphore_signal(barrier, inc=1, device_id=(other // 2, lax.rem(other, 2)), device_id_type=MESH)
        pl.semaphore_wait(barrier, self.count - 1)

    def copy(self, k, slot):
        other = lax.rem(self.at + k, self.count)
        return pltpu.make_async_remote_copy(
            src_ref=self.tiles.at[other // 2], dst_ref=self.got.at[slot], send_sem=self.send.at[k],
            recv_sem=self.recv.at[slot], device_id=(other // 2, lax.rem(other, 2)), device_id_type=MESH,
        )

    def push(self):
        for k in range(1, self.count):
            self.copy(k, self.at).start()

    def sum(self):
        self.got[self.at] = self.tiles[self.me]
        for k in range(1, self.count):
            self.copy(k, lax.rem(self.at + k, self.count)).wait_recv()
        value = self.got[0]
        for i in range(1, self.count):
            value = value + self.got[i]
        for k in range(1, self.count):
            self.copy(k, self.at).wait_send()
        return value


class Largest:
    def __init__(self, place, own, out, got, kept, send, recv):
        self.p, self.own, self.out, self.got, self.kept, self.send, self.recv = place, own, out, got, kept, send, recv
        d = place.depth
        self.stages = [
            [(place.sibling, 0)], [(place.far_peer, 1)], [(place.near_peer, 2)],
            [(place.column_peers[k], 2 + k) for k in range(1, d)],
        ]

    def copies(self, stage):
        return [
            pltpu.make_async_remote_copy(
                src_ref=self.kept.at[stage], dst_ref=self.got.at[slot], send_sem=self.send.at[slot],
                recv_sem=self.recv.at[slot], device_id=peer, device_id_type=MESH,
            )
            for peer, slot in self.stages[stage]
        ]

    def push(self, stage):
        if stage == 0:
            self.kept[0] = self.own[...]
        for copy in self.copies(stage):
            copy.start()

    def take(self, stage):
        value = self.kept[stage]
        for copy, (_, slot) in zip(self.copies(stage), self.stages[stage]):
            copy.wait_recv()
            value = jnp.maximum(value, self.got[slot])
        if stage == 3:
            self.out[...] = value
            for done in range(4):
                for copy in self.copies(done):
                    copy.wait_send()
        else:
            self.kept[stage + 1] = value


class BlockSum:
    def kinds(full, dtype, sets=1):
        depth, _, rows, cols = full
        one = (rows, cols // 2)
        many = lambda *lead: pltpu.VMEM((sets,) + lead + one, dtype)
        return [
            many(depth, 4), many(2, depth), many(2, depth), many(depth), many(depth), many(depth - 1), many(depth - 1),
            pltpu.VMEM((sets,) + one, F32), pltpu.VMEM((sets,) + one, F32),
            pltpu.SemaphoreType.DMA((sets, 4 + depth)), pltpu.SemaphoreType.DMA((sets, 4 + depth)),
        ]

    def __init__(self, place, full, scratch, at=0):
        self.p, self.full = place, full
        (self.got_one, self.send_two, self.got_two, self.send_three, self.got_three, self.send_four, self.got_four,
         self.total, self.joined, self.send, self.recv) = (ref.at[at] for ref in scratch)
        self.dtype = scratch[0].dtype
        self.cols, self.others = half_of(full, place.core), half_of(full, 1 - place.core)

    def copy(self, slot):
        p = self.p
        if slot < 4:
            src, dst, peer = (
                (self.full.at[:, :, :, self.others], self.got_one, p.sibling),
                (self.send_two.at[0], self.got_two.at[0], p.far_peer),
                (self.send_two.at[1], self.got_two.at[1], p.far_peer),
                (self.send_three, self.got_three, p.near_peer),
            )[slot]
        elif slot < 3 + p.depth:
            src, dst, peer = self.send_four.at[slot - 4], self.got_four.at[slot - 4], p.column_peers[slot - 3]
        else:
            src, dst, peer = self.total, self.joined, p.sibling
        return pltpu.make_async_remote_copy(
            src_ref=src, dst_ref=dst, send_sem=self.send.at[slot], recv_sem=self.recv.at[slot],
            device_id=peer, device_id_type=MESH,
        )

    def pair(self, near, far):
        at = near * self.p.near_step + far * self.p.far_step
        return self.full[:, at, :, self.cols].astype(F32) + self.got_one[:, at].astype(F32)

    def first(self):
        self.copy(0).start()

    def second(self):
        p = self.p
        self.copy(0).wait_recv()
        for slot, near in ((1, 1 - p.near), (0, p.near)):
            at = near * p.near_step + (1 - p.far) * p.far_step
            self.send_two[slot] = self.full[:, at, :, self.cols] + self.got_one[:, at]
            self.copy(1 + slot).start()

    def third(self):
        p = self.p
        self.copy(2).wait_recv()
        self.send_three[...] = (self.pair(1 - p.near, p.far) + self.got_two[1].astype(F32)).astype(self.dtype)
        self.copy(3).start()

    def fourth(self):
        p = self.p
        self.copy(1).wait_recv()
        self.copy(3).wait_recv()
        self.copy(0).wait_send()
        at = p.near * p.near_step + p.far * p.far_step

        def value(z):
            return (
                self.full[z, at, :, self.cols].astype(F32) + self.got_one[z, at].astype(F32)
                + self.got_two[0, z].astype(F32) + self.got_three[z].astype(F32)
            )

        for i in range(p.depth - 1):
            self.send_four[i] = value(p.columns[i + 1]).astype(self.dtype)
            self.copy(4 + i).start()
        self.total[...] = value(p.zed)

    def fifth(self):
        p = self.p
        value = self.total[...]
        for i in range(p.depth - 1):
            self.copy(4 + i).wait_recv()
            value = value + self.got_four[i].astype(F32)
        self.total[...] = value
        self.copy(3 + p.depth).start()

    def finish(self, write):
        self.copy(3 + self.p.depth).wait_recv()
        write(self.p.core, self.total[...])
        write(1 - self.p.core, self.joined[...])
        for slot in range(1, 4 + self.p.depth):
            self.copy(slot).wait_send()


class OwnerSum(BlockSum):
    def kinds(full, dtype, depth, sets=1):
        _, _, rows, cols = full
        one = (rows, cols // 2)
        many = lambda *lead: pltpu.VMEM((sets,) + lead + one, dtype)
        return [
            many(1, 4), many(2, 1), many(2, 1), many(1), many(1), many(), pltpu.VMEM((depth - 1,) + one, dtype),
            pltpu.VMEM(one, F32), pltpu.VMEM(one, F32),
            pltpu.SemaphoreType.DMA((sets, 4 + depth)), pltpu.SemaphoreType.DMA((sets, 4 + depth)),
        ]

    def __init__(self, place, full, scratch, at, target):
        self.p, self.full = place, full
        self.got_one, self.send_two, self.got_two, self.send_three, self.got_three, self.send_four = (
            ref.at[at] for ref in scratch[:6]
        )
        self.got_four, self.total, self.joined = scratch[6:9]
        self.send, self.recv = (ref.at[at] for ref in scratch[9:])
        self.dtype = scratch[0].dtype
        self.cols, self.others = half_of(full, place.core), half_of(full, 1 - place.core)
        self.away = lax.rem(target - place.zed + place.depth, place.depth)
        self.target = target

    def line(self, away):
        p = self.p
        return pltpu.make_async_remote_copy(
            src_ref=self.send_four, dst_ref=self.got_four.at[away - 1], send_sem=self.send.at[3 + away],
            recv_sem=self.recv.at[3 + away], device_id=(p.block(self.target, p.near, p.far), p.core), device_id_type=MESH,
        )

    def fourth(self):
        p = self.p
        self.copy(1).wait_recv()
        self.copy(3).wait_recv()
        self.copy(0).wait_send()
        value = self.pair(p.near, p.far)[0] + self.got_two[0, 0].astype(F32) + self.got_three[0].astype(F32)

        @pl.when(self.away == 0)
        def _():
            self.total[...] = value

        @pl.when(self.away > 0)
        def _():
            self.send_four[...] = value.astype(self.dtype)
            self.line(self.away).start()

    def fifth(self):
        @pl.when(self.away == 0)
        def _():
            value = self.total[...]
            for away in range(1, self.p.depth):
                self.line(away).wait_recv()
                value = value + self.got_four[away - 1].astype(F32)
            self.total[...] = value
            self.copy(3 + self.p.depth).start()

    def finish(self, write):
        last = self.copy(3 + self.p.depth)

        @pl.when(self.away == 0)
        def _():
            last.wait_recv()
            write(self.p.core, self.total[...])
            write(1 - self.p.core, self.joined[...])
            last.wait_send()

        @pl.when(self.away > 0)
        def _():
            self.line(self.away).wait_send()

        for slot in range(1, 4):
            self.copy(slot).wait_send()


def writer(ref, rows, first, width):
    def write(core, value):
        ref[rows, pl.ds(pl.multiple_of(first + core * width, width), width)] = value

    return write


def middle_kernel(shards, tall, *refs):
    mid_hbm, dy_ref, own_ref, b0_hbm, w2_ref, vec_ref, hb_ref = refs[:7]
    act_hbm, mg_hbm, bl_hbm, cl_hbm, w2g_ref, w1g_ref, vg_ref, hbg_ref = refs[7:15]
    inp_ref, act_ref, grad_ref, two_ref, stage, w1_ref, fullb, fullc, local = refs[15:24]
    sems, sums = refs[24:26], refs[26:]
    j, p = pl.program_id(0), Place(shards)
    depth = p.depth
    chunk = w2_ref.shape[1] * 4
    rows_all = dy_ref.shape[0]
    turns = rows_all // tall
    gain, shift = vec_ref[5:6], vec_ref[6:7]
    root = math.sqrt(2.0 / math.pi)
    weights = [
        Gather(p, w1_ref, sems, k - 1, k * chunk, chunk) for k in range(1, depth)
    ]
    def blocks(k):
        return (
            OwnerSum(p, fullc.at[lax.rem(k, 2)], sums[11:], k, k),
            BlockSum(p, fullb.at[lax.rem(k, 2)], sums[:11], k),
        )

    def each(k, stage, *args):
        for job in blocks(k):
            getattr(job, stage)(*args)

    def rows_of(t):
        return pl.ds(pl.multiple_of(t * tall, tall), tall)

    def again(t):
        return pltpu.make_async_copy(mid_hbm.at[rows_of(t)], stage.at[t % 2], local.at[t])

    def results(t):
        return pltpu.make_async_copy(two_ref.at[rows_of(t)], mg_hbm.at[rows_of(t)], local.at[2 * turns + t])

    def first_chunk():
        return pltpu.make_async_copy(b0_hbm, w1_ref.at[:, :, :, pl.ds(0, chunk)], local.at[3 * turns])

    @pl.when(j == 0)
    def _():
        first_chunk().start()
        again(0).start()
        w1_ref[p.zed, lax.rem(p.me, 4), :, pl.ds(chunk, (depth - 1) * chunk)] = own_ref[:, pl.ds(chunk, (depth - 1) * chunk)]
        p.greet()
        for w in weights:
            w.own()
        for t in range(turns):
            if t + 1 < turns:
                again(t + 1).start()
            again(t).wait()
            rows = rows_of(t)
            unit, _ = normalise(stage[t % 2])
            inp_ref[rows, :] = (unit * gain + shift).astype(BF)
            two_ref[rows, :] = jnp.zeros((tall, two_ref.shape[1]), F32)
        first_chunk().wait()

    cols = pl.ds(pl.multiple_of(j * chunk, chunk), chunk)

    def chunk_rows(t, carry):
        rows = rows_of(t)
        w1 = w1_ref[:, :, :, cols].reshape(-1, chunk)
        w2 = w2_ref[...].reshape(chunk, -1)
        z = nn(inp_ref[rows, :], w1) + hb_ref[...]
        act_grad = nt(dy_ref[rows, :], w2)
        square = z * z
        bend = jnp.tanh(root * z * (1.0 + 0.044715 * square))
        half = 0.5 * (1.0 + bend)
        act = (z * half).astype(BF)
        slope = half + 0.5 * z * (1.0 - bend * bend) * (root * (1.0 + 0.134145 * square))
        grad = (act_grad * slope).astype(BF)
        act_ref[rows, :] = act
        grad_ref[rows, :] = grad
        two_ref[rows, :] += nt(grad, w1)
        hbg_ref[...] += column_sum(grad.astype(F32))

        first, later = weights[0], weights[1:]

        @pl.when(j == 0)
        def _():
            @pl.when(t == 0)
            def _():
                first.column()

            @pl.when(t == 1)
            def _():
                first.plane()
                for w in later:
                    w.column()

            pl.when(t == 2)(first.rest)

            @pl.when(t == 3)
            def _():
                for w in later:
                    w.plane()

        @pl.when((j == 1) & (t == 0))
        def _():
            for w in later:
                w.rest()

        @pl.when(j > 0)
        def _():
            pl.when(t == 0)(functools.partial(each, j - 1, "second"))
            pl.when(t == 3)(functools.partial(each, j - 1, "third"))

        return carry

    hbg_ref[...] = jnp.zeros_like(hbg_ref)
    lax.fori_loop(0, turns, chunk_rows, 0)
    store = pltpu.make_async_copy(act_ref, act_hbm.at[:, cols], local.at[turns])
    store.start()
    for k, w in enumerate(weights):
        pl.when(j == k)(w.joined)

    fullc[lax.rem(j, 2)] = tn(act_ref[...], dy_ref[...]).astype(BF).reshape(fullc.shape[1:])
    fullb[lax.rem(j, 2)] = tn(inp_ref[...], grad_ref[...]).astype(BF).reshape(fullb.shape[1:])

    store.wait()

    @pl.when(j < depth - 1)
    def _():
        each(j, "first")

    @pl.when(j > 1)
    def _():
        each(j - 2, "fifth")

    @pl.when(j > 0)
    def _():
        each(j - 1, "fourth")

    @pl.when(j == depth - 1)
    def _():
        lasts = (
            pltpu.make_async_copy(fullb.at[(depth - 1) % 2], bl_hbm, local.at[3 * turns]),
            pltpu.make_async_copy(fullc.at[(depth - 1) % 2], cl_hbm, local.at[3 * turns + 1]),
        )
        for copy in lasts:
            copy.start()
        w2g_ref[...] = jnp.zeros_like(w2g_ref)
        again(0).start()
        vg_ref[...] = jnp.zeros_like(vg_ref)
        for t in range(turns):
            rows = rows_of(t)
            if t + 1 < turns:
                again(t + 1).start()
            again(t).wait()
            unit, inverse = normalise(stage[t % 2])
            two, up = two_ref[rows, :], dy_ref[rows, :].astype(F32)
            vg_ref[0:1] += column_sum(two * unit)
            vg_ref[1:2] += column_sum(two)
            vg_ref[2:3] += column_sum(up)
            two_ref[rows, :] = up + norm_back(two, unit, inverse, gain)
            results(t).start()
        each(depth - 2, "fifth")
        for t in range(turns):
            results(t).wait()
        for copy in lasts:
            copy.wait()
        for w in weights:
            w.drained()
        for k in range(depth - 1):
            c, b = blocks(k)
            c.finish(writer(w2g_ref, slice(None), 0, w2g_ref.shape[1] // 2))
            b.finish(writer(w1g_ref, slice(None), k * chunk, chunk // 2))


def middle(shards, mid, dy, w1_own, b0, w2, vec, hb):
    rows, d = mid.shape
    depth = shards // 4
    hidden = w1_own.shape[1]
    chunk = hidden // depth
    tall = min(ROWS, rows)
    turns = rows // tall
    less = depth - 1
    anywhere = pl.BlockSpec(memory_space=pl.ANY)
    fullb = (depth, 4, w1_own.shape[0], chunk)
    w1g = (w1_own.shape[0], less * chunk)
    fullc = (1, 4) + w2.shape[1:]
    return pl.pallas_call(
        lambda *refs: middle_kernel(shards, tall, *refs),
        grid=(depth,),
        in_specs=[
            anywhere, whole(dy.shape), whole(w1_own.shape), anywhere,
            pl.BlockSpec((4,) + w2.shape[1:], lambda j: (j, 0, 0)), whole(vec.shape), pl.BlockSpec((1, chunk), lambda j: (0, j)),
        ],
        out_specs=[
            anywhere, anywhere, anywhere, anywhere, whole(w2.shape[1:]), whole(w1g), whole((8, d)),
            pl.BlockSpec((1, chunk), lambda j: (0, j)),
        ],
        out_shape=[
            shaped((rows, hidden), BF), shaped((rows, d), F32), shaped(fullb, BF), shaped(fullc, BF), shaped(w2.shape[1:], F32),
            shaped(w1g, F32),
            shaped((8, d), F32), shaped((1, hidden), F32),
        ],
        scratch_shapes=[
            pltpu.VMEM((rows, d), BF), pltpu.VMEM((rows, chunk), BF), pltpu.VMEM((rows, chunk), BF),
            pltpu.VMEM((rows, d), F32), pltpu.VMEM((2, tall, d), F32),
            pltpu.VMEM((depth, 4) + w1_own.shape, BF), pltpu.VMEM((2,) + fullb, BF),
            pltpu.VMEM((2,) + fullc, BF), pltpu.SemaphoreType.DMA((3 * turns + 2,)),
        ] + Gather.kinds(depth, less) + BlockSum.kinds(fullb, BF, less) + OwnerSum.kinds(fullc, BF, depth, less),
        compiler_params=pltpu.CompilerParams(
            dimension_semantics=("arbitrary",), collective_id=3, has_side_effects=True, vmem_limit_bytes=VMEM_LIMIT
        ),
        name="middle",
    )(mid, dy, w1_own, b0, w2, vec, hb)


def enter_kernel(shards, width, steps, *refs):
    tok_ref, wq, wk, wv, wo, w1, w2, small = refs[:8]
    attn_out, w1_out, w2_out, small_out, vec_out = refs[8:13]
    results = refs[13:21]
    attn, tiles_in, local = refs[21:24]
    sems = refs[24:26]
    step = pl.program_id(0)
    p = Place(shards)
    depth = p.depth
    rows = wq.shape[0]
    s, b, c, *early = (
        Gather(p, full, sems, i)
        for i, full in enumerate(
            [tiles_in, w1_out, w2_out] + [attn.at[:, :, i * rows : (i + 1) * rows] for i in range(4)]
        )
    )
    early.insert(0, s)

    def start():
        mine = p.zed, lax.rem(p.me, 4)
        copies = [
            pltpu.make_async_copy(w, out.at[mine], local.at[i])
            for i, (w, out) in enumerate(((w1, w1_out), (w2, w2_out)))
        ]
        for copy in copies:
            copy.start()
        attn[mine] = jnp.concatenate([w[...] for w in (wq, wk, wv, wo)], axis=0)
        tiles_in[mine] = small[...]
        for copy in copies:
            copy.wait()
        p.greet()
        for g in early + [b, c]:
            g.own()
        for g in early:
            g.column()
        for g in early:
            g.plane()
        b.column()
        for g in early:
            g.rest()
        b.plane()
        for g in early[:-1]:
            g.joined()
        vec = jnp.zeros(vec_out.shape, F32)
        blank = jnp.zeros((8, vec.shape[1] - 128), F32)
        for i in range(shards):
            piece = jnp.concatenate([tiles_in[i // 4, i % 4, :, :128], blank], axis=1)
            vec = vec + (pltpu.roll(piece, i * rows, 1) if i else piece)
        vec_out[...] = vec
        small_out[...] = tiles_in[...]

    def keep():
        return pltpu.make_async_copy(attn, attn_out, local.at[2])

    def whole_attn():
        early[-1].joined()
        keep().start()

    def end():
        b.joined(), c.joined()
        for g in early + [b, c]:
            g.drained()
        keep().wait()

    pl.when(step == 0)(start)
    plan = {(0, 1): [whole_attn, c.column], (0, 2): [b.rest], (steps // 2 - 1, 3): [c.plane], (steps - 1, 2): [c.rest], (steps - 1, 3): [end]}
    view = [attn.at[:, :, i * rows : (i + 1) * rows, :] for i in range(4)]
    attend_kernel(width, tok_ref, view, vec_out, *results, tick=ticker(plan, step))


def enter(shards, tokens, wq, wk, wv, wo, w1, w2, small, heads):
    rows, d = tokens.shape
    t = min(ROWS, rows)
    pairs = d // PAIR
    blocks = rows // BLOCK
    big = tiles(t, d)
    depth = shards // 4
    lead = (depth, 4)
    anywhere = pl.BlockSpec(memory_space=pl.ANY)
    packed = lead + (4 * wq.shape[0], d)
    full_small = lead + small.shape
    chunk = w1.shape[1] // depth
    return pl.pallas_call(
        lambda *refs: enter_kernel(shards, d // heads, rows // t, *refs),
        grid=(rows // t,),
        in_specs=[big] + [whole(w.shape) for w in (wq, wk, wv, wo)] + [whole((w1.shape[0], chunk))] + [whole(w.shape) for w in (w2, small)],
        out_specs=[
            anywhere, anywhere, anywhere, whole(full_small), whole((8, d)), big, big, big,
            pl.BlockSpec((t // BLOCK, pairs, FRAMES, 2 * BLOCK), lambda i: (i, 0, 0, 0)),
            big, big,
            whole((pairs, FRAMES, 2 * BLOCK)), big,
        ],
        out_shape=[
            shaped(packed, BF), shaped(lead + (w1.shape[0], chunk), BF), shaped(lead + w2.shape, BF),
            shaped(full_small, F32), shaped((8, d), F32),
        ]
        + [shaped((rows, d), BF)] * 3
        + [shaped((blocks, pairs, FRAMES, 2 * BLOCK), F32), shaped((rows, d), BF), shaped((rows, d), F32)]
        + [shaped((pairs, FRAMES, 2 * BLOCK), F32), shaped((rows, d), BF)],
        scratch_shapes=[
            pltpu.VMEM(packed, BF), pltpu.VMEM(full_small, F32), pltpu.SemaphoreType.DMA((3,)),
        ] + Gather.kinds(depth, 7),
        compiler_params=pltpu.CompilerParams(
            dimension_semantics=("arbitrary",), collective_id=0, has_side_effects=True, vmem_limit_bytes=VMEM_LIMIT
        ),
        name="enter",
    )(tokens, wq, wk, wv, wo, w1, w2, small)


def leave_kernel(shards, width, steps, *refs):
    mg_ref, q_ref, k_ref, v_ref, p_ref, mix_ref, wo_ref, fullb, fullc, w1_in, w2_in = refs[:11]
    dq_ref, dk_ref, dv_ref, wog_ref, vg_ref, w1_out, w2_out = refs[11:18]
    acco, mgl_ref = refs[18:20]
    own = refs[20:]
    step, p = pl.program_id(0), Place(shards)
    b = BlockSum(p, fullb, own[:11])
    c = OwnerSum(p, fullc, own[11:22], 0, p.depth - 1)
    wide = fullb.shape[3]

    def others():
        w1_out[:, : (p.depth - 1) * wide] = w1_in[...]
        w2_out[...] = w2_in[...]

    def finish():
        c.finish(writer(w2_out, slice(None), 0, w2_out.shape[1] // 2))
        b.finish(writer(w1_out, slice(None), (p.depth - 1) * wide, wide // 2))

    events = [
        (0, p.greet), (0, c.first), (0, b.first), (1, others), (2, c.second), (2, b.second), (5, c.third), (5, b.third),
        (8, c.fourth), (8, b.fourth), (11, c.fifth), (11, b.fifth),
    ]
    points = [(when, where) for when in range(steps) for where in range(3)]
    plan = {}
    for at, event in events:
        plan.setdefault(points[at * len(points) // 12], []).append(event)
    tick = ticker(plan, step)

    @pl.when(step == 0)
    def _():
        acco[...] = jnp.zeros_like(acco)
        vg_ref[...] = jnp.zeros_like(vg_ref)

    tick(0)
    branch = mg_ref[...].astype(BF)
    mgl_ref[...] = nt(branch, square(wo_ref)).astype(BF)
    acco[...] += tn(mix_ref[...], branch)
    vg_ref[4:5] += column_sum(branch.astype(F32))
    tick(1)
    attention_back(width, mgl_ref, q_ref, k_ref, v_ref, p_ref, dq_ref, dk_ref, dv_ref)
    vg_ref[2:3] += column_sum(dq_ref[...].astype(F32))
    vg_ref[3:4] += column_sum(dv_ref[...].astype(F32))
    tick(2)

    @pl.when(step == steps - 1)
    def _():
        wog_ref[...] = acco[...].astype(BF).reshape(wog_ref.shape)
        finish()


def leave(shards, mg, q, k, v, p, mixed, attn, fullb, fullc, w1g, w2g, heads):
    rows, d = mg.shape
    t = min(ROWS, rows)
    pairs = d // PAIR
    big = tiles(t, d)
    w1_out, w2_out = (w1g.shape[0], shards // 4 * fullb.shape[3]), w2g.shape
    wog = (shards // 4, 4, attn.shape[1] // 4, d)
    return pl.pallas_call(
        lambda *refs: leave_kernel(shards, d // heads, rows // t, *refs),
        grid=(rows // t,),
        in_specs=[
            big, big, big, big,
            pl.BlockSpec((t // BLOCK, pairs, FRAMES, 2 * BLOCK), lambda i: (i, 0, 0, 0)),
            big, weight_specs((attn,))[3],
        ] + [whole(x.shape) for x in (fullb, fullc, w1g, w2g)],
        out_specs=[big, big, big, whole(wog), whole((8, d)), whole(w1_out), whole(w2_out)],
        out_shape=[shaped((rows, d), BF)] * 3
        + [shaped(wog, BF), shaped((8, d), F32), shaped(w1_out, F32), shaped(w2_out, F32)],
        scratch_shapes=[pltpu.VMEM((d, d), F32), pltpu.VMEM((t, d), BF)]
        + BlockSum.kinds(fullb.shape, BF) + OwnerSum.kinds(fullc.shape, BF, shards // 4),
        compiler_params=pltpu.CompilerParams(
            dimension_semantics=("arbitrary",), collective_id=1, has_side_effects=True, vmem_limit_bytes=VMEM_LIMIT
        ),
        name="leave",
    )(mg, q, k, v, p, mixed, attn, fullb, fullc, w1g, w2g)


def last_kernel(shards, steps, *refs):
    tok_ref, mg_ref, dq_hbm, dk_hbm, dv_hbm, one_hbm, wq, wk, wv, vec_ref, wog_ref, vgin_ref, hbt_ref, top_ref, mid_ref, act_ref, w2_hbm = refs[:17]
    gt_ref, lo_ref, attn_out, small_out, top_out = refs[17:22]
    d_ref, one_ref, full, tile, vg, w2_ref, local = refs[22:29]
    jobs, little, most, straight = refs[29:40], refs[40:51], refs[51:55], refs[55:]
    turns = (steps - 3) // 2
    step, p = pl.program_id(0), Place(shards)
    rows = wog_ref.shape[2]
    d = vg.shape[1]
    wide = attn_out.shape[1] // 2
    o = BlockSum(p, wog_ref, jobs, 3)
    s = BlockSum(p, tile, little)
    t = Largest(p, top_ref, top_out, *most)
    late = Direct(p, straight)
    weight = lambda i: BlockSum(p, full.at[i], jobs, i)
    q, k, v = weight(0), weight(1), weight(2)
    many = functools.partial
    events = [
        (1, o.second), (1, s.second), (2, q.second), (3, many(t.take, 0)), (3, many(t.push, 1)), (3, s.third), (4, o.third),
        (5, k.second), (5, many(t.take, 1)), (5, many(t.push, 2)), (5, s.fourth), (7, v.second), (7, q.third),
        (8, o.fourth), (9, many(t.take, 2)), (9, many(t.push, 3)), (9, s.fifth), (9, k.third), (11, q.fourth),
        (11, v.third), (13, o.fifth), (13, k.fourth), (13, many(t.take, 3)), (15, v.fourth), (15, q.fifth), (18, k.fifth),
        (20, v.fifth),
    ]
    plan = {}
    for at, event in events:
        at = min(at, 2 * steps - 1)
        plan.setdefault((at // 2, at % 2), []).append(event)
    tick = ticker(plan, step)
    fetches = [
        pltpu.make_async_copy(src, dst, local.at[i])
        for i, (src, dst) in enumerate(
            ((dq_hbm, d_ref.at[0]), (dk_hbm, d_ref.at[1]), (dv_hbm, d_ref.at[2]), (one_hbm, one_ref), (w2_hbm, w2_ref))
        )
    ]

    def spread(value, put):
        for i in range(shards):
            put(i, (pltpu.roll(value, d - i * rows, 1) if i else value)[:, :128])

    @pl.when(step == 0)
    def _():
        for i in (3, 0, 1, 2, 4):
            fetches[i].start()
        vg[...] = jnp.zeros_like(vg)

        def put(i, piece):
            tile[i // 4, i % 4, :, :128] = piece

        spread(vgin_ref[...], put)
        tile[:, :, :, 128:] = hbt_ref[...]
        late.greet()
        o.first(), s.first(), t.push(0)
        fetches[3].wait()

    tick(0)

    for i in range(3):
        pl.when(step == i)(fetches[i].wait)

    @pl.when(step < 3)
    def _():
        full[step] = tn(one_ref[...], d_ref[step]).astype(BF).reshape(full.shape[1:])
        weight(step).first()

    pl.when(step == 3 + turns)(fetches[4].wait)

    @pl.when(step >= 3 + turns)
    def _():
        w2 = square(w2_ref)
        lo_ref[...] = (mid_ref[...] + (nn(act_ref[...], w2) + vec_ref[7:8])).astype(BF)

    @pl.when((step >= 3) & (step < 3 + turns))
    def _():
        tall = tok_ref.shape[0]
        at = pl.ds(pl.multiple_of((step - 3) * tall, tall), tall)
        unit, inverse = normalise(tok_ref[...].astype(F32))
        grad = nt(d_ref[0, at], square(wq)) + nt(d_ref[1, at], square(wk)) + nt(d_ref[2, at], square(wv))
        vg[0:1] += column_sum(grad * unit)
        vg[1:2] += column_sum(grad)
        gt_ref[...] = (mg_ref[...] + norm_back(grad, unit, inverse, vec_ref[0:1])).astype(BF)

    @pl.when(step == 2 + turns)
    def _():
        def put(i, piece):
            late.tiles[i] = piece

        spread(vg[...], put)
        late.push()

    tick(1)

    @pl.when(step == steps - 1)
    def _():
        s.finish(writer(small_out, slice(None), 0, small_out.shape[1] // 2))
        small_out[0:2, :128] = late.sum()[0:2]
        for i, job in ((3, o), (0, q), (1, k), (2, v)):
            job.finish(writer(attn_out, slice(i * rows, (i + 1) * rows), 0, wide))


def last(shards, tokens, mg, dq, dk, dv, one, attn, vec, wog, vgin, hbt, top, mid, act, w2):
    rows, d = tokens.shape
    t = min(ROWS, rows)
    depth = shards // 4
    turns = rows // t
    steps = 3 + 2 * turns
    later = pl.BlockSpec((t, d), lambda i: (jnp.clip(i - 3, 0, turns - 1), 0))
    latest = lambda width: pl.BlockSpec((t, width), lambda i: (jnp.maximum(i - 3 - turns, 0), 0))
    anywhere = pl.BlockSpec(memory_space=pl.ANY)
    small = (depth, 4, 8, 256)
    return pl.pallas_call(
        lambda *refs: last_kernel(shards, steps, *refs),
        grid=(steps,),
        in_specs=[later, later] + [anywhere] * 4 + weight_specs((attn,))[:3]
        + [whole(x.shape) for x in (vec, wog, vgin, hbt, top)] + [latest(d), latest(act.shape[1]), anywhere],
        out_specs=[later, latest(d), whole((4 * wog.shape[2], d)), whole((8, 256)), whole((8, 128))],
        out_shape=[
            shaped((rows, d), BF), shaped((rows, d), BF), shaped((4 * wog.shape[2], d), F32), shaped((8, 256), F32), shaped((8, 128), F32),
        ],
        scratch_shapes=[
            pltpu.VMEM((3, rows, d), BF), pltpu.VMEM((rows, d), BF), pltpu.VMEM((3,) + wog.shape, BF),
            pltpu.VMEM(small, F32), pltpu.VMEM((8, d), F32), pltpu.VMEM(w2.shape, BF), pltpu.SemaphoreType.DMA((5,)),
        ] + BlockSum.kinds(wog.shape, BF, 4) + BlockSum.kinds(small, F32) + [
            pltpu.VMEM((depth + 2, 8, 128), F32), pltpu.VMEM((4, 8, 128), F32),
            pltpu.SemaphoreType.DMA((depth + 2,)), pltpu.SemaphoreType.DMA((depth + 2,)),
        ] + Direct.kinds(shards),
        compiler_params=pltpu.CompilerParams(
            dimension_semantics=("arbitrary",), collective_id=2, has_side_effects=True, vmem_limit_bytes=VMEM_LIMIT
        ),
        name="last",
    )(tokens, mg, dq, dk, dv, one, attn, attn, attn, vec, wog, vgin, hbt, top, mid, act, w2)


def on_device(shards, reps, *args):
    (
        tokens, grad_out, first_gain, first_shift, query_proj, query_bias, key_proj, value_proj, value_bias,
        output_proj, output_bias, second_gain, second_shift, hidden_proj, hidden_bias, final_proj, final_bias, threshold,
    ) = args
    heads = threshold.shape[0]
    d = tokens.shape[1]
    hidden = hidden_proj.shape[1]
    head_dim = d // heads
    small = (first_gain, first_shift, query_bias, value_bias, output_bias, second_gain, second_shift, final_bias)
    rows, more = small[0].shape[0], hidden_bias.shape[0] // 8
    whole_chunks = shards % 4 == 0 and hidden * 4 % (shards * 256) == 0 and hidden * 4 // shards == 4 * final_proj.shape[0]
    own = whole_chunks and reps == 2 and shards % 4 == 0 and shards > 4 and rows % 16 == 0 and rows <= 128 and more <= 128

    def gather(x):
        return lax.all_gather(x, "shard", axis=0, tiled=True)

    def scatter(x):
        y = lax.psum_scatter(x.astype(BF), "shard", scatter_dimension=0, tiled=True)
        return lax.psum(y, "rep").astype(F32)

    if own:
        tile = jnp.concatenate(
            [
                jnp.pad(jnp.stack(small).astype(F32), ((0, 0), (0, 128 - rows))),
                jnp.pad(hidden_bias.astype(F32).reshape(8, more), ((0, 0), (0, 128 - more))),
            ],
            axis=1,
        )
        attn, w1, w2, tile, vec, q, k, v, p, mixed, mid, top, one = enter(
            shards, tokens, query_proj, key_proj, value_proj, output_proj, hidden_proj, final_proj, tile, heads
        )
        tile = tile.reshape(shards, 8, -1)
        hb = tile[:, :, 128 : 128 + more].reshape(1, hidden)
        attn, w2 = attn.reshape(shards, -1, d), w2.reshape(shards, -1, d)
    else:
        weights = tuple(gather(x) for x in (query_proj, key_proj, value_proj, output_proj))
        w1, w2 = gather(hidden_proj), gather(final_proj)
        vec = jnp.stack([gather(x) for x in small]).astype(F32)
        hb = gather(hidden_bias).astype(F32)[None]
        q, k, v, p, mixed, mid, top = attend(tokens, weights, vec, heads)
    local = jnp.max(top.reshape(top.shape[0], FRAMES, 2, BLOCK), axis=(1, 3)).reshape(heads)
    if own:
        act, mg, b3g, c3g, w2g, w1g, vg2, hbg = middle(shards, mid, grad_out, hidden_proj, w1, w2, vec, hb)
        dq, dk, dv, wog, vg1, w1g, w2g = leave(
            shards, mg, q, k, v, p, mixed, attn, b3g, c3g, w1g, w2g, heads
        )
        hbt = jnp.pad(hbg.reshape(shards // 4, 4, 8, more), ((0, 0), (0, 0), (0, 0), (0, 128 - more)))
        grad_tokens, layer_output, attn, tile, top = last(
            shards, tokens, mg, dq, dk, dv, one, attn, vec, wog, jnp.concatenate([vg1[:5], vg2[:3]]), hbt,
            jnp.broadcast_to(jnp.pad(local, (0, 128 - heads))[None], (8, 128)),
            mid, act, w2,
        )
    else:
        layer_output, mg, w1g, w2g, vg2, hbg = mlp(mid, grad_out, w1, w2, vec, hb)
        grad_tokens, wg, vg1 = back(tokens, mg, q, k, v, p, mixed, weights, vec, heads)
    if own:
        wg = tuple(attn[i * rows : (i + 1) * rows] for i in range(4))
        vg = tuple(tile[i, :rows] for i in range(8))
        hbg = tile[:, 128 : 128 + more].reshape(-1)
        global_max = top[0, :heads]
    else:
        vg = jnp.concatenate([vg1[:5], vg2[:3]])
        global_max = lax.pmax(local, ("shard", "rep"))
        wg = tuple(scatter(x) for x in wg)
        w1g, w2g = scatter(w1g), scatter(w2g)
        vg = tuple(scatter(vg[i]) for i in range(8))
        hbg = scatter(hbg[0])
    factor = jnp.minimum(1.0, threshold / global_max)
    column_scale = jnp.repeat(jnp.sqrt(factor), head_dim)
    bias_scale = lax.dynamic_slice_in_dim(column_scale, lax.axis_index("shard") * rows, rows)
    return (
        layer_output, grad_tokens, vg[0], vg[1], wg[0], vg[2], wg[1], wg[2], vg[3], wg[3], vg[4], vg[5], vg[6],
        w1g, hbg, w2g, vg[7], global_max, factor,
        query_proj.astype(F32) * column_scale[None, :], query_bias.astype(F32) * bias_scale,
        key_proj.astype(F32) * column_scale[None, :],
    )


def solution(mesh):
    in_specs = (
        P(("shard", "rep"), None),
        P(("shard", "rep"), None),
        P("shard"),
        P("shard"),
        P("shard", None),
        P("shard"),
        P("shard", None),
        P("shard", None),
        P("shard"),
        P("shard", None),
        P("shard"),
        P("shard"),
        P("shard"),
        P("shard", None),
        P("shard"),
        P("shard", None),
        P("shard"),
        P(),
    )
    out_specs = (
        P(("shard", "rep"), None),
        P(("shard", "rep"), None),
        P("shard"),
        P("shard"),
        P("shard", None),
        P("shard"),
        P("shard", None),
        P("shard", None),
        P("shard"),
        P("shard", None),
        P("shard"),
        P("shard"),
        P("shard"),
        P("shard", None),
        P("shard"),
        P("shard", None),
        P("shard"),
        P(),
        P(),
        P("shard", None),
        P("shard"),
        P("shard", None),
    )
    shards, reps = mesh.shape["shard"], mesh.shape["rep"]
    return jax.shard_map(
        functools.partial(on_device, shards, reps), mesh=mesh, in_specs=in_specs, out_specs=out_specs, check_vma=False
    )
```

```python
import functools
import math

import jax
import jax.numpy as jnp
from jax import lax
from jax.experimental import pallas as pl
from jax.experimental.pallas import tpu as pltpu
from jax.sharding import PartitionSpec as P

FRAMES = 16
EPSILON = 1e-06
BF = jnp.bfloat16
F32 = jnp.float32
ROWS = 512
BLOCK = 128
PAIR = 128


def nn(left, right):
    return lax.dot_general(left, right, (((1,), (0,)), ((), ())), preferred_element_type=F32)


def nt(left, right):
    return lax.dot_general(left, right, (((1,), (1,)), ((), ())), preferred_element_type=F32)


def tn(left, right):
    return lax.dot_general(left, right, (((0,), (0,)), ((), ())), preferred_element_type=F32)


def normalise(values):
    centred = values - jnp.mean(values, axis=-1, keepdims=True)
    inverse = lax.rsqrt(jnp.mean(centred * centred, axis=-1, keepdims=True) + EPSILON)
    return centred * inverse, inverse


def norm_back(grad, unit, inverse, gain):
    scaled = grad * gain
    return inverse * (
        scaled
        - jnp.mean(scaled, axis=-1, keepdims=True)
        - unit * jnp.mean(scaled * unit, axis=-1, keepdims=True)
    )


def column_sum(values):
    return jnp.sum(values, axis=0, keepdims=True)


def place_masks():
    lane = lax.broadcasted_iota(jnp.int32, (FRAMES, 2 * BLOCK), 1)
    return [(lane % BLOCK) // FRAMES == p for p in range(BLOCK // FRAMES)]


def halves(width):
    lane = lax.broadcasted_iota(jnp.int32, (1, PAIR), 1)
    first = (lane < width).astype(F32)
    return first.astype(BF), (1.0 - first).astype(BF)


def compress(wide, masks):
    total = wide[:FRAMES]
    for p in range(1, len(masks)):
        total = jnp.where(masks[p], wide[p * FRAMES : (p + 1) * FRAMES], total)
    return total


def expand(packed, masks):
    zero = jnp.zeros_like(packed)
    return jnp.concatenate([jnp.where(m, packed, zero).astype(BF) for m in masks], axis=0)


def split(two, first, second):
    return jnp.concatenate([two * first, two * second], axis=0)


def stack(wide):
    return jnp.concatenate([wide[:, :BLOCK], wide[:, BLOCK:]], axis=0)


def square(ref):
    value = ref[...]
    return value.reshape(-1, value.shape[-1])


def attend_kernel(
    width, tok_ref, w_refs, vec_ref,
    q_ref, k_ref, v_ref, p_ref, mix_ref, mid_ref, top_ref, one_ref=None, tick=lambda point: None,
):
    scale = 1.0 / math.sqrt(width)
    wq, wk, wv = (square(w) for w in w_refs[:3])
    gain, shift = vec_ref[0:1], vec_ref[1:2]
    tok = tok_ref[...].astype(F32)
    unit, _ = normalise(tok)
    one = (unit * gain + shift).astype(BF)
    if one_ref is not None:
        one_ref[...] = one
    q_ref[...] = (nn(one, wq) + vec_ref[2:3]).astype(BF)
    k_ref[...] = nn(one, wk).astype(BF)
    v_ref[...] = (nn(one, wv) + vec_ref[3:4]).astype(BF)
    tick(1)
    masks = place_masks()
    first, second = halves(width)
    pairs = tok_ref.shape[1] // PAIR

    @pl.when(pl.program_id(0) == 0)
    def _():
        top_ref[...] = jnp.full(top_ref.shape, -3e38, F32)

    def body(i, carry):
        rows = pl.ds(pl.multiple_of(i * BLOCK, BLOCK), BLOCK)
        for h in range(pairs):
            cols = slice(h * PAIR, (h + 1) * PAIR)
            two_q, two_k, two_v = q_ref[rows, cols], k_ref[rows, cols], v_ref[rows, cols]
            scores = compress(nt(two_k, split(two_q, first, second)), masks) * scale
            top_ref[h] = jnp.maximum(top_ref[h], scores)
            expo = jnp.exp(scores - jnp.max(scores, axis=0, keepdims=True))
            probs = expo / jnp.sum(expo, axis=0, keepdims=True)
            p_ref[i, h] = probs
            mixed = tn(stack(expand(probs, masks)), split(two_v, first, second))
            mix_ref[rows, cols] = mixed.astype(BF)
        return carry

    lax.fori_loop(0, tok_ref.shape[0] // BLOCK, body, 0, unroll=2)
    tick(2)
    mid_ref[...] = tok_ref[...].astype(F32) + (nn(mix_ref[...], square(w_refs[3])) + vec_ref[4:5])
    tick(3)


def mlp_kernel(
    chunk, mid_ref, dy_ref, w1_ref, w2_ref, vec_ref, hb_ref,
    out_ref, mg_ref, w1g_ref, w2g_ref, vg_ref, hbg_ref,
    acc1, acc2, res_ref, two_ref,
):
    step, last = pl.program_id(0), pl.num_programs(0) - 1
    gain, shift = vec_ref[5:6], vec_ref[6:7]
    mid = mid_ref[...]
    unit, inverse = normalise(mid)
    inp = (unit * gain + shift).astype(BF)
    dy = dy_ref[...]
    hidden = w1_ref.shape[1]

    @pl.when(step == 0)
    def _():
        acc1[...] = jnp.zeros_like(acc1)
        acc2[...] = jnp.zeros_like(acc2)
        vg_ref[...] = jnp.zeros_like(vg_ref)
        hbg_ref[...] = jnp.zeros_like(hbg_ref)

    res_ref[...] = mid + vec_ref[7:8]
    two_ref[...] = jnp.zeros_like(two_ref)
    root = math.sqrt(2.0 / math.pi)

    def body(j, carry):
        cols = pl.ds(pl.multiple_of(j * chunk, chunk), chunk)
        z = nn(inp, w1_ref[:, cols]) + hb_ref[:, cols]
        act_grad = nt(dy, w2_ref[cols, :])
        square = z * z
        bend = jnp.tanh(root * z * (1.0 + 0.044715 * square))
        half = 0.5 * (1.0 + bend)
        act = (z * half).astype(BF)
        slope = half + 0.5 * z * (1.0 - bend * bend) * (root * (1.0 + 0.134145 * square))
        grad = (act_grad * slope).astype(BF)
        res_ref[...] += nn(act, w2_ref[cols, :])
        two_ref[...] += nt(grad, w1_ref[:, cols])
        acc2[cols, :] += tn(act, dy)
        acc1[:, cols] += tn(inp, grad)
        hbg_ref[:, cols] += column_sum(grad.astype(F32))
        return carry

    lax.fori_loop(0, hidden // chunk, body, 0)
    out_ref[...] = res_ref[...].astype(BF)
    two = two_ref[...]
    up = dy.astype(F32)
    mg_ref[...] = up + norm_back(two, unit, inverse, gain)
    vg_ref[0:1] += column_sum(two * unit)
    vg_ref[1:2] += column_sum(two)
    vg_ref[2:3] += column_sum(up)

    @pl.when(step == last)
    def _():
        w1g_ref[...] = acc1[...].astype(BF)
        w2g_ref[...] = acc2[...].astype(BF)


def attention_back(width, mgl_ref, q_ref, k_ref, v_ref, p_ref, dq_ref, dk_ref, dv_ref):
    scale = 1.0 / math.sqrt(width)
    masks = place_masks()
    first, second = halves(width)
    pairs = q_ref.shape[1] // PAIR

    def body(i, carry):
        rows = pl.ds(pl.multiple_of(i * BLOCK, BLOCK), BLOCK)
        for h in range(pairs):
            cols = slice(h * PAIR, (h + 1) * PAIR)
            two_q, two_k, two_v = q_ref[rows, cols], k_ref[rows, cols], v_ref[rows, cols]
            mixed = split(mgl_ref[rows, cols], first, second)
            probs = p_ref[i, h]
            slope = compress(nt(two_v, mixed), masks)
            score = probs * (slope - jnp.sum(slope * probs, axis=0, keepdims=True))
            wide = expand(score, masks)
            dv_ref[rows, cols] = nn(expand(probs, masks), mixed).astype(BF)
            dk_ref[rows, cols] = (nn(wide, split(two_q, first, second)) * scale).astype(BF)
            dq_ref[rows, cols] = (tn(stack(wide), split(two_k, first, second)) * scale).astype(BF)
        return carry

    lax.fori_loop(0, q_ref.shape[0] // BLOCK, body, 0, unroll=4)


def back_kernel(
    width, tok_ref, mg_ref, q_ref, k_ref, v_ref, p_ref, mix_ref,
    w_refs, vec_ref,
    gt_ref, wg_refs, vg_ref,
    accq, acck, accv, acco, mgl_ref, dq_ref, dk_ref, dv_ref,
):
    step, last = pl.program_id(0), pl.num_programs(0) - 1
    gain, shift = vec_ref[0:1], vec_ref[1:2]
    accs = (accq, acck, accv, acco)
    wq, wk, wv, wo = (square(w) for w in w_refs)

    @pl.when(step == 0)
    def _():
        for acc in accs:
            acc[...] = jnp.zeros_like(acc)
        vg_ref[...] = jnp.zeros_like(vg_ref)

    branch = mg_ref[...].astype(BF)
    mgl_ref[...] = nt(branch, wo).astype(BF)
    acco[...] += tn(mix_ref[...], branch)
    vg_ref[4:5] += column_sum(branch.astype(F32))
    attention_back(width, mgl_ref, q_ref, k_ref, v_ref, p_ref, dq_ref, dk_ref, dv_ref)
    unit, inverse = normalise(tok_ref[...].astype(F32))
    one = (unit * gain + shift).astype(BF)
    dq, dk, dv = dq_ref[...], dk_ref[...], dv_ref[...]
    vg_ref[2:3] += column_sum(dq.astype(F32))
    vg_ref[3:4] += column_sum(dv.astype(F32))
    accq[...] += tn(one, dq)
    acck[...] += tn(one, dk)
    accv[...] += tn(one, dv)
    grad = nt(dq, wq) + nt(dk, wk) + nt(dv, wv)
    vg_ref[0:1] += column_sum(grad * unit)
    vg_ref[1:2] += column_sum(grad)
    gt_ref[...] = (mg_ref[...] + norm_back(grad, unit, inverse, gain)).astype(BF)

    @pl.when(step == last)
    def _():
        for i, acc in enumerate(accs):
            value = acc[...].astype(BF)
            if len(wg_refs) == 1:
                rows = wg_refs[0].shape[1] // 4
                wg_refs[0][:, i * rows : (i + 1) * rows, :] = value.reshape(-1, rows, value.shape[1])
            else:
                wg_refs[i][...] = value


def whole(shape):
    return pl.BlockSpec(shape, lambda i: (0,) * len(shape), pipeline_mode=pl.Buffered(1))


def tiles(height, width):
    return pl.BlockSpec((height, width), lambda i: (i, 0))


def shaped(shape, dtype):
    return jax.ShapeDtypeStruct(shape, dtype)


VMEM_LIMIT = 60 * 1024 * 1024


def params():
    return pltpu.CompilerParams(
        dimension_semantics=("arbitrary",), vmem_limit_bytes=VMEM_LIMIT
    )


def weight_specs(weights):
    if len(weights) == 1:
        shards, rows, d = weights[0].shape
        return [
            pl.BlockSpec((shards, rows // 4, d), lambda i, j=j: (0, j, 0), pipeline_mode=pl.Buffered(1))
            for j in range(4)
        ]
    return [whole(w.shape) for w in weights]


def four(weights):
    return tuple(weights) * (4 // len(weights))


def attend(tokens, weights, vec, heads):
    rows, d = tokens.shape
    t = min(ROWS, rows)
    pairs = d // PAIR
    blocks = rows // BLOCK
    big = tiles(t, d)
    return pl.pallas_call(
        lambda tok, wq, wk, wv, wo, *refs: attend_kernel(d // heads, tok, (wq, wk, wv, wo), *refs),
        grid=(rows // t,),
        in_specs=[big] + weight_specs(weights) + [whole(vec.shape)],
        out_specs=[
            big, big, big,
            pl.BlockSpec((t // BLOCK, pairs, FRAMES, 2 * BLOCK), lambda i: (i, 0, 0, 0)),
            big, big,
            whole((pairs, FRAMES, 2 * BLOCK)),
        ],
        out_shape=[shaped((rows, d), BF)] * 3
        + [shaped((blocks, pairs, FRAMES, 2 * BLOCK), F32), shaped((rows, d), BF), shaped((rows, d), F32)]
        + [shaped((pairs, FRAMES, 2 * BLOCK), F32)],
        compiler_params=params(),
        cost_estimate=pl.CostEstimate(flops=10 * rows * d * d, bytes_accessed=24 * rows * d, transcendentals=0),
        name="attend",
    )(tokens, *four(weights), vec)


def mlp(middle, dy, w1, w2, vec, hb):
    rows, d = middle.shape
    hidden = w1.shape[1]
    t = min(ROWS, rows)
    big = tiles(t, d)
    return pl.pallas_call(
        lambda *refs: mlp_kernel(768, *refs),
        grid=(rows // t,),
        in_specs=[big, big, whole(w1.shape), whole(w2.shape), whole(vec.shape), whole(hb.shape)],
        out_specs=[big, big, whole(w1.shape), whole(w2.shape), whole((8, d)), whole((1, hidden))],
        out_shape=[
            shaped((rows, d), BF), shaped((rows, d), F32), shaped(w1.shape, BF), shaped(w2.shape, BF),
            shaped((8, d), F32), shaped((1, hidden), F32),
        ],
        scratch_shapes=[
            pltpu.VMEM(w1.shape, F32), pltpu.VMEM(w2.shape, F32), pltpu.VMEM((t, d), F32), pltpu.VMEM((t, d), F32),
        ],
        compiler_params=params(),
        cost_estimate=pl.CostEstimate(flops=12 * rows * d * hidden, bytes_accessed=14 * rows * d, transcendentals=0),
        name="mlp",
    )(middle, dy, w1, w2, vec, hb)


def back(tokens, mg, q, k, v, p, mixed, weights, vec, heads):
    rows, d = tokens.shape
    t = min(ROWS, rows)
    pairs = d // PAIR
    big = tiles(t, d)
    count = len(weights)

    def kernel(*refs):
        ins, w_refs, vec_ref, gt_ref = refs[:7], refs[7:11], refs[11], refs[12]
        wg_refs, rest = refs[13 : 13 + count], refs[13 + count :]
        back_kernel(d // heads, *ins, w_refs, vec_ref, gt_ref, wg_refs, *rest)

    out = pl.pallas_call(
        kernel,
        grid=(rows // t,),
        in_specs=[
            big, big, big, big, big,
            pl.BlockSpec((t // BLOCK, pairs, FRAMES, 2 * BLOCK), lambda i: (i, 0, 0, 0)),
            big,
        ] + weight_specs(weights) + [whole(vec.shape)],
        out_specs=[big] + [whole(w.shape) for w in weights] + [whole((8, d))],
        out_shape=[shaped((rows, d), BF)] + [shaped(w.shape, BF) for w in weights] + [shaped((8, d), F32)],
        scratch_shapes=[pltpu.VMEM((d, d), F32)] * 4 + [pltpu.VMEM((t, d), BF)] * 4,
        compiler_params=params(),
        cost_estimate=pl.CostEstimate(flops=20 * rows * d * d, bytes_accessed=24 * rows * d, transcendentals=0),
        name="back",
    )(tokens, mg, q, k, v, p, mixed, *four(weights), vec)
    return out[0], out[1 : 1 + count], out[1 + count]


MESH = pl.DeviceIdType.MESH


class Place:
    def __init__(self, shards):
        self.shards = shards
        self.depth = shards // 4
        self.me = lax.axis_index("shard")
        self.core = lax.axis_index("rep")
        self.zed = self.me // 4
        x, y = self.me % 2, (self.me // 2) % 2
        self.near_step, self.far_step = 1 + self.core, 2 - self.core
        self.near = x + self.core * (y - x)
        self.far = y + self.core * (x - y)
        self.sibling = (self.me, 1 - self.core)
        self.near_peer = (self.block(self.zed, 1 - self.near, self.far), self.core)
        self.far_peer = (self.block(self.zed, self.near, 1 - self.far), self.core)
        self.columns = [lax.rem(self.zed + k, self.depth) for k in range(self.depth)]
        self.column_peers = [(self.block(z, self.near, self.far), self.core) for z in self.columns]

    def block(self, zed, near, far):
        return zed * 4 + near * self.near_step + far * self.far_step

    def greet(self):
        barrier = pltpu.get_barrier_semaphore()
        peers = [self.sibling, self.near_peer, self.far_peer] + self.column_peers[1:]
        for peer in peers:
            pl.semaphore_signal(barrier, inc=1, device_id=peer, device_id_type=MESH)
        pl.semaphore_wait(barrier, len(peers))


def half_of(ref, core):
    width = ref.shape[-1] // 2
    return pl.ds(pl.multiple_of(core * width, width), width)


class Gather:
    def kinds(depth, count):
        return [pltpu.SemaphoreType.DMA((count, depth + 6)), pltpu.SemaphoreType.DMA((count, depth + 6))]

    def __init__(self, place, full, sems, at, first=0, width=None):
        self.p, self.full = place, full
        self.send, self.recv = (sem.at[at] for sem in sems)
        half = (width or full.shape[-1]) // 2
        self.cols = pl.ds(pl.multiple_of(first + place.core * half, half), half)
        self.here = place.near * place.near_step + place.far * place.far_step
        self.there = (1 - place.near) * place.near_step + place.far * place.far_step
        self.beyond = [near * place.near_step + (1 - place.far) * place.far_step for near in (place.near, 1 - place.near)]

    def copy(self, slot):
        p, d = self.p, self.p.depth
        if slot < d - 1:
            view, peer = self.full.at[p.zed, self.here, :, self.cols], p.column_peers[slot + 1]
        elif slot < d + 1:
            view, peer = self.full.at[:, self.here, :, self.cols], (p.near_peer, p.far_peer)[slot - d + 1]
        elif slot == d + 1:
            view, peer = self.full.at[:, self.there, :, self.cols], p.far_peer
        else:
            at = (self.here, self.there, *self.beyond)[slot - d - 2]
            view, peer = self.full.at[:, at, :, self.cols], p.sibling
        return pltpu.make_async_remote_copy(
            src_ref=view, dst_ref=view, send_sem=self.send.at[slot], recv_sem=self.recv.at[slot],
            device_id=peer, device_id_type=MESH,
        )

    def own(self):
        for slot in range(self.p.depth - 1):
            self.copy(slot).start()

    def column(self):
        d = self.p.depth
        for slot in range(d - 1):
            self.copy(slot).wait_recv()
        for slot in (d - 1, d, d + 2):
            self.copy(slot).start()

    def plane(self):
        d = self.p.depth
        self.copy(d - 1).wait_recv()
        self.copy(d + 1).start()
        self.copy(d + 3).start()

    def rest(self):
        d = self.p.depth
        for slot in (d, d + 1):
            self.copy(slot).wait_recv()
            self.copy(slot + 4).start()

    def joined(self):
        for slot in range(self.p.depth + 2, self.p.depth + 6):
            self.copy(slot).wait_recv()

    def drained(self):
        for slot in range(self.p.depth + 6):
            self.copy(slot).wait_send()


def ticker(plan, step):
    def tick(point):
        for (when, where), events in plan.items():
            if where == point:
                @pl.when(step == when)
                def _():
                    for event in events:
                        event()

    return tick


class Direct:
    def kinds(shards):
        return [
            pltpu.VMEM((shards, 8, 128), F32), pltpu.VMEM((2 * shards, 8, 128), F32),
            pltpu.SemaphoreType.DMA((2 * shards,)), pltpu.SemaphoreType.DMA((2 * shards,)),
        ]

    def __init__(self, place, scratch):
        self.tiles, self.got, self.send, self.recv = scratch
        self.count = 2 * place.shards
        self.at = 2 * place.me + place.core
        self.me = place.me

    def greet(self):
        barrier = pltpu.get_barrier_semaphore()
        for k in range(1, self.count):
            other = lax.rem(self.at + k, self.count)
            pl.semaphore_signal(barrier, inc=1, device_id=(other // 2, lax.rem(other, 2)), device_id_type=MESH)
        pl.semaphore_wait(barrier, self.count - 1)

    def copy(self, k, slot):
        other = lax.rem(self.at + k, self.count)
        return pltpu.make_async_remote_copy(
            src_ref=self.tiles.at[other // 2], dst_ref=self.got.at[slot], send_sem=self.send.at[k],
            recv_sem=self.recv.at[slot], device_id=(other // 2, lax.rem(other, 2)), device_id_type=MESH,
        )

    def push(self):
        for k in range(1, self.count):
            self.copy(k, self.at).start()

    def sum(self):
        self.got[self.at] = self.tiles[self.me]
        for k in range(1, self.count):
            self.copy(k, lax.rem(self.at + k, self.count)).wait_recv()
        value = self.got[0]
        for i in range(1, self.count):
            value = value + self.got[i]
        for k in range(1, self.count):
            self.copy(k, self.at).wait_send()
        return value


class Largest:
    def __init__(self, place, own, out, got, kept, send, recv):
        self.p, self.own, self.out, self.got, self.kept, self.send, self.recv = place, own, out, got, kept, send, recv
        d = place.depth
        self.stages = [
            [(place.sibling, 0)], [(place.far_peer, 1)], [(place.near_peer, 2)],
            [(place.column_peers[k], 2 + k) for k in range(1, d)],
        ]

    def copies(self, stage):
        return [
            pltpu.make_async_remote_copy(
                src_ref=self.kept.at[stage], dst_ref=self.got.at[slot], send_sem=self.send.at[slot],
                recv_sem=self.recv.at[slot], device_id=peer, device_id_type=MESH,
            )
            for peer, slot in self.stages[stage]
        ]

    def push(self, stage):
        if stage == 0:
            self.kept[0] = self.own[...]
        for copy in self.copies(stage):
            copy.start()

    def take(self, stage):
        value = self.kept[stage]
        for copy, (_, slot) in zip(self.copies(stage), self.stages[stage]):
            copy.wait_recv()
            value = jnp.maximum(value, self.got[slot])
        if stage == 3:
            self.out[...] = value
            for done in range(4):
                for copy in self.copies(done):
                    copy.wait_send()
        else:
            self.kept[stage + 1] = value


class BlockSum:
    def kinds(full, dtype, sets=1):
        depth, _, rows, cols = full
        one = (rows, cols // 2)
        many = lambda *lead: pltpu.VMEM((sets,) + lead + one, dtype)
        return [
            many(depth, 4), many(2, depth), many(2, depth), many(depth), many(depth), many(depth - 1), many(depth - 1),
            pltpu.VMEM((sets,) + one, F32), pltpu.VMEM((sets,) + one, F32),
            pltpu.SemaphoreType.DMA((sets, 4 + depth)), pltpu.SemaphoreType.DMA((sets, 4 + depth)),
        ]

    def __init__(self, place, full, scratch, at=0):
        self.p, self.full = place, full
        (self.got_one, self.send_two, self.got_two, self.send_three, self.got_three, self.send_four, self.got_four,
         self.total, self.joined, self.send, self.recv) = (ref.at[at] for ref in scratch)
        self.dtype = scratch[0].dtype
        self.cols, self.others = half_of(full, place.core), half_of(full, 1 - place.core)

    def copy(self, slot):
        p = self.p
        if slot < 4:
            src, dst, peer = (
                (self.full.at[:, :, :, self.others], self.got_one, p.sibling),
                (self.send_two.at[0], self.got_two.at[0], p.far_peer),
                (self.send_two.at[1], self.got_two.at[1], p.far_peer),
                (self.send_three, self.got_three, p.near_peer),
            )[slot]
        elif slot < 3 + p.depth:
            src, dst, peer = self.send_four.at[slot - 4], self.got_four.at[slot - 4], p.column_peers[slot - 3]
        else:
            src, dst, peer = self.total, self.joined, p.sibling
        return pltpu.make_async_remote_copy(
            src_ref=src, dst_ref=dst, send_sem=self.send.at[slot], recv_sem=self.recv.at[slot],
            device_id=peer, device_id_type=MESH,
        )

    def pair(self, near, far):
        at = near * self.p.near_step + far * self.p.far_step
        return self.full[:, at, :, self.cols].astype(F32) + self.got_one[:, at].astype(F32)

    def first(self):
        self.copy(0).start()

    def second(self):
        p = self.p
        self.copy(0).wait_recv()
        for slot, near in ((1, 1 - p.near), (0, p.near)):
            at = near * p.near_step + (1 - p.far) * p.far_step
            self.send_two[slot] = self.full[:, at, :, self.cols] + self.got_one[:, at]
            self.copy(1 + slot).start()

    def third(self):
        p = self.p
        self.copy(2).wait_recv()
        self.send_three[...] = (self.pair(1 - p.near, p.far) + self.got_two[1].astype(F32)).astype(self.dtype)
        self.copy(3).start()

    def fourth(self):
        p = self.p
        self.copy(1).wait_recv()
        self.copy(3).wait_recv()
        self.copy(0).wait_send()
        at = p.near * p.near_step + p.far * p.far_step

        def value(z):
            return (
                self.full[z, at, :, self.cols].astype(F32) + self.got_one[z, at].astype(F32)
                + self.got_two[0, z].astype(F32) + self.got_three[z].astype(F32)
            )

        for i in range(p.depth - 1):
            self.send_four[i] = value(p.columns[i + 1]).astype(self.dtype)
            self.copy(4 + i).start()
        self.total[...] = value(p.zed)

    def fifth(self):
        p = self.p
        value = self.total[...]
        for i in range(p.depth - 1):
            self.copy(4 + i).wait_recv()
            value = value + self.got_four[i].astype(F32)
        self.total[...] = value
        self.copy(3 + p.depth).start()

    def finish(self, write):
        self.copy(3 + self.p.depth).wait_recv()
        write(self.p.core, self.total[...])
        write(1 - self.p.core, self.joined[...])
        for slot in range(1, 4 + self.p.depth):
            self.copy(slot).wait_send()


class OwnerSum(BlockSum):
    def kinds(full, dtype, depth, sets=1):
        _, _, rows, cols = full
        one = (rows, cols // 2)
        many = lambda *lead: pltpu.VMEM((sets,) + lead + one, dtype)
        return [
            many(1, 4), many(2, 1), many(2, 1), many(1), many(1), many(), pltpu.VMEM((depth - 1,) + one, dtype),
            pltpu.VMEM(one, F32), pltpu.VMEM(one, F32),
            pltpu.SemaphoreType.DMA((sets, 4 + depth)), pltpu.SemaphoreType.DMA((sets, 4 + depth)),
        ]

    def __init__(self, place, full, scratch, at, target):
        self.p, self.full = place, full
        self.got_one, self.send_two, self.got_two, self.send_three, self.got_three, self.send_four = (
            ref.at[at] for ref in scratch[:6]
        )
        self.got_four, self.total, self.joined = scratch[6:9]
        self.send, self.recv = (ref.at[at] for ref in scratch[9:])
        self.dtype = scratch[0].dtype
        self.cols, self.others = half_of(full, place.core), half_of(full, 1 - place.core)
        self.away = lax.rem(target - place.zed + place.depth, place.depth)
        self.target = target

    def line(self, away):
        p = self.p
        return pltpu.make_async_remote_copy(
            src_ref=self.send_four, dst_ref=self.got_four.at[away - 1], send_sem=self.send.at[3 + away],
            recv_sem=self.recv.at[3 + away], device_id=(p.block(self.target, p.near, p.far), p.core), device_id_type=MESH,
        )

    def fourth(self):
        p = self.p
        self.copy(1).wait_recv()
        self.copy(3).wait_recv()
        self.copy(0).wait_send()
        value = self.pair(p.near, p.far)[0] + self.got_two[0, 0].astype(F32) + self.got_three[0].astype(F32)

        @pl.when(self.away == 0)
        def _():
            self.total[...] = value

        @pl.when(self.away > 0)
        def _():
            self.send_four[...] = value.astype(self.dtype)
            self.line(self.away).start()

    def fifth(self):
        @pl.when(self.away == 0)
        def _():
            value = self.total[...]
            for away in range(1, self.p.depth):
                self.line(away).wait_recv()
                value = value + self.got_four[away - 1].astype(F32)
            self.total[...] = value
            self.copy(3 + self.p.depth).start()

    def finish(self, write):
        last = self.copy(3 + self.p.depth)

        @pl.when(self.away == 0)
        def _():
            last.wait_recv()
            write(self.p.core, self.total[...])
            write(1 - self.p.core, self.joined[...])
            last.wait_send()

        @pl.when(self.away > 0)
        def _():
            self.line(self.away).wait_send()

        for slot in range(1, 4):
            self.copy(slot).wait_send()


def writer(ref, rows, first, width):
    def write(core, value):
        ref[rows, pl.ds(pl.multiple_of(first + core * width, width), width)] = value

    return write


def middle_kernel(shards, tall, *refs):
    mid_hbm, dy_ref, own_ref, b0_hbm, w2_ref, vec_ref, hb_ref = refs[:7]
    act_hbm, mg_hbm, bl_hbm, cl_hbm, w2g_ref, w1g_ref, vg_ref, hbg_ref = refs[7:15]
    inp_ref, act_ref, grad_ref, two_ref, stage, w1_ref, fullb, fullc, local = refs[15:24]
    sems, sums = refs[24:26], refs[26:]
    j, p = pl.program_id(0), Place(shards)
    depth = p.depth
    chunk = w2_ref.shape[1] * 4
    rows_all = dy_ref.shape[0]
    turns = rows_all // tall
    gain, shift = vec_ref[5:6], vec_ref[6:7]
    root = math.sqrt(2.0 / math.pi)
    weights = [
        Gather(p, w1_ref, sems, k - 1, k * chunk, chunk) for k in range(1, depth)
    ]
    def blocks(k):
        return (
            OwnerSum(p, fullc.at[lax.rem(k, 2)], sums[11:], k, k),
            BlockSum(p, fullb.at[lax.rem(k, 2)], sums[:11], k),
        )

    def each(k, stage, *args):
        for job in blocks(k):
            getattr(job, stage)(*args)

    def rows_of(t):
        return pl.ds(pl.multiple_of(t * tall, tall), tall)

    def again(t):
        return pltpu.make_async_copy(mid_hbm.at[rows_of(t)], stage.at[t % 2], local.at[t])

    def results(t):
        return pltpu.make_async_copy(two_ref.at[rows_of(t)], mg_hbm.at[rows_of(t)], local.at[2 * turns + t])

    def first_chunk():
        return pltpu.make_async_copy(b0_hbm, w1_ref.at[:, :, :, pl.ds(0, chunk)], local.at[3 * turns])

    @pl.when(j == 0)
    def _():
        first_chunk().start()
        again(0).start()
        w1_ref[p.zed, lax.rem(p.me, 4), :, pl.ds(chunk, (depth - 1) * chunk)] = own_ref[:, pl.ds(chunk, (depth - 1) * chunk)]
        p.greet()
        for w in weights:
            w.own()
        for t in range(turns):
            if t + 1 < turns:
                again(t + 1).start()
            again(t).wait()
            rows = rows_of(t)
            unit, _ = normalise(stage[t % 2])
            inp_ref[rows, :] = (unit * gain + shift).astype(BF)
            two_ref[rows, :] = jnp.zeros((tall, two_ref.shape[1]), F32)
        first_chunk().wait()

    cols = pl.ds(pl.multiple_of(j * chunk, chunk), chunk)

    def chunk_rows(t, carry):
        rows = rows_of(t)
        w1 = w1_ref[:, :, :, cols].reshape(-1, chunk)
        w2 = w2_ref[...].reshape(chunk, -1)
        z = nn(inp_ref[rows, :], w1) + hb_ref[...]
        act_grad = nt(dy_ref[rows, :], w2)
        square = z * z
        bend = jnp.tanh(root * z * (1.0 + 0.044715 * square))
        half = 0.5 * (1.0 + bend)
        act = (z * half).astype(BF)
        slope = half + 0.5 * z * (1.0 - bend * bend) * (root * (1.0 + 0.134145 * square))
        grad = (act_grad * slope).astype(BF)
        act_ref[rows, :] = act
        grad_ref[rows, :] = grad
        two_ref[rows, :] += nt(grad, w1)
        hbg_ref[...] += column_sum(grad.astype(F32))

        first, later = weights[0], weights[1:]

        @pl.when(j == 0)
        def _():
            @pl.when(t == 0)
            def _():
                first.column()

            @pl.when(t == 1)
            def _():
                first.plane()
                for w in later:
                    w.column()

            pl.when(t == 2)(first.rest)

            @pl.when(t == 3)
            def _():
                for w in later:
                    w.plane()

        @pl.when((j == 1) & (t == 0))
        def _():
            for w in later:
                w.rest()

        @pl.when(j > 0)
        def _():
            pl.when(t == 0)(functools.partial(each, j - 1, "second"))
            pl.when(t == 3)(functools.partial(each, j - 1, "third"))

        return carry

    hbg_ref[...] = jnp.zeros_like(hbg_ref)
    lax.fori_loop(0, turns, chunk_rows, 0)
    store = pltpu.make_async_copy(act_ref, act_hbm.at[:, cols], local.at[turns])
    store.start()
    for k, w in enumerate(weights):
        pl.when(j == k)(w.joined)

    fullc[lax.rem(j, 2)] = tn(act_ref[...], dy_ref[...]).astype(BF).reshape(fullc.shape[1:])
    fullb[lax.rem(j, 2)] = tn(inp_ref[...], grad_ref[...]).astype(BF).reshape(fullb.shape[1:])

    store.wait()

    @pl.when(j < depth - 1)
    def _():
        each(j, "first")

    @pl.when(j > 1)
    def _():
        each(j - 2, "fifth")

    @pl.when(j > 0)
    def _():
        each(j - 1, "fourth")

    @pl.when(j == depth - 1)
    def _():
        lasts = (
            pltpu.make_async_copy(fullb.at[(depth - 1) % 2], bl_hbm, local.at[3 * turns]),
            pltpu.make_async_copy(fullc.at[(depth - 1) % 2], cl_hbm, local.at[3 * turns + 1]),
        )
        for copy in lasts:
            copy.start()
        w2g_ref[...] = jnp.zeros_like(w2g_ref)
        again(0).start()
        vg_ref[...] = jnp.zeros_like(vg_ref)
        for t in range(turns):
            rows = rows_of(t)
            if t + 1 < turns:
                again(t + 1).start()
            again(t).wait()
            unit, inverse = normalise(stage[t % 2])
            two, up = two_ref[rows, :], dy_ref[rows, :].astype(F32)
            vg_ref[5:6] += column_sum(two * unit)
            vg_ref[6:7] += column_sum(two)
            vg_ref[7:8] += column_sum(up)
            two_ref[rows, :] = up + norm_back(two, unit, inverse, gain)
            results(t).start()
        each(depth - 2, "fifth")
        for t in range(turns):
            results(t).wait()
        for copy in lasts:
            copy.wait()
        for w in weights:
            w.drained()
        for k in range(depth - 1):
            c, b = blocks(k)
            c.finish(writer(w2g_ref, slice(None), 0, w2g_ref.shape[1] // 2))
            b.finish(writer(w1g_ref, slice(None), k * chunk, chunk // 2))


def middle(shards, mid, dy, w1_own, b0, w2, vec, hb):
    rows, d = mid.shape
    depth = shards // 4
    hidden = w1_own.shape[1]
    chunk = hidden // depth
    tall = min(ROWS, rows)
    turns = rows // tall
    less = depth - 1
    anywhere = pl.BlockSpec(memory_space=pl.ANY)
    fullb = (depth, 4, w1_own.shape[0], chunk)
    w1g = (w1_own.shape[0], less * chunk)
    fullc = (1, 4) + w2.shape[1:]
    return pl.pallas_call(
        lambda *refs: middle_kernel(shards, tall, *refs),
        grid=(depth,),
        in_specs=[
            anywhere, whole(dy.shape), whole(w1_own.shape), anywhere,
            pl.BlockSpec((4,) + w2.shape[1:], lambda j: (j, 0, 0)), whole(vec.shape), pl.BlockSpec((1, chunk), lambda j: (0, j)),
        ],
        out_specs=[
            anywhere, anywhere, anywhere, anywhere, whole(w2.shape[1:]), whole(w1g), whole((8, d)),
            pl.BlockSpec((1, chunk), lambda j: (0, j)),
        ],
        out_shape=[
            shaped((rows, hidden), BF), shaped((rows, d), F32), shaped(fullb, BF), shaped(fullc, BF), shaped(w2.shape[1:], F32),
            shaped(w1g, F32),
            shaped((8, d), F32), shaped((1, hidden), F32),
        ],
        scratch_shapes=[
            pltpu.VMEM((rows, d), BF), pltpu.VMEM((rows, chunk), BF), pltpu.VMEM((rows, chunk), BF),
            pltpu.VMEM((rows, d), F32), pltpu.VMEM((2, tall, d), F32),
            pltpu.VMEM((depth, 4) + w1_own.shape, BF), pltpu.VMEM((2,) + fullb, BF),
            pltpu.VMEM((2,) + fullc, BF), pltpu.SemaphoreType.DMA((3 * turns + 2,)),
        ] + Gather.kinds(depth, less) + BlockSum.kinds(fullb, BF, less) + OwnerSum.kinds(fullc, BF, depth, less),
        compiler_params=pltpu.CompilerParams(
            dimension_semantics=("arbitrary",), collective_id=3, has_side_effects=True, vmem_limit_bytes=VMEM_LIMIT
        ),
        name="middle",
    )(mid, dy, w1_own, b0, w2, vec, hb)


def enter_kernel(shards, width, steps, *refs):
    tok_ref, wq, wk, wv, wo, w1, w2, small = refs[:8]
    attn_out, w1_out, w2_out, hb_out, vec_out = refs[8:13]
    results, top_out, one_out = refs[13:19], refs[19], refs[20]
    attn, tiles_in, tops, local = refs[21:25]
    sems = refs[25:27]
    hidden_rows = hb_out.shape[1] // shards
    step = pl.program_id(0)
    p = Place(shards)
    depth = p.depth
    rows = wq.shape[0]
    s, b, c, *early = (
        Gather(p, full, sems, i)
        for i, full in enumerate(
            [tiles_in, w1_out, w2_out] + [attn.at[:, :, i * rows : (i + 1) * rows] for i in range(4)]
        )
    )
    early.insert(0, s)

    def start():
        mine = p.zed, lax.rem(p.me, 4)
        copies = [
            pltpu.make_async_copy(w, out.at[mine], local.at[i])
            for i, (w, out) in enumerate(((w1, w1_out), (w2, w2_out)))
        ]
        for copy in copies:
            copy.start()
        attn[mine] = jnp.concatenate([w[...] for w in (wq, wk, wv, wo)], axis=0)
        tiles_in[mine] = small[...]
        for copy in copies:
            copy.wait()
        p.greet()
        for g in early + [b, c]:
            g.own()
        for g in early:
            g.column()
        for g in early:
            g.plane()
        b.column()
        for g in early:
            g.rest()
        b.plane()
        for g in early[:-1]:
            g.joined()
        vec = jnp.zeros(vec_out.shape, F32)
        blank = jnp.zeros((8, vec.shape[1] - 128), F32)
        for i in range(shards):
            piece = jnp.concatenate([tiles_in[i // 4, i % 4, :, :128], blank], axis=1)
            vec = vec + (pltpu.roll(piece, i * rows, 1) if i else piece)
        vec_out[...] = vec
        empty = jnp.zeros((8, 2 * hidden_rows - 256), F32)
        for i in range(0, shards, 2):
            even, odd = (
                jnp.concatenate([tiles_in[n // 4, n % 4, :, 256:], empty], axis=1) for n in (i, i + 1)
            )
            both = even + pltpu.roll(odd, hidden_rows, 1)
            hb_out[:, i * hidden_rows : (i + 2) * hidden_rows] = both[0:1]

    def keep():
        return pltpu.make_async_copy(attn, attn_out, local.at[2])

    def whole_attn():
        early[-1].joined()
        keep().start()

    def end():
        lane = lax.broadcasted_iota(jnp.int32, (8, 128), 1)
        tile = jnp.zeros((8, 128), F32)
        for pair in range(tops.shape[0]):
            best = jnp.max(tops[pair], axis=0, keepdims=True)
            for i in range(2):
                one = jnp.max(best[:, i * BLOCK : (i + 1) * BLOCK], axis=1, keepdims=True)
                tile = jnp.where(lane == 2 * pair + i, one, tile)
        top_out[...] = tile
        b.joined(), c.joined()
        for g in early + [b, c]:
            g.drained()
        keep().wait()

    pl.when(step == 0)(start)
    plan = {(0, 1): [whole_attn, c.column], (0, 2): [b.rest], (steps // 2 - 1, 3): [c.plane], (steps - 1, 2): [c.rest], (steps - 1, 3): [end]}
    view = [attn.at[:, :, i * rows : (i + 1) * rows, :] for i in range(4)]
    attend_kernel(width, tok_ref, view, vec_out, *results, tops, one_out, tick=ticker(plan, step))


def enter(shards, tokens, wq, wk, wv, wo, w1, w2, small, heads):
    rows, d = tokens.shape
    t = min(ROWS, rows)
    pairs = d // PAIR
    blocks = rows // BLOCK
    big = tiles(t, d)
    depth = shards // 4
    lead = (depth, 4)
    anywhere = pl.BlockSpec(memory_space=pl.ANY)
    packed = lead + (4 * wq.shape[0], d)
    full_small = lead + small.shape
    chunk = w1.shape[1] // depth
    return pl.pallas_call(
        lambda *refs: enter_kernel(shards, d // heads, rows // t, *refs),
        grid=(rows // t,),
        in_specs=[big] + [whole(w.shape) for w in (wq, wk, wv, wo)] + [whole((w1.shape[0], chunk))] + [whole(w.shape) for w in (w2, small)],
        out_specs=[
            anywhere, anywhere, anywhere, whole((1, w1.shape[1])), whole((8, d)), big, big, big,
            pl.BlockSpec((t // BLOCK, pairs, FRAMES, 2 * BLOCK), lambda i: (i, 0, 0, 0)),
            big, big,
            whole((8, 128)), big,
        ],
        out_shape=[
            shaped(packed, BF), shaped(lead + (w1.shape[0], chunk), BF), shaped(lead + w2.shape, BF),
            shaped((1, w1.shape[1]), F32), shaped((8, d), F32),
        ]
        + [shaped((rows, d), BF)] * 3
        + [shaped((blocks, pairs, FRAMES, 2 * BLOCK), F32), shaped((rows, d), BF), shaped((rows, d), F32)]
        + [shaped((8, 128), F32), shaped((rows, d), BF)],
        scratch_shapes=[
            pltpu.VMEM(packed, BF), pltpu.VMEM(full_small, F32), pltpu.VMEM((pairs, FRAMES, 2 * BLOCK), F32),
            pltpu.SemaphoreType.DMA((3,)),
        ] + Gather.kinds(depth, 7),
        compiler_params=pltpu.CompilerParams(
            dimension_semantics=("arbitrary",), collective_id=0, has_side_effects=True, vmem_limit_bytes=VMEM_LIMIT
        ),
        name="enter",
    )(tokens, wq, wk, wv, wo, w1, w2, small)


def leave_kernel(shards, width, steps, *refs):
    mg_ref, q_ref, k_ref, v_ref, p_ref, mix_ref, wo_ref, fullb, fullc, w1_in, w2_in = refs[:11]
    dq_ref, dk_ref, dv_ref, wog_ref, vg_ref, w1_out, w2_out = refs[11:18]
    acco, mgl_ref = refs[18:20]
    own = refs[20:]
    step, p = pl.program_id(0), Place(shards)
    b = BlockSum(p, fullb, own[:11])
    c = OwnerSum(p, fullc, own[11:22], 0, p.depth - 1)
    wide = fullb.shape[3]

    def others():
        w1_out[:, : (p.depth - 1) * wide] = w1_in[...]
        w2_out[...] = w2_in[...]

    def finish():
        c.finish(writer(w2_out, slice(None), 0, w2_out.shape[1] // 2))
        b.finish(writer(w1_out, slice(None), (p.depth - 1) * wide, wide // 2))

    events = [
        (0, p.greet), (0, c.first), (0, b.first), (1, others), (2, c.second), (2, b.second), (5, c.third), (5, b.third),
        (8, c.fourth), (8, b.fourth), (11, c.fifth), (11, b.fifth),
    ]
    points = [(when, where) for when in range(steps) for where in range(3)]
    plan = {}
    for at, event in events:
        plan.setdefault(points[at * len(points) // 12], []).append(event)
    tick = ticker(plan, step)

    @pl.when(step == 0)
    def _():
        acco[...] = jnp.zeros_like(acco)
        vg_ref[...] = jnp.zeros_like(vg_ref)

    tick(0)
    branch = mg_ref[...].astype(BF)
    mgl_ref[...] = nt(branch, square(wo_ref)).astype(BF)
    acco[...] += tn(mix_ref[...], branch)
    vg_ref[4:5] += column_sum(branch.astype(F32))
    tick(1)
    attention_back(width, mgl_ref, q_ref, k_ref, v_ref, p_ref, dq_ref, dk_ref, dv_ref)
    vg_ref[2:3] += column_sum(dq_ref[...].astype(F32))
    vg_ref[3:4] += column_sum(dv_ref[...].astype(F32))
    tick(2)

    @pl.when(step == steps - 1)
    def _():
        wog_ref[...] = acco[...].astype(BF).reshape(wog_ref.shape)
        finish()


def leave(shards, mg, q, k, v, p, mixed, attn, fullb, fullc, w1g, w2g, heads):
    rows, d = mg.shape
    t = min(ROWS, rows)
    pairs = d // PAIR
    big = tiles(t, d)
    w1_out, w2_out = (w1g.shape[0], shards // 4 * fullb.shape[3]), w2g.shape
    wog = (shards // 4, 4, attn.shape[1] // 4, d)
    return pl.pallas_call(
        lambda *refs: leave_kernel(shards, d // heads, rows // t, *refs),
        grid=(rows // t,),
        in_specs=[
            big, big, big, big,
            pl.BlockSpec((t // BLOCK, pairs, FRAMES, 2 * BLOCK), lambda i: (i, 0, 0, 0)),
            big, weight_specs((attn,))[3],
        ] + [whole(x.shape) for x in (fullb, fullc, w1g, w2g)],
        out_specs=[big, big, big, whole(wog), whole((8, d)), whole(w1_out), whole(w2_out)],
        out_shape=[shaped((rows, d), BF)] * 3
        + [shaped(wog, BF), shaped((8, d), F32), shaped(w1_out, F32), shaped(w2_out, F32)],
        scratch_shapes=[pltpu.VMEM((d, d), F32), pltpu.VMEM((t, d), BF)]
        + BlockSum.kinds(fullb.shape, BF) + OwnerSum.kinds(fullc.shape, BF, shards // 4),
        compiler_params=pltpu.CompilerParams(
            dimension_semantics=("arbitrary",), collective_id=1, has_side_effects=True, vmem_limit_bytes=VMEM_LIMIT
        ),
        name="leave",
    )(mg, q, k, v, p, mixed, attn, fullb, fullc, w1g, w2g)


def last_kernel(shards, steps, *refs):
    tok_ref, mg_ref, dq_hbm, dk_hbm, dv_hbm, one_hbm, wq, wk, wv, vec_ref, wog_ref, vga_ref, vgb_ref, hbg_ref, top_ref, mid_ref, act_ref, w2_hbm = refs[:18]
    gt_ref, lo_ref, attn_out, small_out, top_out = refs[18:23]
    d_ref, one_ref, full, tile, vg, w2_ref, local = refs[23:30]
    jobs, little, most, straight = refs[30:41], refs[41:52], refs[52:56], refs[56:]
    hidden_rows = hbg_ref.shape[1] // shards
    turns = (steps - 3) // 2
    step, p = pl.program_id(0), Place(shards)
    rows = wog_ref.shape[2]
    d = vg.shape[1]
    wide = attn_out.shape[1] // 2
    o = BlockSum(p, wog_ref, jobs, 3)
    s = BlockSum(p, tile, little)
    t = Largest(p, top_ref, top_out, *most)
    late = Direct(p, straight)
    weight = lambda i: BlockSum(p, full.at[i], jobs, i)
    q, k, v = weight(0), weight(1), weight(2)
    many = functools.partial
    events = [
        (1, o.second), (1, s.second), (2, q.second), (3, many(t.take, 0)), (3, many(t.push, 1)), (3, s.third), (4, o.third),
        (5, k.second), (5, many(t.take, 1)), (5, many(t.push, 2)), (5, s.fourth), (7, v.second), (7, q.third),
        (8, o.fourth), (9, many(t.take, 2)), (9, many(t.push, 3)), (9, s.fifth), (9, k.third), (11, q.fourth),
        (11, v.third), (13, o.fifth), (13, k.fourth), (13, many(t.take, 3)), (15, v.fourth), (15, q.fifth), (18, k.fifth),
        (20, v.fifth),
    ]
    plan = {}
    for at, event in events:
        at = min(at, 2 * steps - 1)
        plan.setdefault((at // 2, at % 2), []).append(event)
    tick = ticker(plan, step)
    fetches = [
        pltpu.make_async_copy(src, dst, local.at[i])
        for i, (src, dst) in enumerate(
            ((dq_hbm, d_ref.at[0]), (dk_hbm, d_ref.at[1]), (dv_hbm, d_ref.at[2]), (one_hbm, one_ref), (w2_hbm, w2_ref))
        )
    ]

    def spread(value, put):
        for i in range(shards):
            put(i, (pltpu.roll(value, d - i * rows, 1) if i else value)[:, :128])

    @pl.when(step == 0)
    def _():
        for i in (3, 0, 1, 2, 4):
            fetches[i].start()
        vg[...] = jnp.zeros_like(vg)

        def put(i, piece):
            tile[i // 4, i % 4, :, :128] = piece

        spread(vga_ref[...] + vgb_ref[...], put)
        tile[:, :, :, 128:256] = jnp.zeros(tile.shape[:3] + (128,), F32)
        for i in range(0, shards, 2):
            both = jnp.broadcast_to(
                hbg_ref[:, i * hidden_rows : (i + 2) * hidden_rows], (8, 2 * hidden_rows)
            )
            tile[i // 4, i % 4, :, 256:] = both[:, :256]
            tile[i // 4, i % 4 + 1, :, 256:] = pltpu.roll(both, hidden_rows, 1)[:, :256]
        late.greet()
        o.first(), s.first(), t.push(0)
        fetches[3].wait()

    tick(0)

    for i in range(3):
        pl.when(step == i)(fetches[i].wait)

    @pl.when(step < 3)
    def _():
        full[step] = tn(one_ref[...], d_ref[step]).astype(BF).reshape(full.shape[1:])
        weight(step).first()

    pl.when(step == 3 + turns)(fetches[4].wait)

    @pl.when(step >= 3 + turns)
    def _():
        w2 = square(w2_ref)
        lo_ref[...] = (mid_ref[...] + (nn(act_ref[...], w2) + vec_ref[7:8])).astype(BF)

    @pl.when((step >= 3) & (step < 3 + turns))
    def _():
        tall = tok_ref.shape[0]
        at = pl.ds(pl.multiple_of((step - 3) * tall, tall), tall)
        unit, inverse = normalise(tok_ref[...].astype(F32))
        grad = nt(d_ref[0, at], square(wq)) + nt(d_ref[1, at], square(wk)) + nt(d_ref[2, at], square(wv))
        vg[0:1] += column_sum(grad * unit)
        vg[1:2] += column_sum(grad)
        gt_ref[...] = (mg_ref[...] + norm_back(grad, unit, inverse, vec_ref[0:1])).astype(BF)

    @pl.when(step == 2 + turns)
    def _():
        def put(i, piece):
            late.tiles[i] = piece

        spread(vg[...], put)
        late.push()

    tick(1)

    @pl.when(step == steps - 1)
    def _():
        s.finish(writer(small_out, slice(None), 0, small_out.shape[1] // 2))
        small_out[0:2, :128] = late.sum()[0:2]
        for i, job in ((3, o), (0, q), (1, k), (2, v)):
            job.finish(writer(attn_out, slice(i * rows, (i + 1) * rows), 0, wide))


def last(shards, tokens, mg, dq, dk, dv, one, attn, vec, wog, vga, vgb, hbg, top, mid, act, w2):
    rows, d = tokens.shape
    t = min(ROWS, rows)
    depth = shards // 4
    turns = rows // t
    steps = 3 + 2 * turns
    later = pl.BlockSpec((t, d), lambda i: (jnp.clip(i - 3, 0, turns - 1), 0))
    latest = lambda width: pl.BlockSpec((t, width), lambda i: (jnp.maximum(i - 3 - turns, 0), 0))
    anywhere = pl.BlockSpec(memory_space=pl.ANY)
    small = (depth, 4, 8, 512)
    return pl.pallas_call(
        lambda *refs: last_kernel(shards, steps, *refs),
        grid=(steps,),
        in_specs=[later, later] + [anywhere] * 4 + weight_specs((attn,))[:3]
        + [whole(x.shape) for x in (vec, wog, vga, vgb, hbg, top)] + [latest(d), latest(act.shape[1]), anywhere],
        out_specs=[later, latest(d), whole((4 * wog.shape[2], d)), whole((8, 512)), whole((8, 128))],
        out_shape=[
            shaped((rows, d), BF), shaped((rows, d), BF), shaped((4 * wog.shape[2], d), F32), shaped((8, 512), F32), shaped((8, 128), F32),
        ],
        scratch_shapes=[
            pltpu.VMEM((3, rows, d), BF), pltpu.VMEM((rows, d), BF), pltpu.VMEM((3,) + wog.shape, BF),
            pltpu.VMEM(small, F32), pltpu.VMEM((8, d), F32), pltpu.VMEM(w2.shape, BF), pltpu.SemaphoreType.DMA((5,)),
        ] + BlockSum.kinds(wog.shape, BF, 4) + BlockSum.kinds(small, F32) + [
            pltpu.VMEM((depth + 2, 8, 128), F32), pltpu.VMEM((4, 8, 128), F32),
            pltpu.SemaphoreType.DMA((depth + 2,)), pltpu.SemaphoreType.DMA((depth + 2,)),
        ] + Direct.kinds(shards),
        compiler_params=pltpu.CompilerParams(
            dimension_semantics=("arbitrary",), collective_id=2, has_side_effects=True, vmem_limit_bytes=VMEM_LIMIT
        ),
        name="last",
    )(tokens, mg, dq, dk, dv, one, attn, attn, attn, vec, wog, vga, vgb, hbg, top, mid, act, w2)


def on_device(shards, reps, *args):
    (
        tokens, grad_out, first_gain, first_shift, query_proj, query_bias, key_proj, value_proj, value_bias,
        output_proj, output_bias, second_gain, second_shift, hidden_proj, hidden_bias, final_proj, final_bias, threshold,
    ) = args
    heads = threshold.shape[0]
    d = tokens.shape[1]
    hidden = hidden_proj.shape[1]
    head_dim = d // heads
    small = (first_gain, first_shift, query_bias, value_bias, output_bias, second_gain, second_shift, final_bias)
    rows, more = small[0].shape[0], hidden_bias.shape[0]
    whole_chunks = shards % 4 == 0 and hidden * 4 % (shards * 256) == 0 and hidden * 4 // shards == 4 * final_proj.shape[0]
    own = whole_chunks and reps == 2 and shards % 4 == 0 and shards > 4 and rows % 16 == 0 and rows <= 128 and more <= 256 and more % 64 == 0 and more > 128

    def gather(x):
        return lax.all_gather(x, "shard", axis=0, tiled=True)

    def scatter(x):
        y = lax.psum_scatter(x.astype(BF), "shard", scatter_dimension=0, tiled=True)
        return lax.psum(y, "rep").astype(F32)

    if own:
        tile = jnp.concatenate(
            [
                jnp.pad(jnp.stack(small).astype(F32), ((0, 0), (0, 256 - rows))),
                jnp.pad(hidden_bias.astype(F32)[None], ((0, 7), (0, 256 - more))),
            ],
            axis=1,
        )
        attn, w1, w2, hb, vec, q, k, v, p, mixed, mid, top, one = enter(
            shards, tokens, query_proj, key_proj, value_proj, output_proj, hidden_proj, final_proj, tile, heads
        )
        attn, w2 = attn.reshape(shards, -1, d), w2.reshape(shards, -1, d)
    else:
        weights = tuple(gather(x) for x in (query_proj, key_proj, value_proj, output_proj))
        w1, w2 = gather(hidden_proj), gather(final_proj)
        vec = jnp.stack([gather(x) for x in small]).astype(F32)
        hb = gather(hidden_bias).astype(F32)[None]
        q, k, v, p, mixed, mid, top = attend(tokens, weights, vec, heads)
    if own:
        act, mg, b3g, c3g, w2g, w1g, vg2, hbg = middle(shards, mid, grad_out, hidden_proj, w1, w2, vec, hb)
        dq, dk, dv, wog, vg1, w1g, w2g = leave(
            shards, mg, q, k, v, p, mixed, attn, b3g, c3g, w1g, w2g, heads
        )
        grad_tokens, layer_output, attn, tile, top = last(
            shards, tokens, mg, dq, dk, dv, one, attn, vec, wog, vg1, vg2, hbg, top, mid, act, w2
        )
    else:
        layer_output, mg, w1g, w2g, vg2, hbg = mlp(mid, grad_out, w1, w2, vec, hb)
        grad_tokens, wg, vg1 = back(tokens, mg, q, k, v, p, mixed, weights, vec, heads)
    if own:
        wg = tuple(attn[i * rows : (i + 1) * rows] for i in range(4))
        vg = tuple(tile[i, :rows] for i in range(8))
        hbg = tile[0, 256 : 256 + more]
        global_max = top[0, :heads]
    else:
        vg = jnp.concatenate([vg1[:5], vg2[:3]])
        local = jnp.max(top.reshape(top.shape[0], FRAMES, 2, BLOCK), axis=(1, 3)).reshape(heads)
        global_max = lax.pmax(local, ("shard", "rep"))
        wg = tuple(scatter(x) for x in wg)
        w1g, w2g = scatter(w1g), scatter(w2g)
        vg = tuple(scatter(vg[i]) for i in range(8))
        hbg = scatter(hbg[0])
    factor = jnp.minimum(1.0, threshold / global_max)
    column_scale = jnp.repeat(jnp.sqrt(factor), head_dim)
    bias_scale = lax.dynamic_slice_in_dim(column_scale, lax.axis_index("shard") * rows, rows)
    return (
        layer_output, grad_tokens, vg[0], vg[1], wg[0], vg[2], wg[1], wg[2], vg[3], wg[3], vg[4], vg[5], vg[6],
        w1g, hbg, w2g, vg[7], global_max, factor,
        query_proj.astype(F32) * column_scale[None, :], query_bias.astype(F32) * bias_scale,
        key_proj.astype(F32) * column_scale[None, :],
    )


def solution(mesh):
    in_specs = (
        P(("shard", "rep"), None),
        P(("shard", "rep"), None),
        P("shard"),
        P("shard"),
        P("shard", None),
        P("shard"),
        P("shard", None),
        P("shard", None),
        P("shard"),
        P("shard", None),
        P("shard"),
        P("shard"),
        P("shard"),
        P("shard", None),
        P("shard"),
        P("shard", None),
        P("shard"),
        P(),
    )
    out_specs = (
        P(("shard", "rep"), None),
        P(("shard", "rep"), None),
        P("shard"),
        P("shard"),
        P("shard", None),
        P("shard"),
        P("shard", None),
        P("shard", None),
        P("shard"),
        P("shard", None),
        P("shard"),
        P("shard"),
        P("shard"),
        P("shard", None),
        P("shard"),
        P("shard", None),
        P("shard"),
        P(),
        P(),
        P("shard", None),
        P("shard"),
        P("shard", None),
    )
    shards, reps = mesh.shape["shard"], mesh.shape["rep"]
    return jax.shard_map(
        functools.partial(on_device, shards, reps), mesh=mesh, in_specs=in_specs, out_specs=out_specs, check_vma=False
    )
```

```python
import functools
import math

import jax
import jax.numpy as jnp
from jax import lax
from jax.experimental import pallas as pl
from jax.experimental.pallas import tpu as pltpu
from jax.sharding import PartitionSpec as P

FRAMES = 16
EPSILON = 1e-06
BF = jnp.bfloat16
F32 = jnp.float32
ROWS = 512
BLOCK = 128
PAIR = 128


def nn(left, right):
    return lax.dot_general(left, right, (((1,), (0,)), ((), ())), preferred_element_type=F32)


def nt(left, right):
    return lax.dot_general(left, right, (((1,), (1,)), ((), ())), preferred_element_type=F32)


def tn(left, right):
    return lax.dot_general(left, right, (((0,), (0,)), ((), ())), preferred_element_type=F32)


def normalise(values):
    centred = values - jnp.mean(values, axis=-1, keepdims=True)
    inverse = lax.rsqrt(jnp.mean(centred * centred, axis=-1, keepdims=True) + EPSILON)
    return centred * inverse, inverse


def norm_back(grad, unit, inverse, gain):
    scaled = grad * gain
    return inverse * (
        scaled
        - jnp.mean(scaled, axis=-1, keepdims=True)
        - unit * jnp.mean(scaled * unit, axis=-1, keepdims=True)
    )


def column_sum(values):
    return jnp.sum(values, axis=0, keepdims=True)


def place_masks():
    lane = lax.broadcasted_iota(jnp.int32, (FRAMES, 2 * BLOCK), 1)
    return [(lane % BLOCK) // FRAMES == p for p in range(BLOCK // FRAMES)]


def halves(width):
    lane = lax.broadcasted_iota(jnp.int32, (1, PAIR), 1)
    first = (lane < width).astype(F32)
    return first.astype(BF), (1.0 - first).astype(BF)


def compress(wide, masks):
    total = wide[:FRAMES]
    for p in range(1, len(masks)):
        total = jnp.where(masks[p], wide[p * FRAMES : (p + 1) * FRAMES], total)
    return total


def expand(packed, masks):
    zero = jnp.zeros_like(packed)
    return jnp.concatenate([jnp.where(m, packed, zero).astype(BF) for m in masks], axis=0)


def split(two, first, second):
    return jnp.concatenate([two * first, two * second], axis=0)


def stack(wide):
    return jnp.concatenate([wide[:, :BLOCK], wide[:, BLOCK:]], axis=0)


def square(ref):
    value = ref[...]
    return value.reshape(-1, value.shape[-1])


def attend_kernel(
    width, tok_ref, w_refs, vec_ref,
    q_ref, k_ref, v_ref, p_ref, mix_ref, mid_ref, top_ref, one_ref=None, tick=lambda point: None,
):
    scale = 1.0 / math.sqrt(width)
    wq, wk, wv = (square(w) for w in w_refs[:3])
    gain, shift = vec_ref[0:1], vec_ref[1:2]
    tok = tok_ref[...].astype(F32)
    unit, _ = normalise(tok)
    one = (unit * gain + shift).astype(BF)
    if one_ref is not None:
        one_ref[...] = one
    q_ref[...] = (nn(one, wq) + vec_ref[2:3]).astype(BF)
    k_ref[...] = nn(one, wk).astype(BF)
    v_ref[...] = (nn(one, wv) + vec_ref[3:4]).astype(BF)
    tick(1)
    masks = place_masks()
    first, second = halves(width)
    pairs = tok_ref.shape[1] // PAIR

    @pl.when(pl.program_id(0) == 0)
    def _():
        top_ref[...] = jnp.full(top_ref.shape, -3e38, F32)

    def body(i, carry):
        rows = pl.ds(pl.multiple_of(i * BLOCK, BLOCK), BLOCK)
        for h in range(pairs):
            cols = slice(h * PAIR, (h + 1) * PAIR)
            two_q, two_k, two_v = q_ref[rows, cols], k_ref[rows, cols], v_ref[rows, cols]
            scores = compress(nt(two_k, split(two_q, first, second)), masks) * scale
            top_ref[h] = jnp.maximum(top_ref[h], scores)
            expo = jnp.exp(scores - jnp.max(scores, axis=0, keepdims=True))
            probs = expo / jnp.sum(expo, axis=0, keepdims=True)
            p_ref[i, h] = probs
            mixed = tn(stack(expand(probs, masks)), split(two_v, first, second))
            mix_ref[rows, cols] = mixed.astype(BF)
        return carry

    lax.fori_loop(0, tok_ref.shape[0] // BLOCK, body, 0, unroll=2)
    tick(2)
    mid_ref[...] = tok_ref[...].astype(F32) + (nn(mix_ref[...], square(w_refs[3])) + vec_ref[4:5])
    tick(3)


def mlp_kernel(
    chunk, mid_ref, dy_ref, w1_ref, w2_ref, vec_ref, hb_ref,
    out_ref, mg_ref, w1g_ref, w2g_ref, vg_ref, hbg_ref,
    acc1, acc2, res_ref, two_ref,
):
    step, last = pl.program_id(0), pl.num_programs(0) - 1
    gain, shift = vec_ref[5:6], vec_ref[6:7]
    mid = mid_ref[...]
    unit, inverse = normalise(mid)
    inp = (unit * gain + shift).astype(BF)
    dy = dy_ref[...]
    hidden = w1_ref.shape[1]

    @pl.when(step == 0)
    def _():
        acc1[...] = jnp.zeros_like(acc1)
        acc2[...] = jnp.zeros_like(acc2)
        vg_ref[...] = jnp.zeros_like(vg_ref)
        hbg_ref[...] = jnp.zeros_like(hbg_ref)

    res_ref[...] = mid + vec_ref[7:8]
    two_ref[...] = jnp.zeros_like(two_ref)
    root = math.sqrt(2.0 / math.pi)

    def body(j, carry):
        cols = pl.ds(pl.multiple_of(j * chunk, chunk), chunk)
        z = nn(inp, w1_ref[:, cols]) + hb_ref[:, cols]
        act_grad = nt(dy, w2_ref[cols, :])
        square = z * z
        bend = jnp.tanh(root * z * (1.0 + 0.044715 * square))
        half = 0.5 * (1.0 + bend)
        act = (z * half).astype(BF)
        slope = half + 0.5 * z * (1.0 - bend * bend) * (root * (1.0 + 0.134145 * square))
        grad = (act_grad * slope).astype(BF)
        res_ref[...] += nn(act, w2_ref[cols, :])
        two_ref[...] += nt(grad, w1_ref[:, cols])
        acc2[cols, :] += tn(act, dy)
        acc1[:, cols] += tn(inp, grad)
        hbg_ref[:, cols] += column_sum(grad.astype(F32))
        return carry

    lax.fori_loop(0, hidden // chunk, body, 0)
    out_ref[...] = res_ref[...].astype(BF)
    two = two_ref[...]
    up = dy.astype(F32)
    mg_ref[...] = up + norm_back(two, unit, inverse, gain)
    vg_ref[0:1] += column_sum(two * unit)
    vg_ref[1:2] += column_sum(two)
    vg_ref[2:3] += column_sum(up)

    @pl.when(step == last)
    def _():
        w1g_ref[...] = acc1[...].astype(BF)
        w2g_ref[...] = acc2[...].astype(BF)


def attention_back(width, mgl_ref, q_ref, k_ref, v_ref, p_ref, dq_ref, dk_ref, dv_ref):
    scale = 1.0 / math.sqrt(width)
    masks = place_masks()
    first, second = halves(width)
    pairs = q_ref.shape[1] // PAIR

    def body(i, carry):
        rows = pl.ds(pl.multiple_of(i * BLOCK, BLOCK), BLOCK)
        for h in range(pairs):
            cols = slice(h * PAIR, (h + 1) * PAIR)
            two_q, two_k, two_v = q_ref[rows, cols], k_ref[rows, cols], v_ref[rows, cols]
            mixed = split(mgl_ref[rows, cols], first, second)
            probs = p_ref[i, h]
            slope = compress(nt(two_v, mixed), masks)
            score = probs * (slope - jnp.sum(slope * probs, axis=0, keepdims=True))
            wide = expand(score, masks)
            dv_ref[rows, cols] = nn(expand(probs, masks), mixed).astype(BF)
            dk_ref[rows, cols] = (nn(wide, split(two_q, first, second)) * scale).astype(BF)
            dq_ref[rows, cols] = (tn(stack(wide), split(two_k, first, second)) * scale).astype(BF)
        return carry

    lax.fori_loop(0, q_ref.shape[0] // BLOCK, body, 0, unroll=4)


def back_kernel(
    width, tok_ref, mg_ref, q_ref, k_ref, v_ref, p_ref, mix_ref,
    w_refs, vec_ref,
    gt_ref, wg_refs, vg_ref,
    accq, acck, accv, acco, mgl_ref, dq_ref, dk_ref, dv_ref,
):
    step, last = pl.program_id(0), pl.num_programs(0) - 1
    gain, shift = vec_ref[0:1], vec_ref[1:2]
    accs = (accq, acck, accv, acco)
    wq, wk, wv, wo = (square(w) for w in w_refs)

    @pl.when(step == 0)
    def _():
        for acc in accs:
            acc[...] = jnp.zeros_like(acc)
        vg_ref[...] = jnp.zeros_like(vg_ref)

    branch = mg_ref[...].astype(BF)
    mgl_ref[...] = nt(branch, wo).astype(BF)
    acco[...] += tn(mix_ref[...], branch)
    vg_ref[4:5] += column_sum(branch.astype(F32))
    attention_back(width, mgl_ref, q_ref, k_ref, v_ref, p_ref, dq_ref, dk_ref, dv_ref)
    unit, inverse = normalise(tok_ref[...].astype(F32))
    one = (unit * gain + shift).astype(BF)
    dq, dk, dv = dq_ref[...], dk_ref[...], dv_ref[...]
    vg_ref[2:3] += column_sum(dq.astype(F32))
    vg_ref[3:4] += column_sum(dv.astype(F32))
    accq[...] += tn(one, dq)
    acck[...] += tn(one, dk)
    accv[...] += tn(one, dv)
    grad = nt(dq, wq) + nt(dk, wk) + nt(dv, wv)
    vg_ref[0:1] += column_sum(grad * unit)
    vg_ref[1:2] += column_sum(grad)
    gt_ref[...] = (mg_ref[...] + norm_back(grad, unit, inverse, gain)).astype(BF)

    @pl.when(step == last)
    def _():
        for i, acc in enumerate(accs):
            value = acc[...].astype(BF)
            if len(wg_refs) == 1:
                rows = wg_refs[0].shape[1] // 4
                wg_refs[0][:, i * rows : (i + 1) * rows, :] = value.reshape(-1, rows, value.shape[1])
            else:
                wg_refs[i][...] = value


def whole(shape):
    return pl.BlockSpec(shape, lambda i: (0,) * len(shape), pipeline_mode=pl.Buffered(1))


def tiles(height, width):
    return pl.BlockSpec((height, width), lambda i: (i, 0))


def shaped(shape, dtype):
    return jax.ShapeDtypeStruct(shape, dtype)


VMEM_LIMIT = 60 * 1024 * 1024


def params():
    return pltpu.CompilerParams(
        dimension_semantics=("arbitrary",), vmem_limit_bytes=VMEM_LIMIT
    )


def weight_specs(weights):
    if len(weights) == 1:
        shards, rows, d = weights[0].shape
        return [
            pl.BlockSpec((shards, rows // 4, d), lambda i, j=j: (0, j, 0), pipeline_mode=pl.Buffered(1))
            for j in range(4)
        ]
    return [whole(w.shape) for w in weights]


def four(weights):
    return tuple(weights) * (4 // len(weights))


def attend(tokens, weights, vec, heads):
    rows, d = tokens.shape
    t = min(ROWS, rows)
    pairs = d // PAIR
    blocks = rows // BLOCK
    big = tiles(t, d)
    return pl.pallas_call(
        lambda tok, wq, wk, wv, wo, *refs: attend_kernel(d // heads, tok, (wq, wk, wv, wo), *refs),
        grid=(rows // t,),
        in_specs=[big] + weight_specs(weights) + [whole(vec.shape)],
        out_specs=[
            big, big, big,
            pl.BlockSpec((t // BLOCK, pairs, FRAMES, 2 * BLOCK), lambda i: (i, 0, 0, 0)),
            big, big,
            whole((pairs, FRAMES, 2 * BLOCK)),
        ],
        out_shape=[shaped((rows, d), BF)] * 3
        + [shaped((blocks, pairs, FRAMES, 2 * BLOCK), F32), shaped((rows, d), BF), shaped((rows, d), F32)]
        + [shaped((pairs, FRAMES, 2 * BLOCK), F32)],
        compiler_params=params(),
        cost_estimate=pl.CostEstimate(flops=10 * rows * d * d, bytes_accessed=24 * rows * d, transcendentals=0),
        name="attend",
    )(tokens, *four(weights), vec)


def mlp(middle, dy, w1, w2, vec, hb):
    rows, d = middle.shape
    hidden = w1.shape[1]
    t = min(ROWS, rows)
    big = tiles(t, d)
    return pl.pallas_call(
        lambda *refs: mlp_kernel(768, *refs),
        grid=(rows // t,),
        in_specs=[big, big, whole(w1.shape), whole(w2.shape), whole(vec.shape), whole(hb.shape)],
        out_specs=[big, big, whole(w1.shape), whole(w2.shape), whole((8, d)), whole((1, hidden))],
        out_shape=[
            shaped((rows, d), BF), shaped((rows, d), F32), shaped(w1.shape, BF), shaped(w2.shape, BF),
            shaped((8, d), F32), shaped((1, hidden), F32),
        ],
        scratch_shapes=[
            pltpu.VMEM(w1.shape, F32), pltpu.VMEM(w2.shape, F32), pltpu.VMEM((t, d), F32), pltpu.VMEM((t, d), F32),
        ],
        compiler_params=params(),
        cost_estimate=pl.CostEstimate(flops=12 * rows * d * hidden, bytes_accessed=14 * rows * d, transcendentals=0),
        name="mlp",
    )(middle, dy, w1, w2, vec, hb)


def back(tokens, mg, q, k, v, p, mixed, weights, vec, heads):
    rows, d = tokens.shape
    t = min(ROWS, rows)
    pairs = d // PAIR
    big = tiles(t, d)
    count = len(weights)

    def kernel(*refs):
        ins, w_refs, vec_ref, gt_ref = refs[:7], refs[7:11], refs[11], refs[12]
        wg_refs, rest = refs[13 : 13 + count], refs[13 + count :]
        back_kernel(d // heads, *ins, w_refs, vec_ref, gt_ref, wg_refs, *rest)

    out = pl.pallas_call(
        kernel,
        grid=(rows // t,),
        in_specs=[
            big, big, big, big, big,
            pl.BlockSpec((t // BLOCK, pairs, FRAMES, 2 * BLOCK), lambda i: (i, 0, 0, 0)),
            big,
        ] + weight_specs(weights) + [whole(vec.shape)],
        out_specs=[big] + [whole(w.shape) for w in weights] + [whole((8, d))],
        out_shape=[shaped((rows, d), BF)] + [shaped(w.shape, BF) for w in weights] + [shaped((8, d), F32)],
        scratch_shapes=[pltpu.VMEM((d, d), F32)] * 4 + [pltpu.VMEM((t, d), BF)] * 4,
        compiler_params=params(),
        cost_estimate=pl.CostEstimate(flops=20 * rows * d * d, bytes_accessed=24 * rows * d, transcendentals=0),
        name="back",
    )(tokens, mg, q, k, v, p, mixed, *four(weights), vec)
    return out[0], out[1 : 1 + count], out[1 + count]


MESH = pl.DeviceIdType.MESH


class Place:
    def __init__(self, shards):
        self.shards = shards
        self.depth = shards // 4
        self.me = lax.axis_index("shard")
        self.core = lax.axis_index("rep")
        self.zed = self.me // 4
        x, y = self.me % 2, (self.me // 2) % 2
        self.near_step, self.far_step = 1 + self.core, 2 - self.core
        self.near = x + self.core * (y - x)
        self.far = y + self.core * (x - y)
        self.sibling = (self.me, 1 - self.core)
        self.near_peer = (self.block(self.zed, 1 - self.near, self.far), self.core)
        self.far_peer = (self.block(self.zed, self.near, 1 - self.far), self.core)
        self.columns = [lax.rem(self.zed + k, self.depth) for k in range(self.depth)]
        self.column_peers = [(self.block(z, self.near, self.far), self.core) for z in self.columns]

    def block(self, zed, near, far):
        return zed * 4 + near * self.near_step + far * self.far_step

    def greet(self):
        barrier = pltpu.get_barrier_semaphore()
        peers = [self.sibling, self.near_peer, self.far_peer] + self.column_peers[1:]
        for peer in peers:
            pl.semaphore_signal(barrier, inc=1, device_id=peer, device_id_type=MESH)
        pl.semaphore_wait(barrier, len(peers))


def half_of(ref, core):
    width = ref.shape[-1] // 2
    return pl.ds(pl.multiple_of(core * width, width), width)


class Gather:
    def kinds(depth, count):
        return [pltpu.SemaphoreType.DMA((count, depth + 6)), pltpu.SemaphoreType.DMA((count, depth + 6))]

    def __init__(self, place, full, sems, at, first=0, width=None):
        self.p, self.full = place, full
        self.send, self.recv = (sem.at[at] for sem in sems)
        half = (width or full.shape[-1]) // 2
        self.cols = pl.ds(pl.multiple_of(first + place.core * half, half), half)
        self.here = place.near * place.near_step + place.far * place.far_step
        self.there = (1 - place.near) * place.near_step + place.far * place.far_step
        self.beyond = [near * place.near_step + (1 - place.far) * place.far_step for near in (place.near, 1 - place.near)]

    def copy(self, slot):
        p, d = self.p, self.p.depth
        if slot < d - 1:
            view, peer = self.full.at[p.zed, self.here, :, self.cols], p.column_peers[slot + 1]
        elif slot < d + 1:
            view, peer = self.full.at[:, self.here, :, self.cols], (p.near_peer, p.far_peer)[slot - d + 1]
        elif slot == d + 1:
            view, peer = self.full.at[:, self.there, :, self.cols], p.far_peer
        else:
            at = (self.here, self.there, *self.beyond)[slot - d - 2]
            view, peer = self.full.at[:, at, :, self.cols], p.sibling
        return pltpu.make_async_remote_copy(
            src_ref=view, dst_ref=view, send_sem=self.send.at[slot], recv_sem=self.recv.at[slot],
            device_id=peer, device_id_type=MESH,
        )

    def own(self):
        for slot in range(self.p.depth - 1):
            self.copy(slot).start()

    def column(self):
        d = self.p.depth
        for slot in range(d - 1):
            self.copy(slot).wait_recv()
        for slot in (d - 1, d, d + 2):
            self.copy(slot).start()

    def plane(self):
        d = self.p.depth
        self.copy(d - 1).wait_recv()
        self.copy(d + 1).start()
        self.copy(d + 3).start()

    def rest(self):
        d = self.p.depth
        for slot in (d, d + 1):
            self.copy(slot).wait_recv()
            self.copy(slot + 4).start()

    def joined(self):
        for slot in range(self.p.depth + 2, self.p.depth + 6):
            self.copy(slot).wait_recv()

    def drained(self):
        for slot in range(self.p.depth + 6):
            self.copy(slot).wait_send()


def ticker(plan, step):
    def tick(point):
        for (when, where), events in plan.items():
            if where == point:
                @pl.when(step == when)
                def _():
                    for event in events:
                        event()

    return tick


class Direct:
    def kinds(shards):
        return [
            pltpu.VMEM((shards, 8, 128), F32), pltpu.VMEM((2 * shards, 8, 128), F32),
            pltpu.SemaphoreType.DMA((2 * shards,)), pltpu.SemaphoreType.DMA((2 * shards,)),
        ]

    def __init__(self, place, scratch):
        self.tiles, self.got, self.send, self.recv = scratch
        self.count = 2 * place.shards
        self.at = 2 * place.me + place.core
        self.me = place.me

    def greet(self):
        barrier = pltpu.get_barrier_semaphore()
        for k in range(1, self.count):
            other = lax.rem(self.at + k, self.count)
            pl.semaphore_signal(barrier, inc=1, device_id=(other // 2, lax.rem(other, 2)), device_id_type=MESH)
        pl.semaphore_wait(barrier, self.count - 1)

    def copy(self, k, slot):
        other = lax.rem(self.at + k, self.count)
        return pltpu.make_async_remote_copy(
            src_ref=self.tiles.at[other // 2], dst_ref=self.got.at[slot], send_sem=self.send.at[k],
            recv_sem=self.recv.at[slot], device_id=(other // 2, lax.rem(other, 2)), device_id_type=MESH,
        )

    def push(self):
        for k in range(1, self.count):
            self.copy(k, self.at).start()

    def sum(self):
        self.got[self.at] = self.tiles[self.me]
        for k in range(1, self.count):
            self.copy(k, lax.rem(self.at + k, self.count)).wait_recv()
        value = self.got[0]
        for i in range(1, self.count):
            value = value + self.got[i]
        for k in range(1, self.count):
            self.copy(k, self.at).wait_send()
        return value


class Largest:
    def __init__(self, place, own, out, got, kept, send, recv):
        self.p, self.own, self.out, self.got, self.kept, self.send, self.recv = place, own, out, got, kept, send, recv
        d = place.depth
        self.stages = [
            [(place.sibling, 0)], [(place.far_peer, 1)], [(place.near_peer, 2)],
            [(place.column_peers[k], 2 + k) for k in range(1, d)],
        ]

    def copies(self, stage):
        return [
            pltpu.make_async_remote_copy(
                src_ref=self.kept.at[stage], dst_ref=self.got.at[slot], send_sem=self.send.at[slot],
                recv_sem=self.recv.at[slot], device_id=peer, device_id_type=MESH,
            )
            for peer, slot in self.stages[stage]
        ]

    def push(self, stage):
        if stage == 0:
            self.kept[0] = self.own[...]
        for copy in self.copies(stage):
            copy.start()

    def take(self, stage):
        value = self.kept[stage]
        for copy, (_, slot) in zip(self.copies(stage), self.stages[stage]):
            copy.wait_recv()
            value = jnp.maximum(value, self.got[slot])
        if stage == 3:
            self.out[...] = value
            for done in range(4):
                for copy in self.copies(done):
                    copy.wait_send()
        else:
            self.kept[stage + 1] = value


class BlockSum:
    def kinds(full, dtype, sets=1):
        depth, _, rows, cols = full
        one = (rows, cols // 2)
        many = lambda *lead: pltpu.VMEM((sets,) + lead + one, dtype)
        return [
            many(depth, 4), many(2, depth), many(2, depth), many(depth), many(depth), many(depth - 1), many(depth - 1),
            pltpu.VMEM((sets,) + one, F32), pltpu.VMEM((sets,) + one, F32),
            pltpu.SemaphoreType.DMA((sets, 4 + depth)), pltpu.SemaphoreType.DMA((sets, 4 + depth)),
        ]

    def __init__(self, place, full, scratch, at=0):
        self.p, self.full = place, full
        (self.got_one, self.send_two, self.got_two, self.send_three, self.got_three, self.send_four, self.got_four,
         self.total, self.joined, self.send, self.recv) = (ref.at[at] for ref in scratch)
        self.dtype = scratch[0].dtype
        self.cols, self.others = half_of(full, place.core), half_of(full, 1 - place.core)

    def copy(self, slot):
        p = self.p
        if slot < 4:
            src, dst, peer = (
                (self.full.at[:, :, :, self.others], self.got_one, p.sibling),
                (self.send_two.at[0], self.got_two.at[0], p.far_peer),
                (self.send_two.at[1], self.got_two.at[1], p.far_peer),
                (self.send_three, self.got_three, p.near_peer),
            )[slot]
        elif slot < 3 + p.depth:
            src, dst, peer = self.send_four.at[slot - 4], self.got_four.at[slot - 4], p.column_peers[slot - 3]
        else:
            src, dst, peer = self.total, self.joined, p.sibling
        return pltpu.make_async_remote_copy(
            src_ref=src, dst_ref=dst, send_sem=self.send.at[slot], recv_sem=self.recv.at[slot],
            device_id=peer, device_id_type=MESH,
        )

    def pair(self, near, far):
        at = near * self.p.near_step + far * self.p.far_step
        return self.full[:, at, :, self.cols].astype(F32) + self.got_one[:, at].astype(F32)

    def first(self):
        self.copy(0).start()

    def second(self):
        p = self.p
        self.copy(0).wait_recv()
        for slot, near in ((1, 1 - p.near), (0, p.near)):
            at = near * p.near_step + (1 - p.far) * p.far_step
            self.send_two[slot] = self.full[:, at, :, self.cols] + self.got_one[:, at]
            self.copy(1 + slot).start()

    def third(self):
        p = self.p
        self.copy(2).wait_recv()
        self.send_three[...] = (self.pair(1 - p.near, p.far) + self.got_two[1].astype(F32)).astype(self.dtype)
        self.copy(3).start()

    def fourth(self):
        p = self.p
        self.copy(1).wait_recv()
        self.copy(3).wait_recv()
        self.copy(0).wait_send()
        at = p.near * p.near_step + p.far * p.far_step

        def value(z):
            return (
                self.full[z, at, :, self.cols].astype(F32) + self.got_one[z, at].astype(F32)
                + self.got_two[0, z].astype(F32) + self.got_three[z].astype(F32)
            )

        for i in range(p.depth - 1):
            self.send_four[i] = value(p.columns[i + 1]).astype(self.dtype)
            self.copy(4 + i).start()
        self.total[...] = value(p.zed)

    def fifth(self):
        p = self.p
        value = self.total[...]
        for i in range(p.depth - 1):
            self.copy(4 + i).wait_recv()
            value = value + self.got_four[i].astype(F32)
        self.total[...] = value
        self.copy(3 + p.depth).start()

    def finish(self, write):
        self.copy(3 + self.p.depth).wait_recv()
        write(self.p.core, self.total[...])
        write(1 - self.p.core, self.joined[...])
        for slot in range(1, 4 + self.p.depth):
            self.copy(slot).wait_send()


class OwnerSum(BlockSum):
    def kinds(full, dtype, depth, sets=1):
        _, _, rows, cols = full
        one = (rows, cols // 2)
        many = lambda *lead: pltpu.VMEM((sets,) + lead + one, dtype)
        return [
            many(1, 4), many(2, 1), many(2, 1), many(1), many(1), many(), pltpu.VMEM((depth - 1,) + one, dtype),
            pltpu.VMEM(one, F32), pltpu.VMEM(one, F32),
            pltpu.SemaphoreType.DMA((sets, 4 + depth)), pltpu.SemaphoreType.DMA((sets, 4 + depth)),
        ]

    def __init__(self, place, full, scratch, at, target):
        self.p, self.full = place, full
        self.got_one, self.send_two, self.got_two, self.send_three, self.got_three, self.send_four = (
            ref.at[at] for ref in scratch[:6]
        )
        self.got_four, self.total, self.joined = scratch[6:9]
        self.send, self.recv = (ref.at[at] for ref in scratch[9:])
        self.dtype = scratch[0].dtype
        self.cols, self.others = half_of(full, place.core), half_of(full, 1 - place.core)
        self.away = lax.rem(target - place.zed + place.depth, place.depth)
        self.target = target

    def line(self, away):
        p = self.p
        return pltpu.make_async_remote_copy(
            src_ref=self.send_four, dst_ref=self.got_four.at[away - 1], send_sem=self.send.at[3 + away],
            recv_sem=self.recv.at[3 + away], device_id=(p.block(self.target, p.near, p.far), p.core), device_id_type=MESH,
        )

    def fourth(self):
        p = self.p
        self.copy(1).wait_recv()
        self.copy(3).wait_recv()
        self.copy(0).wait_send()
        value = self.pair(p.near, p.far)[0] + self.got_two[0, 0].astype(F32) + self.got_three[0].astype(F32)

        @pl.when(self.away == 0)
        def _():
            self.total[...] = value

        @pl.when(self.away > 0)
        def _():
            self.send_four[...] = value.astype(self.dtype)
            self.line(self.away).start()

    def fifth(self):
        @pl.when(self.away == 0)
        def _():
            value = self.total[...]
            for away in range(1, self.p.depth):
                self.line(away).wait_recv()
                value = value + self.got_four[away - 1].astype(F32)
            self.total[...] = value
            self.copy(3 + self.p.depth).start()

    def finish(self, write):
        last = self.copy(3 + self.p.depth)

        @pl.when(self.away == 0)
        def _():
            last.wait_recv()
            write(self.p.core, self.total[...])
            write(1 - self.p.core, self.joined[...])
            last.wait_send()

        @pl.when(self.away > 0)
        def _():
            self.line(self.away).wait_send()

        for slot in range(1, 4):
            self.copy(slot).wait_send()


def writer(ref, rows, first, width):
    def write(core, value):
        ref[rows, pl.ds(pl.multiple_of(first + core * width, width), width)] = value

    return write


def middle_kernel(shards, tall, *refs):
    mid_hbm, dy_ref, own_ref, b0_hbm, w2_ref, vec_ref, hb_ref = refs[:7]
    act_hbm, mg_hbm, bl_hbm, cl_hbm, w2g_ref, w1g_ref, vg_ref, hbg_ref = refs[7:15]
    inp_ref, act_ref, grad_ref, two_ref, stage, w1_ref, fullb, fullc, local = refs[15:24]
    sems, sums = refs[24:26], refs[26:]
    j, p = pl.program_id(0), Place(shards)
    depth = p.depth
    chunk = w2_ref.shape[1] * 4
    rows_all = dy_ref.shape[0]
    turns = rows_all // tall
    gain, shift = vec_ref[5:6], vec_ref[6:7]
    root = math.sqrt(2.0 / math.pi)
    weights = [
        Gather(p, w1_ref, sems, k - 1, k * chunk, chunk) for k in range(1, depth)
    ]
    def blocks(k):
        return (
            OwnerSum(p, fullc.at[lax.rem(k, 2)], sums[11:], k, k),
            BlockSum(p, fullb.at[lax.rem(k, 2)], sums[:11], k),
        )

    def each(k, stage, *args):
        for job in blocks(k):
            getattr(job, stage)(*args)

    def rows_of(t):
        return pl.ds(pl.multiple_of(t * tall, tall), tall)

    def again(t):
        return pltpu.make_async_copy(mid_hbm.at[rows_of(t)], stage.at[t % 2], local.at[t])

    def results(t):
        return pltpu.make_async_copy(two_ref.at[rows_of(t)], mg_hbm.at[rows_of(t)], local.at[2 * turns + t])

    def first_chunk():
        return pltpu.make_async_copy(b0_hbm, w1_ref.at[:, :, :, pl.ds(0, chunk)], local.at[3 * turns])

    @pl.when(j == 0)
    def _():
        first_chunk().start()
        again(0).start()
        w1_ref[p.zed, lax.rem(p.me, 4), :, pl.ds(chunk, (depth - 1) * chunk)] = own_ref[:, pl.ds(chunk, (depth - 1) * chunk)]
        p.greet()
        for w in weights:
            w.own()
        for t in range(turns):
            if t + 1 < turns:
                again(t + 1).start()
            again(t).wait()
            rows = rows_of(t)
            unit, _ = normalise(stage[t % 2])
            inp_ref[rows, :] = (unit * gain + shift).astype(BF)
            two_ref[rows, :] = jnp.zeros((tall, two_ref.shape[1]), F32)
        first_chunk().wait()

    cols = pl.ds(pl.multiple_of(j * chunk, chunk), chunk)

    def chunk_rows(t, carry):
        rows = rows_of(t)
        w1 = w1_ref[:, :, :, cols].reshape(-1, chunk)
        w2 = w2_ref[...].reshape(chunk, -1)
        z = nn(inp_ref[rows, :], w1) + hb_ref[...]
        act_grad = nt(dy_ref[rows, :], w2)
        square = z * z
        bend = jnp.tanh(root * z * (1.0 + 0.044715 * square))
        half = 0.5 * (1.0 + bend)
        act = (z * half).astype(BF)
        slope = half + 0.5 * z * (1.0 - bend * bend) * (root * (1.0 + 0.134145 * square))
        grad = (act_grad * slope).astype(BF)
        act_ref[rows, :] = act
        grad_ref[rows, :] = grad
        two_ref[rows, :] += nt(grad, w1)
        hbg_ref[...] += column_sum(grad.astype(F32))

        first, later = weights[0], weights[1:]

        @pl.when(j == 0)
        def _():
            @pl.when(t == 0)
            def _():
                first.column()

            @pl.when(t == 1)
            def _():
                first.plane()
                for w in later:
                    w.column()

            pl.when(t == 2)(first.rest)

            @pl.when(t == 3)
            def _():
                for w in later:
                    w.plane()

        @pl.when((j == 1) & (t == 0))
        def _():
            for w in later:
                w.rest()

        @pl.when(j > 0)
        def _():
            pl.when(t == 0)(functools.partial(each, j - 1, "second"))
            pl.when(t == 3)(functools.partial(each, j - 1, "third"))

        return carry

    hbg_ref[...] = jnp.zeros_like(hbg_ref)
    lax.fori_loop(0, turns, chunk_rows, 0)
    store = pltpu.make_async_copy(act_ref, act_hbm.at[:, cols], local.at[turns])
    store.start()
    for k, w in enumerate(weights):
        pl.when(j == k)(w.joined)

    fullc[lax.rem(j, 2)] = tn(act_ref[...], dy_ref[...]).astype(BF).reshape(fullc.shape[1:])
    fullb[lax.rem(j, 2)] = tn(inp_ref[...], grad_ref[...]).astype(BF).reshape(fullb.shape[1:])

    store.wait()

    @pl.when(j < depth - 1)
    def _():
        each(j, "first")

    @pl.when(j > 1)
    def _():
        each(j - 2, "fifth")

    @pl.when(j > 0)
    def _():
        each(j - 1, "fourth")

    @pl.when(j == depth - 1)
    def _():
        lasts = (
            pltpu.make_async_copy(fullb.at[(depth - 1) % 2], bl_hbm, local.at[3 * turns]),
            pltpu.make_async_copy(fullc.at[(depth - 1) % 2], cl_hbm, local.at[3 * turns + 1]),
        )
        for copy in lasts:
            copy.start()
        w2g_ref[...] = jnp.zeros_like(w2g_ref)
        again(0).start()
        vg_ref[...] = jnp.zeros_like(vg_ref)
        for t in range(turns):
            rows = rows_of(t)
            if t + 1 < turns:
                again(t + 1).start()
            again(t).wait()
            unit, inverse = normalise(stage[t % 2])
            two, up = two_ref[rows, :], dy_ref[rows, :].astype(F32)
            vg_ref[5:6] += column_sum(two * unit)
            vg_ref[6:7] += column_sum(two)
            vg_ref[7:8] += column_sum(up)
            two_ref[rows, :] = up + norm_back(two, unit, inverse, gain)
            results(t).start()
        each(depth - 2, "fifth")
        for t in range(turns):
            results(t).wait()
        for copy in lasts:
            copy.wait()
        for w in weights:
            w.drained()
        for k in range(depth - 1):
            c, b = blocks(k)
            c.finish(writer(w2g_ref, slice(None), 0, w2g_ref.shape[1] // 2))
            b.finish(writer(w1g_ref, slice(None), k * chunk, chunk // 2))


def middle(shards, mid, dy, w1_own, b0, w2, vec, hb):
    rows, d = mid.shape
    depth = shards // 4
    hidden = w1_own.shape[1]
    chunk = hidden // depth
    tall = min(ROWS, rows)
    turns = rows // tall
    less = depth - 1
    anywhere = pl.BlockSpec(memory_space=pl.ANY)
    fullb = (depth, 4, w1_own.shape[0], chunk)
    w1g = (w1_own.shape[0], less * chunk)
    fullc = (1, 4) + w2.shape[1:]
    return pl.pallas_call(
        lambda *refs: middle_kernel(shards, tall, *refs),
        grid=(depth,),
        in_specs=[
            anywhere, whole(dy.shape), whole(w1_own.shape), anywhere,
            pl.BlockSpec((4,) + w2.shape[1:], lambda j: (j, 0, 0)), whole(vec.shape), pl.BlockSpec((1, chunk), lambda j: (0, j)),
        ],
        out_specs=[
            anywhere, anywhere, anywhere, anywhere, whole(w2.shape[1:]), whole(w1g), whole((8, d)),
            pl.BlockSpec((1, chunk), lambda j: (0, j)),
        ],
        out_shape=[
            shaped((rows, hidden), BF), shaped((rows, d), F32), shaped(fullb, BF), shaped(fullc, BF), shaped(w2.shape[1:], F32),
            shaped(w1g, F32),
            shaped((8, d), F32), shaped((1, hidden), F32),
        ],
        scratch_shapes=[
            pltpu.VMEM((rows, d), BF), pltpu.VMEM((rows, chunk), BF), pltpu.VMEM((rows, chunk), BF),
            pltpu.VMEM((rows, d), F32), pltpu.VMEM((2, tall, d), F32),
            pltpu.VMEM((depth, 4) + w1_own.shape, BF), pltpu.VMEM((2,) + fullb, BF),
            pltpu.VMEM((2,) + fullc, BF), pltpu.SemaphoreType.DMA((3 * turns + 2,)),
        ] + Gather.kinds(depth, less) + BlockSum.kinds(fullb, BF, less) + OwnerSum.kinds(fullc, BF, depth, less),
        compiler_params=pltpu.CompilerParams(
            dimension_semantics=("arbitrary",), collective_id=3, has_side_effects=True, vmem_limit_bytes=VMEM_LIMIT
        ),
        name="middle",
    )(mid, dy, w1_own, b0, w2, vec, hb)


def enter_kernel(shards, width, steps, *refs):
    tok_ref, wq, wk, wv, wo, w1, w2, small = refs[:8]
    attn_out, w1_out, w2_out, hb_out, vec_out = refs[8:13]
    results, top_out, one_out = refs[13:19], refs[19], refs[20]
    attn, tiles_in, tops, local = refs[21:25]
    sems = refs[25:27]
    hidden_rows = hb_out.shape[1] // shards
    step = pl.program_id(0)
    p = Place(shards)
    depth = p.depth
    rows = wq.shape[0]
    s, b, c, *early = (
        Gather(p, full, sems, i)
        for i, full in enumerate(
            [tiles_in, w1_out, w2_out] + [attn.at[:, :, i * rows : (i + 1) * rows] for i in range(4)]
        )
    )
    early.insert(0, s)

    def start():
        mine = p.zed, lax.rem(p.me, 4)
        copies = [
            pltpu.make_async_copy(w, out.at[mine], local.at[i])
            for i, (w, out) in enumerate(((w1, w1_out), (w2, w2_out)))
        ]
        for copy in copies:
            copy.start()
        attn[mine] = jnp.concatenate([w[...] for w in (wq, wk, wv, wo)], axis=0)
        tiles_in[mine] = small[...]
        for copy in copies:
            copy.wait()
        p.greet()
        for g in early + [b, c]:
            g.own()
        for g in early:
            g.column()
        for g in early:
            g.plane()
        b.column()
        for g in early:
            g.rest()
        b.plane()
        for g in early[:-1]:
            g.joined()
        c.column()
        vec = jnp.zeros(vec_out.shape, F32)
        blank = jnp.zeros((8, vec.shape[1] - 128), F32)
        for i in range(shards):
            piece = jnp.concatenate([tiles_in[i // 4, i % 4, :, :128], blank], axis=1)
            vec = vec + (pltpu.roll(piece, i * rows, 1) if i else piece)
        vec_out[...] = vec
        empty = jnp.zeros((8, 2 * hidden_rows - 256), F32)
        for i in range(0, shards, 2):
            even, odd = (
                jnp.concatenate([tiles_in[n // 4, n % 4, :, 256:], empty], axis=1) for n in (i, i + 1)
            )
            both = even + pltpu.roll(odd, hidden_rows, 1)
            hb_out[:, i * hidden_rows : (i + 2) * hidden_rows] = both[0:1]

    def keep():
        return pltpu.make_async_copy(attn, attn_out, local.at[2])

    def whole_attn():
        early[-1].joined()
        keep().start()

    def end():
        lane = lax.broadcasted_iota(jnp.int32, (8, 128), 1)
        tile = jnp.zeros((8, 128), F32)
        for pair in range(tops.shape[0]):
            best = jnp.max(tops[pair], axis=0, keepdims=True)
            for i in range(2):
                one = jnp.max(best[:, i * BLOCK : (i + 1) * BLOCK], axis=1, keepdims=True)
                tile = jnp.where(lane == 2 * pair + i, one, tile)
        top_out[...] = tile
        b.joined(), c.joined()
        for g in early + [b, c]:
            g.drained()
        keep().wait()

    pl.when(step == 0)(start)
    plan = {(0, 1): [whole_attn], (0, 2): [b.rest], (min(1, steps - 1), 2): [c.plane], (steps - 1, 1): [c.rest], (steps - 1, 3): [end]}
    view = [attn.at[:, :, i * rows : (i + 1) * rows, :] for i in range(4)]
    attend_kernel(width, tok_ref, view, vec_out, *results, tops, one_out, tick=ticker(plan, step))


def enter(shards, tokens, wq, wk, wv, wo, w1, w2, small, heads):
    rows, d = tokens.shape
    t = min(ROWS, rows)
    pairs = d // PAIR
    blocks = rows // BLOCK
    big = tiles(t, d)
    depth = shards // 4
    lead = (depth, 4)
    anywhere = pl.BlockSpec(memory_space=pl.ANY)
    packed = lead + (4 * wq.shape[0], d)
    full_small = lead + small.shape
    chunk = w1.shape[1] // depth
    return pl.pallas_call(
        lambda *refs: enter_kernel(shards, d // heads, rows // t, *refs),
        grid=(rows // t,),
        in_specs=[big] + [whole(w.shape) for w in (wq, wk, wv, wo)] + [whole((w1.shape[0], chunk))] + [whole(w.shape) for w in (w2, small)],
        out_specs=[
            anywhere, anywhere, anywhere, whole((1, w1.shape[1])), whole((8, d)), big, big, big,
            pl.BlockSpec((t // BLOCK, pairs, FRAMES, 2 * BLOCK), lambda i: (i, 0, 0, 0)),
            big, big,
            whole((8, 128)), big,
        ],
        out_shape=[
            shaped(packed, BF), shaped(lead + (w1.shape[0], chunk), BF), shaped(lead + w2.shape, BF),
            shaped((1, w1.shape[1]), F32), shaped((8, d), F32),
        ]
        + [shaped((rows, d), BF)] * 3
        + [shaped((blocks, pairs, FRAMES, 2 * BLOCK), F32), shaped((rows, d), BF), shaped((rows, d), F32)]
        + [shaped((8, 128), F32), shaped((rows, d), BF)],
        scratch_shapes=[
            pltpu.VMEM(packed, BF), pltpu.VMEM(full_small, F32), pltpu.VMEM((pairs, FRAMES, 2 * BLOCK), F32),
            pltpu.SemaphoreType.DMA((3,)),
        ] + Gather.kinds(depth, 7),
        compiler_params=pltpu.CompilerParams(
            dimension_semantics=("arbitrary",), collective_id=0, has_side_effects=True, vmem_limit_bytes=VMEM_LIMIT
        ),
        name="enter",
    )(tokens, wq, wk, wv, wo, w1, w2, small)


def leave_kernel(shards, width, steps, *refs):
    mg_ref, q_ref, k_ref, v_ref, p_ref, mix_ref, wo_ref, fullb, fullc, w1_in, w2_in = refs[:11]
    dq_ref, dk_ref, dv_ref, wog_ref, vg_ref, w1_out, w2_out = refs[11:18]
    acco, mgl_ref = refs[18:20]
    own = refs[20:]
    step, p = pl.program_id(0), Place(shards)
    b = BlockSum(p, fullb, own[:11])
    c = OwnerSum(p, fullc, own[11:22], 0, p.depth - 1)
    wide = fullb.shape[3]

    def others():
        w1_out[:, : (p.depth - 1) * wide] = w1_in[...]
        w2_out[...] = w2_in[...]

    def finish():
        c.finish(writer(w2_out, slice(None), 0, w2_out.shape[1] // 2))
        b.finish(writer(w1_out, slice(None), (p.depth - 1) * wide, wide // 2))

    events = [
        (0, p.greet), (0, c.first), (0, b.first), (1, others), (2, c.second), (2, b.second), (5, c.third), (5, b.third),
        (8, c.fourth), (8, b.fourth), (11, c.fifth), (11, b.fifth),
    ]
    points = [(when, where) for when in range(steps) for where in range(3)]
    plan = {}
    for at, event in events:
        plan.setdefault(points[at * len(points) // 12], []).append(event)
    tick = ticker(plan, step)

    @pl.when(step == 0)
    def _():
        acco[...] = jnp.zeros_like(acco)
        vg_ref[...] = jnp.zeros_like(vg_ref)

    tick(0)
    branch = mg_ref[...].astype(BF)
    mgl_ref[...] = nt(branch, square(wo_ref)).astype(BF)
    acco[...] += tn(mix_ref[...], branch)
    vg_ref[4:5] += column_sum(branch.astype(F32))
    tick(1)
    attention_back(width, mgl_ref, q_ref, k_ref, v_ref, p_ref, dq_ref, dk_ref, dv_ref)
    vg_ref[2:3] += column_sum(dq_ref[...].astype(F32))
    vg_ref[3:4] += column_sum(dv_ref[...].astype(F32))
    tick(2)

    @pl.when(step == steps - 1)
    def _():
        wog_ref[...] = acco[...].astype(BF).reshape(wog_ref.shape)
        finish()


def leave(shards, mg, q, k, v, p, mixed, attn, fullb, fullc, w1g, w2g, heads):
    rows, d = mg.shape
    t = min(ROWS, rows)
    pairs = d // PAIR
    big = tiles(t, d)
    w1_out, w2_out = (w1g.shape[0], shards // 4 * fullb.shape[3]), w2g.shape
    wog = (shards // 4, 4, attn.shape[1] // 4, d)
    return pl.pallas_call(
        lambda *refs: leave_kernel(shards, d // heads, rows // t, *refs),
        grid=(rows // t,),
        in_specs=[
            big, big, big, big,
            pl.BlockSpec((t // BLOCK, pairs, FRAMES, 2 * BLOCK), lambda i: (i, 0, 0, 0)),
            big, weight_specs((attn,))[3],
        ] + [whole(x.shape) for x in (fullb, fullc, w1g, w2g)],
        out_specs=[big, big, big, whole(wog), whole((8, d)), whole(w1_out), whole(w2_out)],
        out_shape=[shaped((rows, d), BF)] * 3
        + [shaped(wog, BF), shaped((8, d), F32), shaped(w1_out, F32), shaped(w2_out, F32)],
        scratch_shapes=[pltpu.VMEM((d, d), F32), pltpu.VMEM((t, d), BF)]
        + BlockSum.kinds(fullb.shape, BF) + OwnerSum.kinds(fullc.shape, BF, shards // 4),
        compiler_params=pltpu.CompilerParams(
            dimension_semantics=("arbitrary",), collective_id=1, has_side_effects=True, vmem_limit_bytes=VMEM_LIMIT
        ),
        name="leave",
    )(mg, q, k, v, p, mixed, attn, fullb, fullc, w1g, w2g)


def last_kernel(shards, steps, *refs):
    tok_ref, mg_ref, dq_hbm, dk_hbm, dv_hbm, one_hbm, wq, wk, wv, vec_ref, wog_ref, vga_ref, vgb_ref, hbg_ref, top_ref, mid_ref, act_ref, w2_hbm = refs[:18]
    gt_ref, lo_ref, attn_out, small_out, top_out = refs[18:23]
    d_ref, one_ref, full, tile, vg, w2_ref, local = refs[23:30]
    jobs, little, most, straight = refs[30:41], refs[41:52], refs[52:56], refs[56:]
    hidden_rows = hbg_ref.shape[1] // shards
    turns = (steps - 3) // 2
    step, p = pl.program_id(0), Place(shards)
    rows = wog_ref.shape[2]
    d = vg.shape[1]
    wide = attn_out.shape[1] // 2
    o = BlockSum(p, wog_ref, jobs, 3)
    s = BlockSum(p, tile, little)
    t = Largest(p, top_ref, top_out, *most)
    late = Direct(p, straight)
    weight = lambda i: BlockSum(p, full.at[i], jobs, i)
    q, k, v = weight(0), weight(1), weight(2)
    many = functools.partial
    events = [
        (1, o.second), (1, s.second), (2, q.second), (3, many(t.take, 0)), (3, many(t.push, 1)), (3, s.third), (4, o.third),
        (5, k.second), (5, many(t.take, 1)), (5, many(t.push, 2)), (5, s.fourth), (7, v.second), (7, q.third),
        (8, o.fourth), (9, many(t.take, 2)), (9, many(t.push, 3)), (9, s.fifth), (9, k.third), (11, q.fourth),
        (11, v.third), (13, o.fifth), (13, k.fourth), (13, many(t.take, 3)), (15, v.fourth), (15, q.fifth), (18, k.fifth),
        (20, v.fifth),
    ]
    plan = {}
    for at, event in events:
        at = min(at, 2 * steps - 1)
        plan.setdefault((at // 2, at % 2), []).append(event)
    tick = ticker(plan, step)
    fetches = [
        pltpu.make_async_copy(src, dst, local.at[i])
        for i, (src, dst) in enumerate(
            ((dq_hbm, d_ref.at[0]), (dk_hbm, d_ref.at[1]), (dv_hbm, d_ref.at[2]), (one_hbm, one_ref), (w2_hbm, w2_ref))
        )
    ]

    def spread(value, put):
        for i in range(shards):
            put(i, (pltpu.roll(value, d - i * rows, 1) if i else value)[:, :128])

    @pl.when(step == 0)
    def _():
        for i in (3, 0, 1, 2, 4):
            fetches[i].start()
        vg[...] = jnp.zeros_like(vg)

        def put(i, piece):
            tile[i // 4, i % 4, :, :128] = piece

        spread(vga_ref[...] + vgb_ref[...], put)
        tile[:, :, :, 128:256] = jnp.zeros(tile.shape[:3] + (128,), F32)
        for i in range(0, shards, 2):
            both = jnp.broadcast_to(
                hbg_ref[:, i * hidden_rows : (i + 2) * hidden_rows], (8, 2 * hidden_rows)
            )
            tile[i // 4, i % 4, :, 256:] = both[:, :256]
            tile[i // 4, i % 4 + 1, :, 256:] = pltpu.roll(both, hidden_rows, 1)[:, :256]
        late.greet()
        o.first(), s.first(), t.push(0)
        fetches[3].wait()

    tick(0)

    for i in range(3):
        pl.when(step == i)(fetches[i].wait)

    @pl.when(step < 3)
    def _():
        full[step] = tn(one_ref[...], d_ref[step]).astype(BF).reshape(full.shape[1:])
        weight(step).first()

    pl.when(step == 3 + turns)(fetches[4].wait)

    @pl.when(step >= 3 + turns)
    def _():
        w2 = square(w2_ref)
        lo_ref[...] = (mid_ref[...] + (nn(act_ref[...], w2) + vec_ref[7:8])).astype(BF)

    @pl.when((step >= 3) & (step < 3 + turns))
    def _():
        tall = tok_ref.shape[0]
        at = pl.ds(pl.multiple_of((step - 3) * tall, tall), tall)
        unit, inverse = normalise(tok_ref[...].astype(F32))
        grad = nt(d_ref[0, at], square(wq)) + nt(d_ref[1, at], square(wk)) + nt(d_ref[2, at], square(wv))
        vg[0:1] += column_sum(grad * unit)
        vg[1:2] += column_sum(grad)
        gt_ref[...] = (mg_ref[...] + norm_back(grad, unit, inverse, vec_ref[0:1])).astype(BF)

    @pl.when(step == 2 + turns)
    def _():
        def put(i, piece):
            late.tiles[i] = piece

        spread(vg[...], put)
        late.push()

    tick(1)

    @pl.when(step == steps - 1)
    def _():
        s.finish(writer(small_out, slice(None), 0, small_out.shape[1] // 2))
        small_out[0:2, :128] = late.sum()[0:2]
        for i, job in ((3, o), (0, q), (1, k), (2, v)):
            job.finish(writer(attn_out, slice(i * rows, (i + 1) * rows), 0, wide))


def last(shards, tokens, mg, dq, dk, dv, one, attn, vec, wog, vga, vgb, hbg, top, mid, act, w2):
    rows, d = tokens.shape
    t = min(ROWS, rows)
    depth = shards // 4
    turns = rows // t
    steps = 3 + 2 * turns
    later = pl.BlockSpec((t, d), lambda i: (jnp.clip(i - 3, 0, turns - 1), 0))
    latest = lambda width: pl.BlockSpec((t, width), lambda i: (jnp.maximum(i - 3 - turns, 0), 0))
    anywhere = pl.BlockSpec(memory_space=pl.ANY)
    small = (depth, 4, 8, 512)
    return pl.pallas_call(
        lambda *refs: last_kernel(shards, steps, *refs),
        grid=(steps,),
        in_specs=[later, later] + [anywhere] * 4 + weight_specs((attn,))[:3]
        + [whole(x.shape) for x in (vec, wog, vga, vgb, hbg, top)] + [latest(d), latest(act.shape[1]), anywhere],
        out_specs=[later, latest(d), whole((4 * wog.shape[2], d)), whole((8, 512)), whole((8, 128))],
        out_shape=[
            shaped((rows, d), BF), shaped((rows, d), BF), shaped((4 * wog.shape[2], d), F32), shaped((8, 512), F32), shaped((8, 128), F32),
        ],
        scratch_shapes=[
            pltpu.VMEM((3, rows, d), BF), pltpu.VMEM((rows, d), BF), pltpu.VMEM((3,) + wog.shape, BF),
            pltpu.VMEM(small, F32), pltpu.VMEM((8, d), F32), pltpu.VMEM(w2.shape, BF), pltpu.SemaphoreType.DMA((5,)),
        ] + BlockSum.kinds(wog.shape, BF, 4) + BlockSum.kinds(small, F32) + [
            pltpu.VMEM((depth + 2, 8, 128), F32), pltpu.VMEM((4, 8, 128), F32),
            pltpu.SemaphoreType.DMA((depth + 2,)), pltpu.SemaphoreType.DMA((depth + 2,)),
        ] + Direct.kinds(shards),
        compiler_params=pltpu.CompilerParams(
            dimension_semantics=("arbitrary",), collective_id=2, has_side_effects=True, vmem_limit_bytes=VMEM_LIMIT
        ),
        name="last",
    )(tokens, mg, dq, dk, dv, one, attn, attn, attn, vec, wog, vga, vgb, hbg, top, mid, act, w2)


def on_device(shards, reps, *args):
    (
        tokens, grad_out, first_gain, first_shift, query_proj, query_bias, key_proj, value_proj, value_bias,
        output_proj, output_bias, second_gain, second_shift, hidden_proj, hidden_bias, final_proj, final_bias, threshold,
    ) = args
    heads = threshold.shape[0]
    d = tokens.shape[1]
    hidden = hidden_proj.shape[1]
    head_dim = d // heads
    small = (first_gain, first_shift, query_bias, value_bias, output_bias, second_gain, second_shift, final_bias)
    rows, more = small[0].shape[0], hidden_bias.shape[0]
    whole_chunks = shards % 4 == 0 and hidden * 4 % (shards * 256) == 0 and hidden * 4 // shards == 4 * final_proj.shape[0]
    own = whole_chunks and reps == 2 and shards % 4 == 0 and shards > 4 and rows % 16 == 0 and rows <= 128 and more <= 256 and more % 64 == 0 and more > 128

    def gather(x):
        return lax.all_gather(x, "shard", axis=0, tiled=True)

    def scatter(x):
        y = lax.psum_scatter(x.astype(BF), "shard", scatter_dimension=0, tiled=True)
        return lax.psum(y, "rep").astype(F32)

    if own:
        tile = jnp.concatenate(
            [
                jnp.pad(jnp.stack(small).astype(F32), ((0, 0), (0, 256 - rows))),
                jnp.pad(hidden_bias.astype(F32)[None], ((0, 7), (0, 256 - more))),
            ],
            axis=1,
        )
        attn, w1, w2, hb, vec, q, k, v, p, mixed, mid, top, one = enter(
            shards, tokens, query_proj, key_proj, value_proj, output_proj, hidden_proj, final_proj, tile, heads
        )
        attn, w2 = attn.reshape(shards, -1, d), w2.reshape(shards, -1, d)
    else:
        weights = tuple(gather(x) for x in (query_proj, key_proj, value_proj, output_proj))
        w1, w2 = gather(hidden_proj), gather(final_proj)
        vec = jnp.stack([gather(x) for x in small]).astype(F32)
        hb = gather(hidden_bias).astype(F32)[None]
        q, k, v, p, mixed, mid, top = attend(tokens, weights, vec, heads)
    if own:
        act, mg, b3g, c3g, w2g, w1g, vg2, hbg = middle(shards, mid, grad_out, hidden_proj, w1, w2, vec, hb)
        dq, dk, dv, wog, vg1, w1g, w2g = leave(
            shards, mg, q, k, v, p, mixed, attn, b3g, c3g, w1g, w2g, heads
        )
        grad_tokens, layer_output, attn, tile, top = last(
            shards, tokens, mg, dq, dk, dv, one, attn, vec, wog, vg1, vg2, hbg, top, mid, act, w2
        )
    else:
        layer_output, mg, w1g, w2g, vg2, hbg = mlp(mid, grad_out, w1, w2, vec, hb)
        grad_tokens, wg, vg1 = back(tokens, mg, q, k, v, p, mixed, weights, vec, heads)
    if own:
        wg = tuple(attn[i * rows : (i + 1) * rows] for i in range(4))
        vg = tuple(tile[i, :rows] for i in range(8))
        hbg = tile[0, 256 : 256 + more]
        global_max = top[0, :heads]
    else:
        vg = jnp.concatenate([vg1[:5], vg2[:3]])
        local = jnp.max(top.reshape(top.shape[0], FRAMES, 2, BLOCK), axis=(1, 3)).reshape(heads)
        global_max = lax.pmax(local, ("shard", "rep"))
        wg = tuple(scatter(x) for x in wg)
        w1g, w2g = scatter(w1g), scatter(w2g)
        vg = tuple(scatter(vg[i]) for i in range(8))
        hbg = scatter(hbg[0])
    factor = jnp.minimum(1.0, threshold / global_max)
    column_scale = jnp.repeat(jnp.sqrt(factor), head_dim)
    bias_scale = lax.dynamic_slice_in_dim(column_scale, lax.axis_index("shard") * rows, rows)
    return (
        layer_output, grad_tokens, vg[0], vg[1], wg[0], vg[2], wg[1], wg[2], vg[3], wg[3], vg[4], vg[5], vg[6],
        w1g, hbg, w2g, vg[7], global_max, factor,
        query_proj.astype(F32) * column_scale[None, :], query_bias.astype(F32) * bias_scale,
        key_proj.astype(F32) * column_scale[None, :],
    )


def solution(mesh):
    in_specs = (
        P(("shard", "rep"), None),
        P(("shard", "rep"), None),
        P("shard"),
        P("shard"),
        P("shard", None),
        P("shard"),
        P("shard", None),
        P("shard", None),
        P("shard"),
        P("shard", None),
        P("shard"),
        P("shard"),
        P("shard"),
        P("shard", None),
        P("shard"),
        P("shard", None),
        P("shard"),
        P(),
    )
    out_specs = (
        P(("shard", "rep"), None),
        P(("shard", "rep"), None),
        P("shard"),
        P("shard"),
        P("shard", None),
        P("shard"),
        P("shard", None),
        P("shard", None),
        P("shard"),
        P("shard", None),
        P("shard"),
        P("shard"),
        P("shard"),
        P("shard", None),
        P("shard"),
        P("shard", None),
        P("shard"),
        P(),
        P(),
        P("shard", None),
        P("shard"),
        P("shard", None),
    )
    shards, reps = mesh.shape["shard"], mesh.shape["rep"]
    return jax.shard_map(
        functools.partial(on_device, shards, reps), mesh=mesh, in_specs=in_specs, out_specs=out_specs, check_vma=False
    )
```
